256 devices in a mesh: shot: 64 (over x, z, core), cmp: 4 (over y).
Axes of the slice: x: 4, y: 4, z: 8, core: 2. Of those that a mesh axis runs over, the one named last changes fastest.
Arguments:
- gathers: bfloat16 [64, 7680, 512], P('shot', 'cmp'), may hold values from -6 to 6
- trace_slot: int32 [64, 7680], P('shot', 'cmp'), may hold values from 0 to 7679, as said below
- gain: float32 [64, 7680], P('shot', 'cmp'), may hold values from 0.25 to 4
- midbin: int32 [64, 7680], P('shot', 'cmp'), may hold values from 0 to 8191, as said below
- bin_row: int32 [8192], replicated, may hold values from 0 to 8191, as said below
- taps_shot: float32 [3, 31], replicated, may hold values from -1 to 1
- taps_time: float32 [3, 64], replicated, may hold values from -0.75 to 0.75
Outputs:
- stack: float32 [8192, 512], P('shot', 'cmp')
The draws below stay inside these ranges and needn't reach their ends.
Inputs may be any that keep to these rules, and one draw needn't show every extreme that they name: For each shot s and each j, trace_slot[s, j*1920 .. (j+1)*1920 - 1] is a permutation of those channel numbers. bin_row is a permutation. For every block of receivers k*30 .. (k+1)*30 - 1 and every o, at most 60 of its 1920 traces (all shots) have bin_row[midbin] // 128 = o, and exactly 60 for some o.
All inputs are finite; a program needn't handle non-finite values.
Results may differ from the reference program's by a relative error of at most 0.0062.
Values may be sent and summed in bfloat16 or wider, within the bound.
No kernel may reach another device: no remote copies, remote signals or barrier semaphores. Data moves between devices by JAX's collectives and lax.ppermute only.
A program may use at most 192 MiB of HBM per device.

```python
import math
import jax
import jax.numpy as jnp
from jax import lax

CHANNELS = 7680
NT = 512
BIN_DEV = 128
KDIP = 3
TAP_SHOT = 31
TAP_TIME = 64
SHOTS = 64
NBINS = 8192
CH_BLK = 1920
RPD = 30
TRC_DEV = 1920
CAP = 60
N_SHOT = 64
N_CMP = 4


def owner_layout(key):
    bin_row = jax.random.permutation(jax.random.fold_in(key, 11), NBINS).astype(jnp.int32)
    inverse = jnp.argsort(bin_row, stable=True).astype(jnp.int32)
    sources = N_SHOT * N_CMP
    keys = jax.random.split(jax.random.fold_in(key, 12), sources)

    def one_source(src_key):
        key_a, key_b, key_c, key_d = jax.random.split(src_key, 4)
        half = CAP // 2
        spread = jax.random.randint(key_a, (N_SHOT // 2,), 0, half + 1).at[0].set(half)
        counts = jnp.stack([half + spread, half - spread], axis=1).reshape(-1)
        owners = jax.random.permutation(key_b, N_SHOT)
        ends = jnp.cumsum(counts)
        places = jnp.arange(TRC_DEV)
        labels = jnp.sum((places[:, None] >= ends[None, :]).astype(jnp.int32), axis=1)
        owner = jax.random.permutation(key_c, owners[labels])
        local = jax.random.randint(key_d, (TRC_DEV,), 0, BIN_DEV)
        return inverse[owner * BIN_DEV + local]
    bins = jax.vmap(one_source)(keys)
    bins = bins.reshape(N_SHOT, N_CMP, SHOTS, RPD).transpose(2, 1, 0, 3).reshape(SHOTS, CHANNELS)
    return (bin_row, bins.astype(jnp.int32))


def draw_bin_row(key, part):
    table, bins = owner_layout(key)
    return table


def draw_midbin(key, part):
    table, bins = owner_layout(key)
    return bins


def draw_trace_slot(key, part):
    keys = jax.random.split(jax.random.fold_in(key, 21), SHOTS * N_CMP)

    def one_block(block_key):
        return jax.random.permutation(block_key, CH_BLK)
    perms = jax.vmap(one_block)(keys).reshape(SHOTS, N_CMP, CH_BLK)
    starts = (jnp.arange(N_CMP) * CH_BLK)[None, :, None]
    return (perms + starts).reshape(SHOTS, CHANNELS).astype(jnp.int32)


def shard_levels(key, shape, shards, low, top_value):
    def one(axis_at, shards_of):
        heights = jax.random.uniform(jax.random.fold_in(jax.random.fold_in(key, 6), axis_at), (shards_of,), jnp.float32, low / len(shards), top_value / len(shards))
        return jnp.repeat(jnp.exp(heights), shape[axis_at] // shards_of).reshape((-1,) + (1,) * (len(shape) - axis_at - 1))

    level = one(*shards[0])
    for cut in shards[1:]:
        level = level * one(*cut)
    return level


def centred(key, shape, scale, bound, cuts=(), held_as=jnp.bfloat16):
    drawn = jax.random.normal(key, shape, jnp.float32) * scale
    if len(cuts) > 0:
        drawn = shard_levels(key, shape, cuts, -0.22, 0.18) * drawn
    return jnp.clip(drawn, min=-bound, max=bound).astype(held_as)


def setup_inputs(seed: int = 0) -> dict:
    streams_of = jax.random.split(jax.random.key(seed), 8)
    gathers = centred(streams_of[0], (SHOTS, CHANNELS, NT), 1.0, 6.0, ((0, 64), (1, 4)))
    trace_slot = draw_trace_slot(jax.random.fold_in(streams_of[7], 71), 0)
    gain = jnp.clip(jnp.exp(math.log(4.0) - 2.7725887 * jax.random.uniform(streams_of[2], (SHOTS, CHANNELS), jnp.float32) ** shard_levels(streams_of[2], (SHOTS, CHANNELS), ((0, 64), (1, 4)), -0.2, 0.2)), 0.25, 4.0)
    midbin = draw_midbin(jax.random.fold_in(streams_of[7], 71), 0)
    bin_row = draw_bin_row(jax.random.fold_in(streams_of[7], 71), 0)
    taps_shot = centred(streams_of[5], (KDIP, TAP_SHOT), TAP_SHOT ** -0.5, 1.0, (), jnp.float32)
    taps_time = centred(streams_of[6], (KDIP, TAP_TIME), TAP_TIME ** -0.5, 0.75, (), jnp.float32)
    return dict(gathers=gathers, trace_slot=trace_slot, gain=gain, midbin=midbin, bin_row=bin_row, taps_shot=taps_shot, taps_time=taps_time)


def to_bf16_exact(values):
    rounded = lax.optimization_barrier(values.astype(jnp.bfloat16))
    return rounded.astype(jnp.float32)

def reference(gathers, trace_slot, gain, midbin, bin_row, taps_shot, taps_time):
    tb = to_bf16_exact(taps_time)
    ts = to_bf16_exact(taps_shot)
    shot_rows = jnp.arange(SHOTS, dtype=jnp.int32)[:, None]
    scale_out = (NBINS / (SHOTS * CHANNELS)) ** 0.5

    def one_block(stack_acc, index):
        start = (index * RPD).astype(jnp.int32)
        slots = lax.dynamic_slice_in_dim(trace_slot, start, RPD, 1)
        gains = lax.dynamic_slice_in_dim(gain, start, RPD, 1)
        bins = lax.dynamic_slice_in_dim(midbin, start, RPD, 1)
        picked = gathers[shot_rows, slots].astype(jnp.float32)
        scaled = to_bf16_exact(picked * gains[:, :, None])
        lhs = scaled.reshape(SHOTS * RPD, 1, NT)
        timed = lax.conv_general_dilated(lhs, tb[:, None, :], (1,), [(32, TAP_TIME - 33)], precision=lax.Precision.HIGHEST)
        middle = to_bf16_exact(timed)
        middle = middle.reshape(SHOTS, RPD, KDIP, NT).transpose(1, 3, 2, 0).reshape(RPD * NT, KDIP, SHOTS)
        shotted = lax.conv_general_dilated(middle, ts[None, :, :], (1,), [(15, TAP_SHOT - 16)], precision=lax.Precision.HIGHEST)
        filt = shotted.reshape(RPD, NT, SHOTS).transpose(2, 0, 1)
        rms = jnp.sqrt(lax.optimization_barrier(jnp.mean(filt * filt, axis=-1, keepdims=True)) + 1e-06)
        trace = to_bf16_exact(filt / rms)
        rows = bin_row[bins].reshape(-1)
        stack_acc = stack_acc.at[rows].add(trace.reshape(SHOTS * RPD, NT))
        return (stack_acc, None)
    blocks = jnp.arange(CHANNELS // RPD, dtype=jnp.int32)
    stack, unused = lax.scan(one_block, jnp.zeros((NBINS, NT), jnp.float32), blocks)
    return stack * scale_out
```

```python
import jax
import jax.numpy as jnp
from jax import lax
from jax.experimental import pallas as pl
from jax.experimental.pallas import tpu as pltpu
from jax.sharding import Mesh
from jax.sharding import PartitionSpec as P

BF = jnp.bfloat16
F32 = jnp.float32
I32 = jnp.int32
SHOTS, RPD, CHUNKS, PER = 64, 30, 2, 15
ROWS = 16
CROWS = SHOTS * ROWS
VALID = SHOTS * PER
NT, BLK, BIN = 512, 1920, 128
YROWS = VALID + 16
QMAX = (YROWS - 128) // 16
VMEM = pl.BlockSpec(memory_space=pltpu.VMEM)
SMEM = pl.BlockSpec(memory_space=pltpu.SMEM)


def params():
    return pltpu.CompilerParams(vmem_limit_bytes=60 * 1024 * 1024)


def iota(shape, dim):
    return lax.broadcasted_iota(I32, shape, dim)


def mask_bf(mask):
    return jnp.where(mask, 1.0, 0.0).astype(BF)


def mm(a, b):
    return jnp.dot(a, b, preferred_element_type=F32)


def mm_nt(a, b):
    return lax.dot_general(a, b, (((1,), (1,)), ((), ())), preferred_element_type=F32)


def pick_kernel(chunk, x_ref, slot_ref, gain_ref, mid_ref, tab_ref, out_ref):
    table = tab_ref[...]
    owners = lax.shift_right_logical(table, 7).astype(F32).astype(BF)
    locals_ = (table & 127).astype(F32).astype(BF)

    row = iota((128, RPD), 0) & 15
    wanted = (iota((128, RPD), 1) == chunk * PER + row) & (row < PER)

    def column(block):
        tall = jnp.broadcast_to(block[:, None, :], (8, 16, RPD)).reshape(128, RPD)
        return jnp.sum(jnp.where(wanted, tall, 0.0), axis=1, keepdims=True)

    in_block = iota((128, 1), 0) & 15
    real = in_block < PER

    def body(b, carry):
        at = pl.ds(pl.multiple_of(b * 8, 8), 8)
        slot = column(slot_ref[at, :].astype(F32)).astype(I32)
        slot = jnp.where(real, slot, -1)
        gain = column(gain_ref[at, :])
        mid = column(mid_ref[at, :].astype(F32)).astype(I32)
        high = lax.shift_right_logical(mid, 7)
        low = mid & 127
        pick_row = mask_bf(iota((128, 64), 1) == high)
        pick_lane = iota((128, 128), 1) == low
        owner = jnp.sum(jnp.where(pick_lane, mm(pick_row, owners), 0.0), axis=1, keepdims=True)
        local = jnp.sum(jnp.where(pick_lane, mm(pick_row, locals_), 0.0), axis=1, keepdims=True)
        lane = iota((128, NT), 1)
        spread = jnp.where(lane < NT // 2, owner, local)
        spread = jnp.where(((lane & 15) == in_block) & real, spread, 0.0).astype(BF)
        here, there = iota((128, 128), 0), iota((128, 128), 1)
        gather = mask_bf((lax.shift_right_logical(here, 4) == lax.shift_right_logical(there, 4)) & ((here & 15) == 15))
        one_hot = mask_bf(iota((128, BLK), 1) == slot)
        picked = mm(one_hot, x_ref[...])
        out = picked * gain + mm(gather, spread)
        out_ref[pl.ds(pl.multiple_of(b * 128, 128), 128), :] = out.astype(BF)
        return carry

    lax.fori_loop(0, CROWS // 128, body, 0)


def pick(chunk, x, slot, gain, mid, table):
    return pl.pallas_call(
        lambda *refs: pick_kernel(chunk, *refs),
        out_shape=jax.ShapeDtypeStruct((CROWS, NT), BF),
        in_specs=[VMEM] * 5,
        out_specs=VMEM,
        compiler_params=params(),
        name=f"pick{chunk}",
    )(x, slot, gain, mid, table)


def band_kernel(time_ref, shot_ref, time_out, shot_out):
    for k in range(3):
        base = jnp.broadcast_to(time_ref[k : k + 1, :], (NT, NT))
        rolled = pltpu.roll(base, 0, 1, stride=1, stride_axis=0)
        delta = iota((NT, NT), 1) - iota((NT, NT), 0)
        inside = (delta >= -31) & (delta <= 32)
        time_out[:, k * NT : (k + 1) * NT] = jnp.where(inside, rolled, 0.0).astype(BF)
        base = jnp.broadcast_to(shot_ref[k : k + 1, :], (256, 768))
        shot_out[k] = pltpu.roll(base, 0, 1, stride=1, stride_axis=0).astype(BF)


def bands(taps_time, taps_shot):
    rev = taps_time.astype(BF).astype(F32)[:, ::-1]
    time_row = jnp.concatenate([rev[:, 31:], jnp.zeros((3, NT - 64), F32), rev[:, :31]], axis=1)
    shot = taps_shot.astype(BF).astype(F32)
    shot_row = lax.pad(shot, jnp.float32(0), ((0, 0, 0), (16, 768 - 16 - 481, 15)))
    return pl.pallas_call(
        band_kernel,
        out_shape=(jax.ShapeDtypeStruct((NT, 3 * NT), BF), jax.ShapeDtypeStruct((3, 256, 768), BF)),
        in_specs=[VMEM] * 2,
        out_specs=(VMEM, VMEM),
        compiler_params=params(),
        name="bands",
    )(time_row, shot_row)


def filter_kernel(x_ref, time_ref, shot_ref, out_ref, mid_ref, trace_ref):
    for b in range(4):
        rows = slice(256 * b, 256 * b + 256)
        for k in range(3):
            mid_ref[k, rows, :] = mm(x_ref[rows, :], time_ref[:, k * NT : (k + 1) * NT]).astype(BF)
    for b in range(4):
        lo, hi = max(0, b - 1), min(4, b + 2)
        band = slice(256 * (lo - b + 1), 256 * (hi - b + 1))
        filt = jnp.zeros((256, NT), F32)
        for k in range(3):
            filt = filt + mm(shot_ref[k, :, band], mid_ref[k, 256 * lo : 256 * hi, :])
        power = jnp.mean(filt * filt, axis=1, keepdims=True) + 1e-6
        trace_ref[256 * b : 256 * b + 256, :] = (filt * lax.rsqrt(power)).astype(BF)
    row = iota((256, NT), 0)
    lane = iota((256, NT), 1)
    keep = ((row & 15) == 15) & (lax.shift_right_logical(row, 4) == lax.shift_right_logical(lane & 255, 4))
    owner, local = [], []
    for b in range(4):
        part = jnp.where(keep, x_ref[256 * b : 256 * b + 256, :].astype(F32), 0.0)
        ids = jnp.sum(part, axis=0, keepdims=True)
        owner.append(ids[:, :256])
        local.append(ids[:, 256:])
    bad = (iota((1, 256), 1) & 15) == 15
    owner = [jnp.where(bad, 127.0, o) for o in owner]
    before = jnp.zeros((128, 1), F32)
    upper = mask_bf(iota((256, 256), 0) < iota((256, 256), 1))
    marks, ranks = [], []
    for b in range(4):
        mark = jnp.where(iota((128, 256), 0).astype(F32) == owner[b], 1.0, 0.0)
        ranks.append(mm(mark.astype(BF), upper) + before)
        marks.append(mark)
        before = before + jnp.sum(mark, axis=1, keepdims=True)
    lower = mask_bf(iota((128, 128), 1) < iota((128, 128), 0))
    starts = mm(lower, jnp.broadcast_to(before, (128, 128)).astype(BF))[:, :1]
    places = [jnp.sum(marks[b] * (ranks[b] + starts), axis=0, keepdims=True) for b in range(4)]
    place = jnp.concatenate(places, axis=1).astype(I32)
    owner = jnp.concatenate(owner, axis=1)
    local = jnp.concatenate(local, axis=1)
    place_lane = mask_bf(iota((128, CROWS), 0) == (place & 127))
    here = iota((8, CROWS), 0) == lax.shift_right_logical(place, 7)
    ids = jnp.concatenate([jnp.where(here, owner, 0.0), jnp.where(here, local, 0.0)], axis=0)
    ids = mm_nt(ids.astype(BF), place_lane)
    less = mask_bf(owner < iota((128, CROWS), 0).astype(F32))
    first = mm_nt(jnp.ones((16, CROWS), BF), less)
    first = jnp.minimum(lax.shift_right_logical(first.astype(I32), 4), QMAX).astype(F32)
    first = pltpu.roll(first, 64, 1)
    r, c = iota((16, 128), 0), iota((16, 128), 1)
    ids = jnp.where((r == 7) & (c >= 64), first, ids).astype(BF)
    for b in range(4):
        size = 256 if b < 3 else VALID - 768
        order = mask_bf(iota((size, CROWS), 0) + 256 * b == place)
        rows = mm(order, trace_ref[...]).astype(BF)
        for y in range(4):
            out_ref[y, 256 * b : 256 * b + size, :] = rows[:, 128 * y : 128 * y + 128]
    for y in range(4):
        out_ref[y, VALID:, :] = ids


def filtered(x, time_band, shot_band, name):
    return pl.pallas_call(
        filter_kernel,
        out_shape=jax.ShapeDtypeStruct((4, YROWS, 128), BF),
        in_specs=[VMEM] * 3,
        out_specs=VMEM,
        scratch_shapes=[pltpu.VMEM((3, CROWS, NT), BF), pltpu.VMEM((CROWS, NT), BF)],
        compiler_params=params(),
        name=name,
    )(x, time_band, shot_band)


def stack_kernel(core_ref, first_ref, *refs):
    lists, (mine_ref, other_ref, table_ref) = refs[:-3], refs[-3:]
    lane = iota((8, 128), 1)
    sub = iota((8, 128), 0)
    for n, ref in enumerate(lists):
        ids = ref[VALID:, :].astype(F32)
        owner, local = ids[:8], ids[8:]
        code = jnp.where((sub == 7) & (lane >= 64), -1.0, owner * 128.0 + local)
        after = pltpu.roll(code, 7, 0)
        for e in range(8):
            if e == 0:
                table_ref[n, 0] = code
            else:
                a = pltpu.roll(code, 128 - 16 * e, 1)
                b = pltpu.roll(after, 128 - 16 * e, 1)
                table_ref[n, e] = jnp.where(lane < 128 - 16 * e, a, b)
    bins = iota((128, 128), 0).astype(F32)
    core = core_ref[0]
    for target, out_ref in ((core, mine_ref), (1 - core, other_ref)):

        def body(pair, carry):
            o = pair * 2 + target
            want = bins + (o * 128).astype(F32)
            total = jnp.zeros((128, 128), F32)
            for n in range(0, len(lists), 2):
                hots, rows = [], []
                for m in (n, n + 1):
                    q = first_ref[m, o]
                    row = table_ref[m, q & 7, pl.ds(lax.shift_right_logical(q, 3), 1), :]
                    hots.append(mask_bf(row == want))
                    rows.append(lists[m][pl.ds(pl.multiple_of(q * 16, 16), 128), :])
                total = total + mm(jnp.concatenate(hots, axis=1), jnp.concatenate(rows, axis=0))
            out_ref[pair] = total.astype(BF)
            return carry

        lax.fori_loop(0, SHOTS // 2, body, 0)


def stacked(core, first, lists):
    half = jax.ShapeDtypeStruct((SHOTS // 2, BIN, 128), BF)
    return pl.pallas_call(
        stack_kernel,
        out_shape=(half, half),
        in_specs=[SMEM, SMEM] + [VMEM] * len(lists),
        out_specs=(VMEM, VMEM),
        scratch_shapes=[pltpu.VMEM((len(lists), 8, 8, 128), F32)],
        compiler_params=params(),
        name="stack",
    )(core, first, *lists)


def per_device(gathers, trace_slot, gain, midbin, bin_row, taps_shot, taps_time):
    y_pos = lax.axis_index("y")
    x = gathers.reshape(BLK, NT)
    slot = (trace_slot - y_pos * BLK).reshape(SHOTS, RPD)
    gain = gain.reshape(SHOTS, RPD)
    mid = midbin.reshape(SHOTS, RPD)
    table = bin_row.reshape(64, 128)
    time_band, shot_band = bands(taps_time, taps_shot)
    lists = []
    for c in range(CHUNKS):
        send = pick(c, x, slot, gain, mid, table).reshape(SHOTS, ROWS, NT)
        got = lax.all_to_all(send, ("x", "z", "c"), split_axis=0, concat_axis=0, tiled=True)
        quarters = filtered(got.reshape(CROWS, NT), time_band, shot_band, f"filter{c}")
        own = lax.dynamic_index_in_dim(quarters, y_pos, 0, keepdims=False)
        lists.append(own)
        for d in (1, 2, 3):
            part = lax.dynamic_index_in_dim(quarters, (y_pos + d) & 3, 0, keepdims=False)
            lists.append(lax.ppermute(part, "y", [(i, (i + d) % 4) for i in range(4)]))
    first = jnp.stack([v[VALID + 7, 64:] for v in lists]).astype(I32)
    core = lax.axis_index("c").reshape(1)
    mine, other = stacked(core, first, lists)
    other = lax.ppermute(other, "c", [(0, 1), (1, 0)])
    both = (mine.astype(F32) + other.astype(F32)).astype(BF)
    parts = lax.all_to_all(both, ("x", "z"), split_axis=0, concat_axis=0, tiled=True)
    scale = (8192 / 491520) ** 0.5
    return jnp.sum(parts.astype(F32), axis=0) * scale


def solution(mesh):
    finer = Mesh(mesh.devices.reshape(4, 8, 2, mesh.shape["cmp"]), ("x", "z", "c", "y"))
    shot = ("x", "z", "c")
    in_specs = (P(shot, "y", None), P(shot, "y"), P(shot, "y"), P(shot, "y"), P(), P(), P())
    return jax.shard_map(
        per_device, mesh=finer, in_specs=in_specs, out_specs=P(shot, "y"), check_vma=False
    )
```

```python
import jax
import jax.numpy as jnp
from jax import lax
from jax.experimental import pallas as pl
from jax.experimental.pallas import tpu as pltpu
from jax.sharding import Mesh
from jax.sharding import PartitionSpec as P

BF = jnp.bfloat16
F32 = jnp.float32
I32 = jnp.int32
SHOTS, RPD, CHUNKS, PER = 64, 30, 2, 15
ROWS = 16
CROWS = SHOTS * ROWS
VALID = SHOTS * PER
NT, BLK, BIN = 512, 1920, 128
YROWS = VALID + 16
QMAX = (YROWS - 64) // 16
WIDE = 640
VMEM = pl.BlockSpec(memory_space=pltpu.VMEM)
SMEM = pl.BlockSpec(memory_space=pltpu.SMEM)


def params():
    return pltpu.CompilerParams(vmem_limit_bytes=60 * 1024 * 1024)


def iota(shape, dim):
    return lax.broadcasted_iota(I32, shape, dim)


def mask_bf(mask):
    return jnp.where(mask, 1.0, 0.0).astype(BF)


def mm(a, b):
    return jnp.dot(a, b, preferred_element_type=F32)


def mm_nt(a, b):
    return lax.dot_general(a, b, (((1,), (1,)), ((), ())), preferred_element_type=F32)


def column(ref, base, wanted):
    row = ref[:, base : base + WIDE].astype(F32)
    return jnp.sum(jnp.where(wanted, row, 0.0), axis=1, keepdims=True)


def pick_kernel(chunk, x_ref, slot_ref, gain_ref, mid_ref, tab_ref, out_ref):
    table = tab_ref[...]
    owners = lax.shift_right_logical(table, 7).astype(F32).astype(BF)
    locals_ = (table & 127).astype(F32).astype(BF)
    here, there = iota((256, 256), 0), iota((256, 256), 1)
    gather = mask_bf((lax.shift_right_logical(here, 4) == lax.shift_right_logical(there, 4)) & ((here & 15) == 15))
    place = iota((256, 1), 0) & 15
    real = place < PER
    lane = iota((256, NT), 1)
    for b in range(CROWS // 256):
        base = (480 * b) // 128 * 128
        base = min(base, BLK - WIDE)
        receiver = (lax.shift_right_logical(iota((256, 1), 0), 4) + 16 * b) * RPD + chunk * PER + place
        wanted = (iota((256, WIDE), 1) + base == receiver) & real
        slot = column(slot_ref, base, wanted).astype(I32)
        block = (slot >= BLK).astype(I32) + (slot >= 2 * BLK).astype(I32) + (slot >= 3 * BLK).astype(I32)
        slot = jnp.where(real, slot - BLK * block, -1)
        gain = column(gain_ref, base, wanted)
        mid = column(mid_ref, base, wanted).astype(I32)
        pick_row = mask_bf(iota((256, 64), 1) == lax.shift_right_logical(mid, 7))
        pick_lane = iota((256, 128), 1) == (mid & 127)
        owner = jnp.sum(jnp.where(pick_lane, mm(pick_row, owners), 0.0), axis=1, keepdims=True)
        local = jnp.sum(jnp.where(pick_lane, mm(pick_row, locals_), 0.0), axis=1, keepdims=True)
        spread = jnp.where(lane < NT // 2, owner, local)
        spread = jnp.where(((lane & 15) == place) & real, spread, 0.0).astype(BF)
        one_hot = mask_bf(iota((256, BLK), 1) == slot)
        out = mm(one_hot, x_ref[...]) * gain + mm(gather, spread)
        out_ref[256 * b : 256 * b + 256, :] = out.astype(BF)


def pick(chunk, x, slot, gain, mid, table):
    return pl.pallas_call(
        lambda *refs: pick_kernel(chunk, *refs),
        out_shape=jax.ShapeDtypeStruct((CROWS, NT), BF),
        in_specs=[VMEM] * 5,
        out_specs=VMEM,
        compiler_params=params(),
        name=f"pick{chunk}",
    )(x, slot, gain, mid, table)


def band_kernel(time_ref, shot_ref, time_out, shot_out):
    step, col = iota((256, 128), 0), iota((256, 128), 1)
    wrapped = (step < 128) == (col < 32)
    for k in range(3):
        base = jnp.broadcast_to(time_ref[k : k + 1, :], (128, 256))
        rolled = pltpu.roll(base, 0, 1, stride=1, stride_axis=0)
        band = rolled.T
        at = slice(128 * k, 128 * k + 128)
        time_out[0, :, at] = band.astype(BF)
        time_out[1, :, at] = jnp.where(wrapped, band, 0.0).astype(BF)
        base = jnp.broadcast_to(shot_ref[k : k + 1, :], (256, 640))
        rolled = pltpu.roll(base, 0, 1, stride=1, stride_axis=0)
        shot_out[0, :, 384 * k : 384 * k + 384] = rolled[:, 128:512].astype(BF)
        shot_out[1, :, 384 * k : 384 * k + 384] = rolled[:, :384].astype(BF)


def bands(taps_time, taps_shot):
    time_row = jnp.pad(taps_time.astype(BF).astype(F32), ((0, 0), (64, 128)))
    shot = taps_shot.astype(BF).astype(F32)
    shot_row = lax.pad(shot, jnp.float32(0), ((0, 0, 0), (8, 640 - 8 - 241, 7)))
    return pl.pallas_call(
        band_kernel,
        out_shape=(jax.ShapeDtypeStruct((2, 256, 384), BF), jax.ShapeDtypeStruct((2, 256, 1152), BF)),
        in_specs=[VMEM] * 2,
        out_specs=(VMEM, VMEM),
        compiler_params=params(),
        name="bands",
    )(time_row, shot_row)


def filter_kernel(y_ref, x_ref, time_ref, shot_ref, out0, out1, out2, out3, mid_ref, trace_ref):
    outs = (out0, out1, out2, out3)
    for b in range(4):
        rows = slice(256 * b, 256 * b + 256)
        for j in range(4):
            if j:
                lhs, band = x_ref[rows, 128 * j - 128 : 128 * j + 128], time_ref[0]
            else:
                lhs = jnp.concatenate([x_ref[rows, 384:], x_ref[rows, :128]], axis=1)
                band = time_ref[1]
            mids = mm(lhs, band).reshape(16, 2, 8, 384)
            for half in range(2):
                part = mids[:, half].reshape(128, 384).astype(BF)
                for k in range(3):
                    value = part[:, 128 * k : 128 * k + 128]
                    for w in range(2):
                        at = 128 * b - 128 * w
                        if 0 <= at < 384:
                            at += 384 * k
                            mid_ref[half, w, at : at + 128, 128 * j : 128 * j + 128] = value
    y_pos = y_ref[0]
    for w in range(2):
        both = []
        for half in range(2):
            filt = mm(shot_ref[w], mid_ref[half, w])
            power = jnp.mean(filt * filt, axis=1, keepdims=True) + 1e-6
            done = pltpu.roll(filt * lax.rsqrt(power), NT - 32, 1)
            both.append(done.reshape(32, 1, 8, NT))
        trace = jnp.concatenate(both, axis=1).reshape(512, NT).astype(BF)
        for y in range(4):
            trace_ref[(y - y_pos) & 3, 512 * w : 512 * w + 512, :] = trace[:, 128 * y : 128 * y + 128]
    row = iota((256, NT), 0)
    lane = iota((256, NT), 1)
    keep = ((row & 15) == 15) & (lax.shift_right_logical(row, 4) == lax.shift_right_logical(lane & 255, 4))
    owner, local = [], []
    for b in range(4):
        part = jnp.where(keep, x_ref[256 * b : 256 * b + 256, :].astype(F32), 0.0)
        ids = jnp.sum(part, axis=0, keepdims=True)
        owner.append(ids[:, :256])
        local.append(ids[:, 256:])
    bad = (iota((1, 256), 1) & 15) == 15
    owner = [jnp.where(bad, 127.0, o) for o in owner]
    before = jnp.zeros((128, 1), F32)
    upper = mask_bf(iota((256, 256), 0) < iota((256, 256), 1))
    marks, ranks = [], []
    for b in range(4):
        mark = jnp.where(iota((128, 256), 0).astype(F32) == owner[b], 1.0, 0.0)
        ranks.append(mm(mark.astype(BF), upper) + before)
        marks.append(mark)
        before = before + jnp.sum(mark, axis=1, keepdims=True)
    lower = mask_bf(iota((128, 128), 1) < iota((128, 128), 0))
    starts = mm(lower, jnp.broadcast_to(before, (128, 128)).astype(BF))[:, :1]
    places = [jnp.sum(marks[b] * (ranks[b] + starts), axis=0, keepdims=True) for b in range(4)]
    place = jnp.concatenate(places, axis=1).astype(I32)
    owner = jnp.concatenate(owner, axis=1)
    local = jnp.concatenate(local, axis=1)
    place_lane = mask_bf(iota((128, CROWS), 0) == (place & 127))
    here = iota((8, CROWS), 0) == lax.shift_right_logical(place, 7)
    ids = jnp.concatenate([jnp.where(here, owner, 0.0), jnp.where(here, local, 0.0)], axis=0)
    ids = mm_nt(ids.astype(BF), place_lane)
    first = jnp.broadcast_to(starts, (128, 128)).T[:16]
    first = lax.shift_right_logical(first.astype(I32), 4).astype(F32)
    first = pltpu.roll(first, 64, 1)
    r, c = iota((16, 128), 0), iota((16, 128), 1)
    ids = jnp.where((r == 7) & (c >= 64), first, ids).astype(BF)
    traces = jnp.concatenate([trace_ref[d] for d in range(4)], axis=1)
    for b in range(2):
        size = min(512, VALID - 512 * b)
        order = mask_bf(iota((size, CROWS), 0) + 512 * b == place)
        rows = mm(order, traces).astype(BF)
        for d in range(4):
            outs[d][512 * b : 512 * b + size, :] = rows[:, 128 * d : 128 * d + 128]
    for d in range(4):
        outs[d][VALID:, :] = ids


def filtered(y_pos, x, time_band, shot_band, name):
    return pl.pallas_call(
        filter_kernel,
        out_shape=[jax.ShapeDtypeStruct((YROWS, 128), BF)] * 4,
        in_specs=[SMEM] + [VMEM] * 3,
        out_specs=[VMEM] * 4,
        scratch_shapes=[pltpu.VMEM((2, 2, 1152, NT), BF), pltpu.VMEM((4, CROWS, 128), BF)],
        compiler_params=params(),
        name=name,
    )(y_pos, x, time_band, shot_band)


def stack_kernel(last, core_ref, first_ref, l0, l1, l2, l3, *refs):
    lists = (l0, l1, l2, l3)
    table_ref = refs[-1]
    lane = iota((8, 128), 1)
    sub = iota((8, 128), 0)
    for n, ref in enumerate(lists):
        ids = ref[VALID:, :].astype(F32)
        code = jnp.where((sub == 7) & (lane >= 64), -1.0, ids[:8] * 128.0 + ids[8:])
        after = pltpu.roll(code, 7, 0)
        for e in range(8):
            shift = (64 * (n & 1) - 16 * e) % 128
            limit = 128 + 64 * (n & 1) - 16 * e
            a = pltpu.roll(code, shift, 1) if shift else code
            b = pltpu.roll(after, shift, 1) if shift else after
            table_ref[n, e] = jnp.where(lane < limit, a, b)
    core = core_ref[0]
    bins = iota((256, 1), 0)
    bins = (bins & 127) + jnp.where(bins < 128, core, 1 - core) * 128
    flat = iota((1, 128), 1)
    low = flat < 64

    def window(pair, w):
        want = (bins + pair * 256).astype(F32)
        codes, rows = [], []
        for n in range(4):
            q0 = first_ref[n, 2 * pair] + 4 * w
            q = jnp.minimum(q0, QMAX)
            code = table_ref[n, q & 7, pl.ds(lax.shift_right_logical(q, 3), 1), :]
            codes.append(jnp.where((flat & 63) >= (q0 - q) * 16, code, -1.0))
            rows.append(lists[n][pl.ds(pl.multiple_of(q * 16, 16), 64), :])
        left = mask_bf(jnp.where(low, codes[0], codes[1]) == want)
        right = mask_bf(jnp.where(low, codes[2], codes[3]) == want)
        return mm(jnp.concatenate([left, right], axis=1), jnp.concatenate(rows, axis=0))

    def store(pair, total):
        if last:
            total = total + refs[0][pair]
            refs[1][pair] = total[:128].astype(BF)
            refs[2][pair] = total[128:].astype(BF)
        else:
            refs[0][pair] = total

    def body(pair, carry):
        store(pair, window(pair, 0))
        return carry

    lax.fori_loop(0, SHOTS // 2, body, 0, unroll=4)

    def rest(pair, carry):
        count = jnp.int32(1)
        for n in range(4):
            after = first_ref[n, 2 * pair + 2]
            count = jnp.maximum(count, lax.shift_right_logical(after - first_ref[n, 2 * pair] + 4, 2))

        @pl.when(count > 1)
        def _():
            total = lax.fori_loop(1, count, lambda w, t: t + window(pair, w), window(pair, 0))
            store(pair, total)

        return carry

    lax.fori_loop(0, SHOTS // 2, rest, 0)


def stacked(core, lists, sums=None):
    first = jnp.stack([v[VALID + 7, 64:] for v in lists]).astype(I32)
    first = jnp.pad(first, ((0, 0), (0, 64)), constant_values=VALID // 16)
    if sums is None:
        out_shape, extra = jax.ShapeDtypeStruct((SHOTS // 2, 256, 128), F32), []
    else:
        out_shape, extra = (jax.ShapeDtypeStruct((SHOTS // 2, BIN, 128), BF),) * 2, [sums]
    return pl.pallas_call(
        lambda *refs: stack_kernel(sums is not None, *refs),
        out_shape=out_shape,
        in_specs=[SMEM, SMEM] + [VMEM] * (4 + len(extra)),
        out_specs=VMEM if sums is None else (VMEM, VMEM),
        scratch_shapes=[pltpu.VMEM((4, 8, 8, 128), F32)],
        compiler_params=params(),
        name="stack0" if sums is None else "stack1",
    )(core, first, *lists, *extra)


def fold_kernel(x_ref, mine_ref, other_ref, *outs):
    for d in range(4):
        at = pl.ds(8 * ((x_ref[0] + d) & 3), 8)
        outs[d][...] = (mine_ref[at].astype(F32) + other_ref[at].astype(F32)).astype(BF)


def folded(x_pos, mine, other):
    return pl.pallas_call(
        fold_kernel,
        out_shape=[jax.ShapeDtypeStruct((8, BIN, 128), BF)] * 4,
        in_specs=[SMEM, VMEM, VMEM],
        out_specs=[VMEM] * 4,
        compiler_params=params(),
        name="fold",
    )(x_pos, mine, other)


def around(parts, axis):
    n = len(parts)
    return [parts[0]] + [lax.ppermute(parts[d], axis, [(i, (i + d) % n) for i in range(n)]) for d in range(1, n)]


def per_device(gathers, trace_slot, gain, midbin, bin_row, taps_shot, taps_time):
    x_pos, y_pos, core = (lax.axis_index(a).reshape(1) for a in ("x", "y", "c"))
    x = gathers.reshape(BLK, NT)
    table = bin_row.reshape(64, 128)
    time_band, shot_band = bands(taps_time, taps_shot)
    got = []
    for c in range(CHUNKS):
        send = pick(c, x, trace_slot, gain, midbin, table).reshape(SHOTS, ROWS, NT)
        part = lax.all_to_all(send, ("x", "z", "c"), split_axis=0, concat_axis=0, tiled=True)
        got.append(part.reshape(CROWS, NT))
    lists = around(filtered(y_pos, got[0], time_band, shot_band, "filter0"), "y")
    lists, got[1] = lax.optimization_barrier((lists, got[1]))
    sums = stacked(core, lists)
    lists = around(filtered(y_pos, got[1], time_band, shot_band, "filter1"), "y")
    mine, other = stacked(core, lists, sums)
    other = lax.ppermute(other, "c", [(0, 1), (1, 0)])
    parts = around(folded(x_pos, mine, other), "x")
    total = sum(p.astype(F32) for p in parts).astype(BF)
    parts = lax.all_to_all(total, "z", split_axis=0, concat_axis=0, tiled=True)
    scale = (8192 / 491520) ** 0.5
    return jnp.sum(parts.astype(F32), axis=0) * scale


def solution(mesh):
    finer = Mesh(mesh.devices.reshape(4, 8, 2, mesh.shape["cmp"]), ("x", "z", "c", "y"))
    shot = ("x", "z", "c")
    in_specs = (P(shot, "y", None), P(shot, "y"), P(shot, "y"), P(shot, "y"), P(), P(), P())
    return jax.shard_map(
        per_device, mesh=finer, in_specs=in_specs, out_specs=P(shot, "y"), check_vma=False
    )
```

```python
import jax
import jax.numpy as jnp
from jax import lax
from jax.experimental import pallas as pl
from jax.experimental.pallas import tpu as pltpu
from jax.sharding import Mesh
from jax.sharding import PartitionSpec as P

BF = jnp.bfloat16
F32 = jnp.float32
I32 = jnp.int32
SHOTS, RPD, CHUNKS, PER = 64, 30, 2, 15
ROWS = 16
CROWS = SHOTS * ROWS
VALID = SHOTS * PER
NT, BLK, BIN = 512, 1920, 128
YROWS = VALID + 16
QMAX = (YROWS - 64) // 16
WIDE = 640
VMEM = pl.BlockSpec(memory_space=pltpu.VMEM)
SMEM = pl.BlockSpec(memory_space=pltpu.SMEM)


def params(mib=24):
    return pltpu.CompilerParams(vmem_limit_bytes=mib * 1024 * 1024)


def iota(shape, dim):
    return lax.broadcasted_iota(I32, shape, dim)


def mask_bf(mask):
    return jnp.where(mask, 1.0, 0.0).astype(BF)


def mm(a, b):
    return jnp.dot(a, b, preferred_element_type=F32)


def mm_nt(a, b):
    return lax.dot_general(a, b, (((1,), (1,)), ((), ())), preferred_element_type=F32)


def column(ref, base, wanted):
    row = ref[:, base : base + WIDE].astype(F32)
    return jnp.sum(jnp.where(wanted, row, 0.0), axis=1, keepdims=True)


def pick_kernel(chunk, x_ref, slot_ref, gain_ref, mid_ref, tab_ref, out_ref):
    table = tab_ref[...]
    owners = lax.shift_right_logical(table, 7).astype(F32).astype(BF)
    locals_ = (table & 127).astype(F32).astype(BF)
    here, there = iota((256, 256), 0), iota((256, 256), 1)
    gather = mask_bf((lax.shift_right_logical(here, 4) == lax.shift_right_logical(there, 4)) & ((here & 15) == 15))
    place = iota((256, 1), 0) & 15
    real = place < PER
    lane = iota((256, NT), 1)

    def columns(b):
        base = min((480 * b) // 128 * 128, BLK - WIDE)
        receiver = (lax.shift_right_logical(iota((256, 1), 0), 4) + 16 * b) * RPD + chunk * PER + place
        wanted = (iota((256, WIDE), 1) + base == receiver) & real
        slot = column(slot_ref, base, wanted).astype(I32)
        block = (slot >= BLK).astype(I32) + (slot >= 2 * BLK).astype(I32) + (slot >= 3 * BLK).astype(I32)
        slot = jnp.where(real, slot - BLK * block, -1)
        gain = column(gain_ref, base, wanted)
        mid = column(mid_ref, base, wanted).astype(I32)
        pick_row = mask_bf(iota((256, 64), 1) == lax.shift_right_logical(mid, 7))
        pick_lane = iota((256, 128), 1) == (mid & 127)
        owner = jnp.sum(jnp.where(pick_lane, mm(pick_row, owners), 0.0), axis=1, keepdims=True)
        local = jnp.sum(jnp.where(pick_lane, mm(pick_row, locals_), 0.0), axis=1, keepdims=True)
        spread = jnp.where(lane < NT // 2, owner, local)
        spread = jnp.where(((lane & 15) == place) & real, spread, 0.0).astype(BF)
        return slot, gain, spread

    for b in range(CROWS // 256):
        slot, gain, spread = columns(b)
        one_hot = mask_bf(iota((256, BLK), 1) == slot)
        out = mm(one_hot, x_ref[...]) * gain + mm(gather, spread)
        out_ref[256 * b : 256 * b + 256, :] = out.astype(BF)


def pick(chunk, x, slot, gain, mid, table):
    return pl.pallas_call(
        lambda *refs: pick_kernel(chunk, *refs),
        out_shape=jax.ShapeDtypeStruct((CROWS, NT), BF),
        in_specs=[VMEM] * 5,
        out_specs=VMEM,
        compiler_params=params(),
        name=f"pick{chunk}",
    )(x, slot, gain, mid, table)


def band_kernel(time_ref, shot_ref, time_out, shot_out):
    step, col = iota((256, 128), 0), iota((256, 128), 1)
    wrapped = (step < 128) == (col < 32)
    for k in range(3):
        base = jnp.broadcast_to(time_ref[k : k + 1, :], (128, 256))
        rolled = pltpu.roll(base, 0, 1, stride=1, stride_axis=0)
        band = rolled.T
        at = slice(128 * k, 128 * k + 128)
        time_out[0, :, at] = band.astype(BF)
        time_out[1, :, at] = jnp.where(wrapped, band, 0.0).astype(BF)
        base = jnp.broadcast_to(shot_ref[k : k + 1, :], (256, 640))
        rolled = pltpu.roll(base, 0, 1, stride=1, stride_axis=0)
        shot_out[0, :, 384 * k : 384 * k + 384] = rolled[:, 128:512].astype(BF)
        shot_out[1, :, 384 * k : 384 * k + 384] = rolled[:, :384].astype(BF)


def bands(taps_time, taps_shot):
    time_row = jnp.pad(taps_time.astype(BF).astype(F32), ((0, 0), (64, 128)))
    shot = taps_shot.astype(BF).astype(F32)
    shot_row = lax.pad(shot, jnp.float32(0), ((0, 0, 0), (8, 640 - 8 - 241, 7)))
    return pl.pallas_call(
        band_kernel,
        out_shape=(jax.ShapeDtypeStruct((2, 256, 384), BF), jax.ShapeDtypeStruct((2, 256, 1152), BF)),
        in_specs=[VMEM] * 2,
        out_specs=(VMEM, VMEM),
        compiler_params=params(),
        name="bands",
    )(time_row, shot_row)


def filter_kernel(y_ref, x_ref, time_ref, shot_ref, out0, out1, out2, out3, mid_ref, trace_ref):
    outs = (out0, out1, out2, out3)
    row = iota((256, NT), 0)
    lane = iota((256, NT), 1)
    keep = ((row & 15) == 15) & (lax.shift_right_logical(row, 4) == lax.shift_right_logical(lane & 255, 4))
    bad = (iota((1, 256), 1) & 15) == 15
    upper = mask_bf(iota((256, 256), 0) < iota((256, 256), 1))
    owner, local, marks, ranks = [], [], [], []
    before = jnp.zeros((128, 1), F32)
    for b in range(4):
        rows = slice(256 * b, 256 * b + 256)
        part = jnp.where(keep, x_ref[rows, :].astype(F32), 0.0)
        ids = jnp.sum(part, axis=0, keepdims=True)
        owner.append(jnp.where(bad, 127.0, ids[:, :256]))
        local.append(ids[:, 256:])
        for j in range(4):
            if j:
                lhs, band = x_ref[rows, 128 * j - 128 : 128 * j + 128], time_ref[0]
            else:
                lhs = jnp.concatenate([x_ref[rows, 384:], x_ref[rows, :128]], axis=1)
                band = time_ref[1]
            mids = mm(lhs, band).reshape(16, 2, 8, 384)
            for half in range(2):
                part = mids[:, half].reshape(128, 384).astype(BF)
                for k in range(3):
                    value = part[:, 128 * k : 128 * k + 128]
                    for w in range(2):
                        at = 128 * b - 128 * w
                        if 0 <= at < 384:
                            at += 384 * k
                            mid_ref[half, w, at : at + 128, 128 * j : 128 * j + 128] = value
            if j == 1:
                mark = jnp.where(iota((128, 256), 0).astype(F32) == owner[b], 1.0, 0.0)
                ranks.append(mm(mark.astype(BF), upper) + before)
                marks.append(mark)
                before = before + jnp.sum(mark, axis=1, keepdims=True)
    lower = mask_bf(iota((128, 128), 1) < iota((128, 128), 0))
    starts = mm(lower, jnp.broadcast_to(before, (128, 128)).astype(BF))[:, :1]
    y_pos = y_ref[0]
    places = []
    for w in range(2):
        both = []
        for half in range(2):
            filt = mm(shot_ref[w], mid_ref[half, w])
            power = jnp.mean(filt * filt, axis=1, keepdims=True) + 1e-6
            done = pltpu.roll(filt * lax.rsqrt(power), NT - 32, 1)
            both.append(done.reshape(32, 1, 8, NT))
            b = 2 * w + half
            places.append(jnp.sum(marks[b] * (ranks[b] + starts), axis=0, keepdims=True))
        trace = jnp.concatenate(both, axis=1).reshape(512, NT).astype(BF)
        for y in range(4):
            trace_ref[(y - y_pos) & 3, 512 * w : 512 * w + 512, :] = trace[:, 128 * y : 128 * y + 128]
    place = jnp.concatenate(places, axis=1).astype(I32)
    owner = jnp.concatenate(owner, axis=1)
    local = jnp.concatenate(local, axis=1)
    place_lane = mask_bf(iota((128, CROWS), 0) == (place & 127))
    here = iota((8, CROWS), 0) == lax.shift_right_logical(place, 7)
    ids = jnp.concatenate([jnp.where(here, owner, 0.0), jnp.where(here, local, 0.0)], axis=0)
    ids = mm_nt(ids.astype(BF), place_lane)
    first = jnp.broadcast_to(starts, (128, 128)).T[:16]
    first = lax.shift_right_logical(first.astype(I32), 4)
    count = lax.shift_right_logical(pltpu.roll(first, 126, 1) - first + 4, 2)
    count = jnp.maximum(count, 1).astype(F32).astype(BF)
    first = jnp.minimum(first, QMAX).astype(F32).astype(BF)
    here, there = iota((128, 128), 0), iota((128, 128), 1)
    even = 2 * (there & 31)
    pick_first = mask_bf((here == even) & (there >= 64) & (there < 96))
    pick_count = mask_bf((here == even) & (there >= 96))
    first = mm(first, pick_first) + mm(count, pick_count)
    r, c = iota((16, 128), 0), iota((16, 128), 1)
    ids = jnp.where((r == 7) & (c >= 64), first, ids).astype(BF)
    traces = jnp.concatenate([trace_ref[d] for d in range(4)], axis=1)
    for b in range(2):
        size = min(512, VALID - 512 * b)
        order = mask_bf(iota((size, CROWS), 0) + 512 * b == place)
        rows = mm(order, traces).astype(BF)
        for d in range(4):
            outs[d][512 * b : 512 * b + size, :] = rows[:, 128 * d : 128 * d + 128]
    for d in range(4):
        outs[d][VALID:, :] = ids


def filtered(y_pos, x, time_band, shot_band, name):
    return pl.pallas_call(
        filter_kernel,
        out_shape=[jax.ShapeDtypeStruct((YROWS, 128), BF)] * 4,
        in_specs=[SMEM] + [VMEM] * 3,
        out_specs=[VMEM] * 4,
        scratch_shapes=[pltpu.VMEM((2, 2, 1152, NT), BF), pltpu.VMEM((4, CROWS, 128), BF)],
        compiler_params=params(),
        name=name,
    )(y_pos, x, time_band, shot_band)


def stack_kernel(last, core_ref, info_ref, l0, l1, l2, l3, *refs):
    lists = (l0, l1, l2, l3)
    table_ref, long_ref = refs[-2:]
    lane = iota((8, 128), 1)
    sub = iota((8, 128), 0)
    for n, ref in enumerate(lists):
        ids = ref[VALID:, :].astype(F32)
        code = jnp.where((sub == 7) & (lane >= 64), -1.0, ids[:8] * 128.0 + ids[8:])
        after = pltpu.roll(code, 7, 0)
        for e in range(8):
            shift = (64 * (n & 1) - 16 * e) % 128
            limit = 128 + 64 * (n & 1) - 16 * e
            a = pltpu.roll(code, shift, 1) if shift else code
            b = pltpu.roll(after, shift, 1) if shift else after
            rows = jnp.where(lane < limit, a, b)
            for r in range(8):
                table_ref[n, 8 * r + e] = jnp.broadcast_to(rows[r : r + 1, :], (8, 128))
    core = core_ref[0]
    bins = iota((256, 128), 0)
    bins = (bins & 127) + jnp.where(bins < 128, core, 1 - core) * 128
    bins = bins.astype(F32).astype(BF)
    low = lane < 64
    one, zero = jnp.ones((256, 128), BF), jnp.zeros((256, 128), BF)

    def hot(pair, first, second):
        code = jnp.where(low, first, second) - (pair * 256).astype(F32)
        code = jnp.where((code >= 0.0) & (code < 256.0), code, 300.0)
        code = jnp.concatenate([code, code], axis=0).astype(BF)
        code = jnp.broadcast_to(code[None], (16, 16, 128)).reshape(256, 128)
        return jnp.where(code == bins, one, zero)

    def window(pair, w):
        codes, rows = [], []
        for n in range(4):
            q = info_ref[n, pair]
            if w is None:
                code = table_ref[n, q]
            else:
                q0 = q + 4 * w
                q = jnp.minimum(q0, QMAX)
                code = jnp.where((lane & 63) >= (q0 - q) * 16, table_ref[n, q], -1.0)
            codes.append(code)
            rows.append(lists[n][pl.ds(pl.multiple_of(q * 16, 16), 64), :])
        left, right = hot(pair, *codes[:2]), hot(pair, *codes[2:])
        return mm(jnp.concatenate([left, right], axis=1), jnp.concatenate(rows, axis=0))

    def store(pair, total):
        if last:
            total = total + refs[0][pair]
            refs[1][pair] = total[:128].astype(BF)
            refs[2][pair] = total[128:].astype(BF)
        else:
            refs[0][pair] = total

    def windows(pair):
        counts = [info_ref[n, 32 + pair] for n in range(4)]
        return jnp.maximum(jnp.maximum(counts[0], counts[1]), jnp.maximum(counts[2], counts[3]))

    def body(pair, long):
        store(pair, window(pair, None))
        long_ref[long] = pair
        return long + jnp.where(windows(pair) > 1, 1, 0)

    long = lax.fori_loop(0, SHOTS // 2, body, jnp.int32(0), unroll=16)

    def rest(i, carry):
        pair = long_ref[i]
        total = lax.fori_loop(1, windows(pair), lambda w, t: t + window(pair, w), window(pair, None))
        store(pair, total)
        return carry

    lax.fori_loop(0, long, rest, 0)


def stacked(core, lists, sums=None):
    info = jnp.stack([v[VALID + 7, 64:] for v in lists]).astype(I32)
    if sums is None:
        out_shape, extra = jax.ShapeDtypeStruct((SHOTS // 2, 256, 128), F32), []
    else:
        out_shape, extra = (jax.ShapeDtypeStruct((SHOTS // 2, BIN, 128), BF),) * 2, [sums]
    return pl.pallas_call(
        lambda *refs: stack_kernel(sums is not None, *refs),
        out_shape=out_shape,
        in_specs=[SMEM, SMEM] + [VMEM] * (4 + len(extra)),
        out_specs=VMEM if sums is None else (VMEM, VMEM),
        scratch_shapes=[pltpu.VMEM((4, 64, 8, 128), F32), pltpu.SMEM((SHOTS // 2,), I32)],
        compiler_params=params(),
        name="stack0" if sums is None else "stack1",
    )(core, info, *lists, *extra)


def fold_kernel(x_ref, mine_ref, other_ref, *outs):
    for d in range(4):
        at = pl.ds(8 * ((x_ref[0] + d) & 3), 8)
        outs[d][...] = (mine_ref[at].astype(F32) + other_ref[at].astype(F32)).astype(BF)


def folded(x_pos, mine, other):
    return pl.pallas_call(
        fold_kernel,
        out_shape=[jax.ShapeDtypeStruct((8, BIN, 128), BF)] * 4,
        in_specs=[SMEM, VMEM, VMEM],
        out_specs=[VMEM] * 4,
        compiler_params=params(),
        name="fold",
    )(x_pos, mine, other)


def around(parts, axis):
    n = len(parts)
    return [parts[0]] + [lax.ppermute(parts[d], axis, [(i, (i + d) % n) for i in range(n)]) for d in range(1, n)]


def per_device(gathers, trace_slot, gain, midbin, bin_row, taps_shot, taps_time):
    x_pos, y_pos, core = (lax.axis_index(a).reshape(1) for a in ("x", "y", "c"))
    x = gathers.reshape(BLK, NT)
    table = bin_row.reshape(64, 128)
    time_band, shot_band = bands(taps_time, taps_shot)
    got = []
    for c in range(CHUNKS):
        send = pick(c, x, trace_slot, gain, midbin, table).reshape(SHOTS, ROWS, NT)
        part = lax.all_to_all(send, ("x", "z", "c"), split_axis=0, concat_axis=0, tiled=True)
        got.append(part.reshape(CROWS, NT))
    lists = around(filtered(y_pos, got[0], time_band, shot_band, "filter0"), "y")
    lists, got[1] = lax.optimization_barrier((lists, got[1]))
    sums = stacked(core, lists)
    lists = around(filtered(y_pos, got[1], time_band, shot_band, "filter1"), "y")
    mine, other = stacked(core, lists, sums)
    other = lax.ppermute(other, "c", [(0, 1), (1, 0)])
    parts = around(folded(x_pos, mine, other), "x")
    total = sum(p.astype(F32) for p in parts).astype(BF)
    parts = lax.all_to_all(total, "z", split_axis=0, concat_axis=0, tiled=True)
    scale = (8192 / 491520) ** 0.5
    return jnp.sum(parts.astype(F32), axis=0) * scale


def solution(mesh):
    finer = Mesh(mesh.devices.reshape(4, 8, 2, mesh.shape["cmp"]), ("x", "z", "c", "y"))
    shot = ("x", "z", "c")
    in_specs = (P(shot, "y", None), P(shot, "y"), P(shot, "y"), P(shot, "y"), P(), P(), P())
    return jax.shard_map(
        per_device, mesh=finer, in_specs=in_specs, out_specs=P(shot, "y"), check_vma=False
    )
```

```python
import jax
import jax.numpy as jnp
from jax import lax
from jax.experimental import pallas as pl
from jax.experimental.pallas import tpu as pltpu
from jax.sharding import Mesh
from jax.sharding import PartitionSpec as P


BF = jnp.bfloat16
F32 = jnp.float32
I32 = jnp.int32
SHOTS, RPD, PER = 64, 30, 15
ROWS = 16
CROWS = SHOTS * ROWS
VALID = SHOTS * PER
NT, BLK, BIN = 512, 1920, 128
YROWS = VALID + 16
QMAX = (YROWS - 64) // 16
WIDE = 640
PICK_MIB = (60, 24)
VMEM = pl.BlockSpec(memory_space=pltpu.VMEM)
SMEM = pl.BlockSpec(memory_space=pltpu.SMEM)


def params(mib=24):
    return pltpu.CompilerParams(vmem_limit_bytes=mib * 1024 * 1024)


def iota(shape, dim):
    return lax.broadcasted_iota(I32, shape, dim)


def mask_bf(mask):
    return jnp.where(mask, 1.0, 0.0).astype(BF)


def mm(a, b):
    return jnp.dot(a, b, preferred_element_type=F32)


def mm_nt(a, b):
    return lax.dot_general(a, b, (((1,), (1,)), ((), ())), preferred_element_type=F32)


def column(ref, base, wanted):
    row = ref[:, base : base + WIDE].astype(F32)
    return jnp.sum(jnp.where(wanted, row, 0.0), axis=1, keepdims=True)


def pick_kernel(chunk, x_hbm, slot_hbm, gain_hbm, mid_hbm, tab_hbm, *refs):
    if chunk:
        at_ref, refs = refs[0], refs[1:]
        outs, refs = refs[:2], refs[2:]
    else:
        outs, refs = refs[:1], refs[1:]
    x_ref, slot_ref, gain_ref, mid_ref, tab_ref, block_ref, in_sems, out_sems = refs
    sources = (slot_hbm, gain_hbm, mid_hbm, tab_hbm, x_hbm)
    targets = (slot_ref, gain_ref, mid_ref, tab_ref, x_ref)
    copies = [pltpu.make_async_copy(sources[i], targets[i], in_sems.at[i]) for i in range(5)]
    for copy in copies:
        copy.start()
    for copy in copies[:4]:
        copy.wait()
    table = tab_ref[...]
    owners = lax.shift_right_logical(table, 7).astype(F32).astype(BF)
    locals_ = (table & 127).astype(F32).astype(BF)
    here, there = iota((256, 256), 0), iota((256, 256), 1)
    gather = mask_bf((lax.shift_right_logical(here, 4) == lax.shift_right_logical(there, 4)) & ((here & 15) == 15))
    place = iota((256, 1), 0) & 15
    real = place < PER
    lane = iota((256, NT), 1)

    def columns(b):
        base = min((480 * b) // 128 * 128, BLK - WIDE)
        receiver = (lax.shift_right_logical(iota((256, 1), 0), 4) + 16 * b) * RPD + chunk * PER + place
        wanted = (iota((256, WIDE), 1) + base == receiver) & real
        slot = column(slot_ref, base, wanted).astype(I32)
        block = (slot >= BLK).astype(I32) + (slot >= 2 * BLK).astype(I32) + (slot >= 3 * BLK).astype(I32)
        slot = jnp.where(real, slot - BLK * block, -1)
        gain = column(gain_ref, base, wanted)
        mid = column(mid_ref, base, wanted).astype(I32)
        pick_row = mask_bf(iota((256, 64), 1) == lax.shift_right_logical(mid, 7))
        pick_lane = iota((256, 128), 1) == (mid & 127)
        owner = jnp.sum(jnp.where(pick_lane, mm(pick_row, owners), 0.0), axis=1, keepdims=True)
        local = jnp.sum(jnp.where(pick_lane, mm(pick_row, locals_), 0.0), axis=1, keepdims=True)
        spread = jnp.where(lane < NT // 2, owner, local)
        spread = jnp.where(((lane & 15) == place) & real, spread, 0.0).astype(BF)
        return slot, gain, spread

    written = []
    for b in range(CROWS // 256):
        slot, gain, spread = columns(b)
        one_hot = mask_bf(iota((256, BLK), 1) == slot)
        if b == 0:
            copies[4].wait()
        out = mm(one_hot, x_ref[...]) * gain + mm(gather, spread)
        block_ref[b] = out.astype(BF)
        if chunk == 0:
            copy = pltpu.make_async_copy(block_ref.at[b], outs[0].at[256 * b : 256 * b + 256], out_sems.at[b])
            copy.start()
            written.append(copy)
        else:
            x_pos, z_pos, core = at_ref[0], at_ref[1], at_ref[2]
            for side in range(2):
                for z in range(8):
                    row = pl.multiple_of((2 * z + (core ^ side)) * 16, 16)
                    piece = block_ref[b, pl.ds(row, 16), :]
                    outs[side][(b - x_pos) & 3, (z - z_pos) & 7] = piece
    for copy in written:
        copy.wait()


def pick(chunk, x, slot, gain, mid, table, at=None):
    any_space = pl.BlockSpec(memory_space=pl.ANY)
    if chunk == 0:
        out_shape, out_specs = jax.ShapeDtypeStruct((CROWS, NT), BF), any_space
    else:
        out_shape, out_specs = [jax.ShapeDtypeStruct((4, 8, ROWS, NT), BF)] * 2, [VMEM] * 2
    return pl.pallas_call(
        lambda *refs: pick_kernel(chunk, *refs),
        out_shape=out_shape,
        in_specs=[any_space] * 5 + [SMEM] * chunk,
        out_specs=out_specs,
        scratch_shapes=[
            pltpu.VMEM((BLK, NT), BF),
            pltpu.VMEM((1, BLK), I32),
            pltpu.VMEM((1, BLK), F32),
            pltpu.VMEM((1, BLK), I32),
            pltpu.VMEM((64, 128), I32),
            pltpu.VMEM((4, 256, NT), BF),
            pltpu.SemaphoreType.DMA((5,)),
            pltpu.SemaphoreType.DMA((4,)),
        ],
        compiler_params=params(PICK_MIB[chunk]),
    )(x, slot, gain, mid, table, *([at] * chunk))


def band_kernel(time_ref, shot_ref, time_out, shot_out):
    step, col = iota((256, 128), 0), iota((256, 128), 1)
    wrapped = (step < 128) == (col < 32)
    for k in range(3):
        base = jnp.broadcast_to(time_ref[k : k + 1, :], (128, 256))
        rolled = pltpu.roll(base, 0, 1, stride=1, stride_axis=0)
        band = rolled.T
        at = slice(128 * k, 128 * k + 128)
        time_out[0, :, at] = band.astype(BF)
        time_out[1, :, at] = jnp.where(wrapped, band, 0.0).astype(BF)
        base = jnp.broadcast_to(shot_ref[k : k + 1, :], (256, 640))
        rolled = pltpu.roll(base, 0, 1, stride=1, stride_axis=0)
        shot_out[0, :, 384 * k : 384 * k + 384] = rolled[:, 128:512].astype(BF)
        shot_out[1, :, 384 * k : 384 * k + 384] = rolled[:, :384].astype(BF)


def band_rows(taps_time, taps_shot):
    time_row = jnp.pad(taps_time.astype(BF).astype(F32), ((0, 0), (64, 128)))
    shot = taps_shot.astype(BF).astype(F32)
    shot_row = lax.pad(shot, jnp.float32(0), ((0, 0, 0), (8, 640 - 8 - 241, 7)))
    return time_row, shot_row


def filter_kernel(count, at_ref, time_row, shot_row, *refs):
    parts, outs = refs[:count], refs[count : count + 4]
    time_ref, shot_ref, mid_ref, trace_ref, *rest = refs[count + 4 :]
    if count == 1:
        x_ref = parts[0]
    else:
        x_ref = rest[0]
        for dz in range(8):
            for dx in range(4):
                for dc in range(2):
                    shot = ((at_ref[0] - dx) & 3) * 16 + ((at_ref[1] - dz) & 7) * 2 + (at_ref[2] ^ dc)
                    place = (dx * 2 + dc) * ROWS
                    to = pl.ds(pl.multiple_of(shot * ROWS, ROWS), ROWS)
                    x_ref[to, :] = parts[dz][place : place + ROWS, :]
    band_kernel(time_row, shot_row, time_ref, shot_ref)
    row = iota((256, NT), 0)
    lane = iota((256, NT), 1)
    keep = ((row & 15) == 15) & (lax.shift_right_logical(row, 4) == lax.shift_right_logical(lane & 255, 4))
    bad = (iota((1, 256), 1) & 15) == 15
    upper = mask_bf(iota((256, 256), 0) < iota((256, 256), 1))
    owner, local, marks, ranks = [], [], [], []
    before = jnp.zeros((128, 1), F32)
    for b in range(4):
        rows = slice(256 * b, 256 * b + 256)
        part = jnp.where(keep, x_ref[rows, :].astype(F32), 0.0)
        ids = jnp.sum(part, axis=0, keepdims=True)
        owner.append(jnp.where(bad, 127.0, ids[:, :256]))
        local.append(ids[:, 256:])
        for j in range(4):
            if j:
                lhs, band = x_ref[rows, 128 * j - 128 : 128 * j + 128], time_ref[0]
            else:
                lhs = jnp.concatenate([x_ref[rows, 384:], x_ref[rows, :128]], axis=1)
                band = time_ref[1]
            mids = mm(lhs, band).reshape(16, 2, 8, 384)
            for half in range(2):
                part = mids[:, half].reshape(128, 384).astype(BF)
                for k in range(3):
                    value = part[:, 128 * k : 128 * k + 128]
                    for w in range(2):
                        at = 128 * b - 128 * w
                        if 0 <= at < 384:
                            at += 384 * k
                            mid_ref[half, w, at : at + 128, 128 * j : 128 * j + 128] = value
            if j == 1:
                mark = jnp.where(iota((128, 256), 0).astype(F32) == owner[b], 1.0, 0.0)
                ranks.append(mm(mark.astype(BF), upper) + before)
                marks.append(mark)
                before = before + jnp.sum(mark, axis=1, keepdims=True)
    lower = mask_bf(iota((128, 128), 1) < iota((128, 128), 0))
    starts = mm(lower, jnp.broadcast_to(before, (128, 128)).astype(BF))[:, :1]
    y_pos = at_ref[3]
    places = []
    for w in range(2):
        both = []
        for half in range(2):
            filt = mm(shot_ref[w], mid_ref[half, w])
            power = jnp.mean(filt * filt, axis=1, keepdims=True) + 1e-6
            done = pltpu.roll(filt * lax.rsqrt(power), NT - 32, 1)
            both.append(done.reshape(32, 1, 8, NT))
            b = 2 * w + half
            places.append(jnp.sum(marks[b] * (ranks[b] + starts), axis=0, keepdims=True))
        trace = jnp.concatenate(both, axis=1).reshape(512, NT).astype(BF)
        for y in range(4):
            trace_ref[(y - y_pos) & 3, 512 * w : 512 * w + 512, :] = trace[:, 128 * y : 128 * y + 128]
    place = jnp.concatenate(places, axis=1).astype(I32)
    owner = jnp.concatenate(owner, axis=1)
    local = jnp.concatenate(local, axis=1)
    place_lane = mask_bf(iota((128, CROWS), 0) == (place & 127))
    here = iota((8, CROWS), 0) == lax.shift_right_logical(place, 7)
    ids = jnp.concatenate([jnp.where(here, owner, 0.0), jnp.where(here, local, 0.0)], axis=0)
    ids = mm_nt(ids.astype(BF), place_lane)
    first = jnp.broadcast_to(starts, (128, 128)).T[:16]
    first = lax.shift_right_logical(first.astype(I32), 4)
    count = lax.shift_right_logical(pltpu.roll(first, 126, 1) - first + 4, 2)
    count = jnp.maximum(count, 1).astype(F32).astype(BF)
    first = jnp.minimum(first, QMAX).astype(F32).astype(BF)
    here, there = iota((128, 128), 0), iota((128, 128), 1)
    even = 2 * (there & 31)
    pick_first = mask_bf((here == even) & (there >= 64) & (there < 96))
    pick_count = mask_bf((here == even) & (there >= 96))
    first = mm(first, pick_first) + mm(count, pick_count)
    r, c = iota((16, 128), 0), iota((16, 128), 1)
    ids = jnp.where((r == 7) & (c >= 64), first, ids).astype(BF)
    traces = jnp.concatenate([trace_ref[d] for d in range(4)], axis=1)
    for b in range(2):
        size = min(512, VALID - 512 * b)
        order = mask_bf(iota((size, CROWS), 0) + 512 * b == place)
        rows = mm(order, traces).astype(BF)
        for d in range(4):
            outs[d][512 * b : 512 * b + size, :] = rows[:, 128 * d : 128 * d + 128]
    for d in range(4):
        outs[d][VALID:, :] = ids


def filtered(at, rows, parts):
    scratch = [
        pltpu.VMEM((2, 256, 384), BF),
        pltpu.VMEM((2, 256, 1152), BF),
        pltpu.VMEM((2, 2, 1152, NT), BF),
        pltpu.VMEM((4, CROWS, 128), BF),
    ]
    if len(parts) > 1:
        scratch.append(pltpu.VMEM((CROWS, NT), BF))
    return pl.pallas_call(
        lambda *refs: filter_kernel(len(parts), *refs),
        out_shape=[jax.ShapeDtypeStruct((YROWS, 128), BF)] * 4,
        in_specs=[SMEM] + [VMEM] * (2 + len(parts)),
        out_specs=[VMEM] * 4,
        scratch_shapes=scratch,
        compiler_params=params(),
    )(at, *rows, *parts)


def regroup_kernel(*refs):
    for dz in range(8):
        for dx in range(4):
            for dc in range(2):
                place = (dx * 2 + dc) * ROWS
                refs[4 + dz][place : place + ROWS, :] = refs[dx][dc, dz]


def regrouped(parts):
    return pl.pallas_call(
        regroup_kernel,
        out_shape=[jax.ShapeDtypeStruct((8 * ROWS, NT), BF)] * 8,
        in_specs=[VMEM] * 4,
        out_specs=[VMEM] * 8,
        compiler_params=params(8),
        name="regroup",
    )(*parts)


def stack_kernel(last, core_ref, info_ref, l0, l1, l2, l3, *refs):
    lists = (l0, l1, l2, l3)
    table_ref, long_ref = refs[-2:]
    lane = iota((8, 128), 1)
    sub = iota((8, 128), 0)
    for n, ref in enumerate(lists):
        ids = ref[VALID:, :].astype(F32)
        code = jnp.where((sub == 7) & (lane >= 64), -1.0, ids[:8] * 128.0 + ids[8:])
        after = pltpu.roll(code, 7, 0)
        for e in range(8):
            shift = (64 * (n & 1) - 16 * e) % 128
            limit = 128 + 64 * (n & 1) - 16 * e
            a = pltpu.roll(code, shift, 1) if shift else code
            b = pltpu.roll(after, shift, 1) if shift else after
            rows = jnp.where(lane < limit, a, b)
            for r in range(8):
                table_ref[n, 8 * r + e] = jnp.broadcast_to(rows[r : r + 1, :], (8, 128))
    core = core_ref[0]
    bins = iota((256, 128), 0)
    bins = (bins & 127) + jnp.where(bins < 128, core, 1 - core) * 128
    bins = bins.astype(F32).astype(BF)
    low = lane < 64
    one, zero = jnp.ones((256, 128), BF), jnp.zeros((256, 128), BF)

    def hot(pair, first, second):
        code = jnp.where(low, first, second) - (pair * 256).astype(F32)
        code = jnp.where((code >= 0.0) & (code < 256.0), code, 300.0)
        code = jnp.concatenate([code, code], axis=0).astype(BF)
        code = jnp.broadcast_to(code[None], (16, 16, 128)).reshape(256, 128)
        return jnp.where(code == bins, one, zero)

    def window(pair, w):
        codes, rows = [], []
        for n in range(4):
            q = info_ref[n, pair]
            if w is None:
                code = table_ref[n, q]
            else:
                q0 = q + 4 * w
                q = jnp.minimum(q0, QMAX)
                code = jnp.where((lane & 63) >= (q0 - q) * 16, table_ref[n, q], -1.0)
            codes.append(code)
            rows.append(lists[n][pl.ds(pl.multiple_of(q * 16, 16), 64), :])
        left, right = hot(pair, *codes[:2]), hot(pair, *codes[2:])
        return mm(jnp.concatenate([left, right], axis=1), jnp.concatenate(rows, axis=0))

    def store(pair, total):
        if last:
            total = total + refs[0][pair]
            refs[1][pair] = total[:128].astype(BF)
            refs[2][pair] = total[128:].astype(BF)
        else:
            refs[0][pair] = total

    def windows(pair):
        counts = [info_ref[n, 32 + pair] for n in range(4)]
        return jnp.maximum(jnp.maximum(counts[0], counts[1]), jnp.maximum(counts[2], counts[3]))

    def body(pair, long):
        store(pair, window(pair, None))
        long_ref[long] = pair
        return long + jnp.where(windows(pair) > 1, 1, 0)

    long = lax.fori_loop(0, SHOTS // 2, body, jnp.int32(0), unroll=16)

    def rest(i, carry):
        pair = long_ref[i]
        total = lax.fori_loop(1, windows(pair), lambda w, t: t + window(pair, w), window(pair, None))
        store(pair, total)
        return carry

    lax.fori_loop(0, long, rest, 0)


def stacked(core, lists, sums=None):
    info = jnp.stack([v[VALID + 7, 64:] for v in lists]).astype(I32)
    if sums is None:
        out_shape, extra = jax.ShapeDtypeStruct((SHOTS // 2, 256, 128), F32), []
    else:
        out_shape, extra = (jax.ShapeDtypeStruct((SHOTS // 2, BIN, 128), BF),) * 2, [sums]
    return pl.pallas_call(
        lambda *refs: stack_kernel(sums is not None, *refs),
        out_shape=out_shape,
        in_specs=[SMEM, SMEM] + [VMEM] * (4 + len(extra)),
        out_specs=VMEM if sums is None else (VMEM, VMEM),
        scratch_shapes=[pltpu.VMEM((4, 64, 8, 128), F32), pltpu.SMEM((SHOTS // 2,), I32)],
        compiler_params=params(),
        name="stack0" if sums is None else "stack1",
    )(core, info, *lists, *extra)


def fold_kernel(x_ref, mine_ref, other_ref, *outs):
    for d in range(4):
        at = pl.ds(8 * ((x_ref[0] + d) & 3), 8)
        outs[d][...] = (mine_ref[at].astype(F32) + other_ref[at].astype(F32)).astype(BF)


def folded(x_pos, mine, other):
    return pl.pallas_call(
        fold_kernel,
        out_shape=[jax.ShapeDtypeStruct((8, BIN, 128), BF)] * 4,
        in_specs=[SMEM, VMEM, VMEM],
        out_specs=[VMEM] * 4,
        compiler_params=params(),
        name="fold",
    )(x_pos, mine, other)


def around(parts, axis):
    n = len(parts)
    out = [parts[0]]
    for d in range(1, n):
        out.append(lax.ppermute(parts[d], axis, [(i, (i + d) % n) for i in range(n)]))
    return out


def swapped(part):
    return lax.ppermute(part, "c", [(0, 1), (1, 0)])


def steps(gathers, trace_slot, gain, midbin, bin_row, taps_shot, taps_time):
    at = jnp.stack([lax.axis_index(a) for a in ("x", "z", "c", "y")])
    x_pos, core = lax.axis_index("x").reshape(1), lax.axis_index("c").reshape(1)
    x = gathers.reshape(BLK, NT)
    table = bin_row.reshape(64, 128)
    rows = band_rows(taps_time, taps_shot)
    send = pick(0, x, trace_slot, gain, midbin, table).reshape(SHOTS, ROWS, NT)
    got = lax.all_to_all(send, ("x", "z", "c"), split_axis=0, concat_axis=0, tiled=True)
    own, other = pick(1, x, trace_slot, gain, midbin, table, at)
    other = swapped(other)
    joined = around([jnp.stack([own[d], other[d]]) for d in range(4)], "x")
    parts = around(regrouped(joined), "z")
    lists = around(filtered(at, rows, [got.reshape(CROWS, NT)]), "y")
    later = around(filtered(at, rows, parts), "y")
    mine, other = stacked(core, later, stacked(core, lists))
    other = swapped(other)
    parts = around(folded(x_pos, mine, other), "x")
    total = sum(p.astype(F32) for p in parts).astype(BF)
    parts = lax.all_to_all(total, "z", split_axis=0, concat_axis=0, tiled=True)
    scale = (8192 / 491520) ** 0.5
    return jnp.sum(parts.astype(F32), axis=0) * scale


def solution(mesh):
    finer = Mesh(mesh.devices.reshape(4, 8, 2, mesh.shape["cmp"]), ("x", "z", "c", "y"))
    shot = ("x", "z", "c")
    in_specs = (P(shot, "y", None), P(shot, "y"), P(shot, "y"), P(shot, "y"), P(), P(), P())
    return jax.shard_map(
        steps, mesh=finer, in_specs=in_specs, out_specs=P(shot, "y"), check_vma=False
    )
```

```python
import jax
import jax.numpy as jnp
from jax import lax
from jax.experimental import pallas as pl
from jax.experimental.pallas import tpu as pltpu
from jax.sharding import Mesh
from jax.sharding import PartitionSpec as P


BF = jnp.bfloat16
F32 = jnp.float32
I32 = jnp.int32
SHOTS, RPD, PER = 64, 30, 15
ROWS = 16
CROWS = SHOTS * ROWS
VALID = SHOTS * PER
NT, BLK, BIN = 512, 1920, 128
YROWS = VALID + 16
QMAX = (YROWS - 64) // 16
WIDE = 640
PICK_MIB = (24, 60)
VMEM = pl.BlockSpec(memory_space=pltpu.VMEM)
SMEM = pl.BlockSpec(memory_space=pltpu.SMEM)


def params(mib=24):
    return pltpu.CompilerParams(vmem_limit_bytes=mib * 1024 * 1024)


def iota(shape, dim):
    return lax.broadcasted_iota(I32, shape, dim)


def mask_bf(mask):
    return jnp.where(mask, 1.0, 0.0).astype(BF)


def mm(a, b):
    return jnp.dot(a, b, preferred_element_type=F32)


def mm_nt(a, b):
    return lax.dot_general(a, b, (((1,), (1,)), ((), ())), preferred_element_type=F32)


def column(ref, base, wanted):
    row = ref[:, base : base + WIDE].astype(F32)
    return jnp.sum(jnp.where(wanted, row, 0.0), axis=1, keepdims=True)


def pick_kernel(chunk, x_hbm, slot_hbm, gain_hbm, mid_hbm, tab_hbm, *refs):
    if chunk:
        at_ref, refs = refs[0], refs[1:]
        outs, refs = refs[:2], refs[2:]
    else:
        outs, refs = refs[:1], refs[1:]
    x_ref, slot_ref, gain_ref, mid_ref, tab_ref, block_ref, in_sems, out_sems = refs
    sources = (slot_hbm, gain_hbm, mid_hbm, tab_hbm, x_hbm)
    targets = (slot_ref, gain_ref, mid_ref, tab_ref, x_ref)
    copies = [pltpu.make_async_copy(sources[i], targets[i], in_sems.at[i]) for i in range(5)]
    for copy in copies:
        copy.start()
    for copy in copies[:4]:
        copy.wait()
    table = tab_ref[...]
    owners = lax.shift_right_logical(table, 7).astype(F32).astype(BF)
    locals_ = (table & 127).astype(F32).astype(BF)
    here, there = iota((256, 256), 0), iota((256, 256), 1)
    gather = mask_bf((lax.shift_right_logical(here, 4) == lax.shift_right_logical(there, 4)) & ((here & 15) == 15))
    place = iota((256, 1), 0) & 15
    real = place < PER
    lane = iota((256, NT), 1)

    def columns(b):
        base = min((480 * b) // 128 * 128, BLK - WIDE)
        receiver = (lax.shift_right_logical(iota((256, 1), 0), 4) + 16 * b) * RPD + chunk * PER + place
        wanted = (iota((256, WIDE), 1) + base == receiver) & real
        slot = column(slot_ref, base, wanted).astype(I32)
        block = (slot >= BLK).astype(I32) + (slot >= 2 * BLK).astype(I32) + (slot >= 3 * BLK).astype(I32)
        slot = jnp.where(real, slot - BLK * block, -1)
        gain = column(gain_ref, base, wanted)
        mid = column(mid_ref, base, wanted).astype(I32)
        pick_row = mask_bf(iota((256, 64), 1) == lax.shift_right_logical(mid, 7))
        pick_lane = iota((256, 128), 1) == (mid & 127)
        owner = jnp.sum(jnp.where(pick_lane, mm(pick_row, owners), 0.0), axis=1, keepdims=True)
        local = jnp.sum(jnp.where(pick_lane, mm(pick_row, locals_), 0.0), axis=1, keepdims=True)
        spread = jnp.where(lane < NT // 2, owner, local)
        spread = jnp.where(((lane & 15) == place) & real, spread, 0.0).astype(BF)
        return slot, gain, spread

    written = []
    for b in range(CROWS // 256):
        slot, gain, spread = columns(b)
        one_hot = mask_bf(iota((256, BLK), 1) == slot)
        if b == 0:
            copies[4].wait()
        out = mm(one_hot, x_ref[...]) * gain + mm(gather, spread)
        block_ref[b] = out.astype(BF)
        if chunk == 0:
            copy = pltpu.make_async_copy(block_ref.at[b], outs[0].at[256 * b : 256 * b + 256], out_sems.at[b])
            copy.start()
            written.append(copy)
        else:
            x_pos, z_pos, core = at_ref[0], at_ref[1], at_ref[2]
            for side in range(2):
                for z in range(8):
                    row = pl.multiple_of((2 * z + (core ^ side)) * 16, 16)
                    piece = block_ref[b, pl.ds(row, 16), :]
                    outs[side][(z - z_pos) & 7, (b - x_pos) & 3] = piece
    for copy in written:
        copy.wait()


def pick(chunk, x, slot, gain, mid, table, at=None):
    any_space = pl.BlockSpec(memory_space=pl.ANY)
    hbm = pl.BlockSpec(memory_space=pltpu.HBM)
    if chunk == 0:
        out_shape, out_specs = jax.ShapeDtypeStruct((CROWS, NT), BF), any_space
    else:
        out_shape, out_specs = [jax.ShapeDtypeStruct((8, 4, ROWS, NT), BF)] * 2, [VMEM] * 2
    return pl.pallas_call(
        lambda *refs: pick_kernel(chunk, *refs),
        out_shape=out_shape,
        in_specs=[hbm] * 5 + [SMEM] * chunk,
        out_specs=out_specs,
        scratch_shapes=[
            pltpu.VMEM((BLK, NT), BF),
            pltpu.VMEM((1, BLK), I32),
            pltpu.VMEM((1, BLK), F32),
            pltpu.VMEM((1, BLK), I32),
            pltpu.VMEM((64, 128), I32),
            pltpu.VMEM((4, 256, NT), BF),
            pltpu.SemaphoreType.DMA((5,)),
            pltpu.SemaphoreType.DMA((4,)),
        ],
        compiler_params=params(PICK_MIB[chunk]),
    )(x, slot, gain, mid, table, *([at] * chunk))


def band_kernel(time_ref, shot_ref, time_out, shot_out):
    step, col = iota((256, 128), 0), iota((256, 128), 1)
    wrapped = (step < 128) == (col < 32)
    for k in range(3):
        base = jnp.broadcast_to(time_ref[k : k + 1, :], (128, 256))
        rolled = pltpu.roll(base, 0, 1, stride=1, stride_axis=0)
        band = rolled.T
        at = slice(128 * k, 128 * k + 128)
        time_out[0, :, at] = band.astype(BF)
        time_out[1, :, at] = jnp.where(wrapped, band, 0.0).astype(BF)
        base = jnp.broadcast_to(shot_ref[k : k + 1, :], (256, 640))
        rolled = pltpu.roll(base, 0, 1, stride=1, stride_axis=0)
        shot_out[0, :, 384 * k : 384 * k + 384] = rolled[:, 128:512].astype(BF)
        shot_out[1, :, 384 * k : 384 * k + 384] = rolled[:, :384].astype(BF)


def band_rows(taps_time, taps_shot):
    time_row = jnp.pad(taps_time.astype(BF).astype(F32), ((0, 0), (64, 128)))
    shot = taps_shot.astype(BF).astype(F32)
    shot_row = lax.pad(shot, jnp.float32(0), ((0, 0, 0), (8, 640 - 8 - 241, 7)))
    return time_row, shot_row


def filter_kernel(count, at_ref, time_row, shot_row, *refs):
    parts, outs = refs[:count], refs[count : count + 4]
    time_ref, shot_ref, mid_ref, trace_ref, *rest = refs[count + 4 :]
    if count == 1:
        x_ref = parts[0]
    else:
        x_ref = rest[0]
        for dx in range(4):
            for dz in range(8):
                for dc in range(2):
                    shot = ((at_ref[0] - dx) & 3) * 16 + ((at_ref[1] - dz) & 7) * 2 + (at_ref[2] ^ dc)
                    place = (dz * 2 + dc) * ROWS
                    to = pl.ds(pl.multiple_of(shot * ROWS, ROWS), ROWS)
                    x_ref[to, :] = parts[dx][place : place + ROWS, :]
    band_kernel(time_row, shot_row, time_ref, shot_ref)
    row = iota((256, NT), 0)
    lane = iota((256, NT), 1)
    keep = ((row & 15) == 15) & (lax.shift_right_logical(row, 4) == lax.shift_right_logical(lane & 255, 4))
    bad = (iota((1, 256), 1) & 15) == 15
    upper = mask_bf(iota((256, 256), 0) < iota((256, 256), 1))
    owner, local, marks, ranks = [], [], [], []
    before = jnp.zeros((128, 1), F32)
    for b in range(4):
        rows = slice(256 * b, 256 * b + 256)
        part = jnp.where(keep, x_ref[rows, :].astype(F32), 0.0)
        ids = jnp.sum(part, axis=0, keepdims=True)
        owner.append(jnp.where(bad, 127.0, ids[:, :256]))
        local.append(ids[:, 256:])
        for j in range(4):
            if j:
                lhs, band = x_ref[rows, 128 * j - 128 : 128 * j + 128], time_ref[0]
            else:
                lhs = jnp.concatenate([x_ref[rows, 384:], x_ref[rows, :128]], axis=1)
                band = time_ref[1]
            mids = mm(lhs, band).reshape(16, 2, 8, 384)
            for half in range(2):
                part = mids[:, half].reshape(128, 384).astype(BF)
                for k in range(3):
                    value = part[:, 128 * k : 128 * k + 128]
                    for w in range(2):
                        at = 128 * b - 128 * w
                        if 0 <= at < 384:
                            at += 384 * k
                            mid_ref[half, w, at : at + 128, 128 * j : 128 * j + 128] = value
            if j == 1:
                mark = jnp.where(iota((128, 256), 0).astype(F32) == owner[b], 1.0, 0.0)
                ranks.append(mm(mark.astype(BF), upper) + before)
                marks.append(mark)
                before = before + jnp.sum(mark, axis=1, keepdims=True)
    lower = mask_bf(iota((128, 128), 1) < iota((128, 128), 0))
    starts = mm(lower, jnp.broadcast_to(before, (128, 128)).astype(BF))[:, :1]
    y_pos = at_ref[3]
    places = []
    for w in range(2):
        both = []
        for half in range(2):
            filt = mm(shot_ref[w], mid_ref[half, w])
            power = jnp.mean(filt * filt, axis=1, keepdims=True) + 1e-6
            done = pltpu.roll(filt * lax.rsqrt(power), NT - 32, 1)
            both.append(done.reshape(32, 1, 8, NT))
            b = 2 * w + half
            places.append(jnp.sum(marks[b] * (ranks[b] + starts), axis=0, keepdims=True))
        trace = jnp.concatenate(both, axis=1).reshape(512, NT).astype(BF)
        for y in range(4):
            trace_ref[(y - y_pos) & 3, 512 * w : 512 * w + 512, :] = trace[:, 128 * y : 128 * y + 128]
    place = jnp.concatenate(places, axis=1).astype(I32)
    owner = jnp.concatenate(owner, axis=1)
    local = jnp.concatenate(local, axis=1)
    place_lane = mask_bf(iota((128, CROWS), 0) == (place & 127))
    here = iota((8, CROWS), 0) == lax.shift_right_logical(place, 7)
    ids = jnp.concatenate([jnp.where(here, owner, 0.0), jnp.where(here, local, 0.0)], axis=0)
    ids = mm_nt(ids.astype(BF), place_lane)
    first = jnp.broadcast_to(starts, (128, 128)).T[:16]
    first = lax.shift_right_logical(first.astype(I32), 4)
    count = lax.shift_right_logical(pltpu.roll(first, 126, 1) - first + 4, 2)
    count = jnp.maximum(count, 1).astype(F32).astype(BF)
    first = jnp.minimum(first, QMAX).astype(F32).astype(BF)
    here, there = iota((128, 128), 0), iota((128, 128), 1)
    even = 2 * (there & 31)
    pick_first = mask_bf((here == even) & (there >= 64) & (there < 96))
    pick_count = mask_bf((here == even) & (there >= 96))
    first = mm(first, pick_first) + mm(count, pick_count)
    r, c = iota((16, 128), 0), iota((16, 128), 1)
    ids = jnp.where((r == 7) & (c >= 64), first, ids).astype(BF)
    traces = jnp.concatenate([trace_ref[d] for d in range(4)], axis=1)
    for b in range(2):
        size = min(512, VALID - 512 * b)
        order = mask_bf(iota((size, CROWS), 0) + 512 * b == place)
        rows = mm(order, traces).astype(BF)
        for d in range(4):
            outs[d][512 * b : 512 * b + size, :] = rows[:, 128 * d : 128 * d + 128]
    for d in range(4):
        outs[d][VALID:, :] = ids


def filtered(at, rows, parts):
    scratch = [
        pltpu.VMEM((2, 256, 384), BF),
        pltpu.VMEM((2, 256, 1152), BF),
        pltpu.VMEM((2, 2, 1152, NT), BF),
        pltpu.VMEM((4, CROWS, 128), BF),
    ]
    if len(parts) > 1:
        scratch.append(pltpu.VMEM((CROWS, NT), BF))
    return pl.pallas_call(
        lambda *refs: filter_kernel(len(parts), *refs),
        out_shape=[jax.ShapeDtypeStruct((YROWS, 128), BF)] * 4,
        in_specs=[SMEM] + [VMEM] * (2 + len(parts)),
        out_specs=[VMEM] * 4,
        scratch_shapes=scratch,
        compiler_params=params(),
    )(at, *rows, *parts)


def join_kernel(own_ref, other_ref, *outs):
    for dz in range(8):
        for dc, ref in enumerate((own_ref, other_ref)):
            for dx in range(4):
                place = (dc * 4 + dx) * ROWS
                outs[dz][place : place + ROWS, :] = ref[dz, dx]


def turn_kernel(*refs):
    for dx in range(4):
        for dz in range(8):
            for dc in range(2):
                source = (dc * 4 + dx) * ROWS
                place = (dz * 2 + dc) * ROWS
                refs[8 + dx][place : place + ROWS, :] = refs[dz][source : source + ROWS, :]


def shuffled(kernel, parts, count):
    rows = CROWS // count
    return pl.pallas_call(
        kernel,
        out_shape=[jax.ShapeDtypeStruct((rows, NT), BF)] * count,
        in_specs=[VMEM] * len(parts),
        out_specs=[VMEM] * count,
        compiler_params=params(8),
    )(*parts)


def stack_kernel(last, core_ref, info_ref, l0, l1, l2, l3, *refs):
    lists = (l0, l1, l2, l3)
    table_ref, long_ref = refs[-2:]
    lane = iota((8, 128), 1)
    sub = iota((8, 128), 0)
    for n, ref in enumerate(lists):
        ids = ref[VALID:, :].astype(F32)
        code = jnp.where((sub == 7) & (lane >= 64), -1.0, ids[:8] * 128.0 + ids[8:])
        after = pltpu.roll(code, 7, 0)
        for e in range(8):
            shift = (64 * (n & 1) - 16 * e) % 128
            limit = 128 + 64 * (n & 1) - 16 * e
            a = pltpu.roll(code, shift, 1) if shift else code
            b = pltpu.roll(after, shift, 1) if shift else after
            rows = jnp.where(lane < limit, a, b)
            for r in range(8):
                table_ref[n, 8 * r + e] = jnp.broadcast_to(rows[r : r + 1, :], (8, 128))
    core = core_ref[0]
    bins = iota((256, 128), 0)
    bins = (bins & 127) + jnp.where(bins < 128, core, 1 - core) * 128
    bins = bins.astype(F32).astype(BF)
    low = lane < 64
    one, zero = jnp.ones((256, 128), BF), jnp.zeros((256, 128), BF)

    def hot(pair, first, second):
        code = jnp.where(low, first, second) - (pair * 256).astype(F32)
        code = jnp.where((code >= 0.0) & (code < 256.0), code, 300.0)
        code = jnp.concatenate([code, code], axis=0).astype(BF)
        code = jnp.broadcast_to(code[None], (16, 16, 128)).reshape(256, 128)
        return jnp.where(code == bins, one, zero)

    def window(pair, w):
        codes, rows = [], []
        for n in range(4):
            q = info_ref[n, pair]
            if w is None:
                code = table_ref[n, q]
            else:
                q0 = q + 4 * w
                q = jnp.minimum(q0, QMAX)
                code = jnp.where((lane & 63) >= (q0 - q) * 16, table_ref[n, q], -1.0)
            codes.append(code)
            rows.append(lists[n][pl.ds(pl.multiple_of(q * 16, 16), 64), :])
        left, right = hot(pair, *codes[:2]), hot(pair, *codes[2:])
        return mm(jnp.concatenate([left, right], axis=1), jnp.concatenate(rows, axis=0))

    def store(pair, total):
        if last:
            total = total + refs[0][pair]
            refs[1][pair] = total[:128].astype(BF)
            refs[2][pair] = total[128:].astype(BF)
        else:
            refs[0][pair] = total

    def windows(pair):
        counts = [info_ref[n, 32 + pair] for n in range(4)]
        return jnp.maximum(jnp.maximum(counts[0], counts[1]), jnp.maximum(counts[2], counts[3]))

    def body(pair, long):
        store(pair, window(pair, None))
        long_ref[long] = pair
        return long + jnp.where(windows(pair) > 1, 1, 0)

    long = lax.fori_loop(0, SHOTS // 2, body, jnp.int32(0), unroll=16)

    def rest(i, carry):
        pair = long_ref[i]
        total = lax.fori_loop(1, windows(pair), lambda w, t: t + window(pair, w), window(pair, None))
        store(pair, total)
        return carry

    lax.fori_loop(0, long, rest, 0)


def stacked(core, lists, sums=None):
    info = jnp.stack([v[VALID + 7, 64:] for v in lists]).astype(I32)
    if sums is None:
        out_shape, extra = jax.ShapeDtypeStruct((SHOTS // 2, 256, 128), F32), []
    else:
        out_shape, extra = (jax.ShapeDtypeStruct((SHOTS // 2, BIN, 128), BF),) * 2, [sums]
    return pl.pallas_call(
        lambda *refs: stack_kernel(sums is not None, *refs),
        out_shape=out_shape,
        in_specs=[SMEM, SMEM] + [VMEM] * (4 + len(extra)),
        out_specs=VMEM if sums is None else (VMEM, VMEM),
        scratch_shapes=[pltpu.VMEM((4, 64, 8, 128), F32), pltpu.SMEM((SHOTS // 2,), I32)],
        compiler_params=params(),
        name="stack0" if sums is None else "stack1",
    )(core, info, *lists, *extra)


def fold_kernel(x_ref, mine_ref, other_ref, *outs):
    for d in range(4):
        at = pl.ds(8 * ((x_ref[0] + d) & 3), 8)
        outs[d][...] = (mine_ref[at].astype(F32) + other_ref[at].astype(F32)).astype(BF)


def folded(x_pos, mine, other):
    return pl.pallas_call(
        fold_kernel,
        out_shape=[jax.ShapeDtypeStruct((8, BIN, 128), BF)] * 4,
        in_specs=[SMEM, VMEM, VMEM],
        out_specs=[VMEM] * 4,
        compiler_params=params(),
        name="fold",
    )(x_pos, mine, other)


def around(parts, axis):
    n = len(parts)
    out = [parts[0]]
    for d in range(1, n):
        out.append(lax.ppermute(parts[d], axis, [(i, (i + d) % n) for i in range(n)]))
    return out


def swapped(part):
    return lax.ppermute(part, "c", [(0, 1), (1, 0)])


def steps(gathers, trace_slot, gain, midbin, bin_row, taps_shot, taps_time):
    at = jnp.stack([lax.axis_index(a) for a in ("x", "z", "c", "y")])
    x_pos, core = lax.axis_index("x").reshape(1), lax.axis_index("c").reshape(1)
    x = gathers.reshape(BLK, NT)
    table = bin_row.reshape(64, 128)
    rows = band_rows(taps_time, taps_shot)
    own, other = pick(1, x, trace_slot, gain, midbin, table, at)
    other = swapped(other)
    parts = around(shuffled(join_kernel, [own, other], 8), "z")
    send = pick(0, x, trace_slot, gain, midbin, table).reshape(SHOTS, ROWS, NT)
    got = lax.all_to_all(send, ("x", "z", "c"), split_axis=0, concat_axis=0, tiled=True)
    parts = around(shuffled(turn_kernel, parts, 4), "x")
    lists = around(filtered(at, rows, parts), "y")
    later = around(filtered(at, rows, [got.reshape(CROWS, NT)]), "y")
    mine, other = stacked(core, later, stacked(core, lists))
    other = swapped(other)
    parts = around(folded(x_pos, mine, other), "x")
    total = sum(p.astype(F32) for p in parts).astype(BF)
    parts = lax.all_to_all(total, "z", split_axis=0, concat_axis=0, tiled=True)
    scale = (8192 / 491520) ** 0.5
    return jnp.sum(parts.astype(F32), axis=0) * scale


def solution(mesh):
    finer = Mesh(mesh.devices.reshape(4, 8, 2, mesh.shape["cmp"]), ("x", "z", "c", "y"))
    shot = ("x", "z", "c")
    in_specs = (P(shot, "y", None), P(shot, "y"), P(shot, "y"), P(shot, "y"), P(), P(), P())
    return jax.shard_map(
        steps, mesh=finer, in_specs=in_specs, out_specs=P(shot, "y"), check_vma=False
    )
```

```python
import jax
import jax.numpy as jnp
from jax import lax
from jax.experimental import pallas as pl
from jax.experimental.pallas import tpu as pltpu
from jax.sharding import Mesh
from jax.sharding import PartitionSpec as P


BF = jnp.bfloat16
F32 = jnp.float32
I32 = jnp.int32
SHOTS, RPD, CHUNKS, PER = 64, 30, 2, 15
ROWS = 16
CROWS = SHOTS * ROWS
VALID = SHOTS * PER
NT, BLK, BIN = 512, 1920, 128
YROWS = VALID + 16
QMAX = (YROWS - 64) // 16
WIDE = 640
VMEM = pl.BlockSpec(memory_space=pltpu.VMEM)
SMEM = pl.BlockSpec(memory_space=pltpu.SMEM)


def params(mib=24):
    return pltpu.CompilerParams(vmem_limit_bytes=mib * 1024 * 1024)


def iota(shape, dim):
    return lax.broadcasted_iota(I32, shape, dim)


def mask_bf(mask):
    return jnp.where(mask, 1.0, 0.0).astype(BF)


def mm(a, b):
    return jnp.dot(a, b, preferred_element_type=F32)


def mm_nt(a, b):
    return lax.dot_general(a, b, (((1,), (1,)), ((), ())), preferred_element_type=F32)


def column(ref, base, wanted):
    row = ref[:, base : base + WIDE].astype(F32)
    return jnp.sum(jnp.where(wanted, row, 0.0), axis=1, keepdims=True)


def pick_kernel(x_hbm, slot_hbm, gain_hbm, mid_hbm, tab_hbm, x_at, z_at, c_at, *refs):
    outs, refs = refs[:12], refs[12:]
    x_ref, slot_ref, gain_ref, mid_ref, tab_ref, block_ref, in_sems = refs
    sources = (slot_hbm, gain_hbm, mid_hbm, tab_hbm, x_hbm)
    targets = (slot_ref, gain_ref, mid_ref, tab_ref, x_ref)
    copies = [pltpu.make_async_copy(sources[i], targets[i], in_sems.at[i]) for i in range(5)]
    for copy in copies:
        copy.start()
    for copy in copies[:4]:
        copy.wait()
    x_pos, z_pos, core = x_at[0], z_at[0], c_at[0]
    table = tab_ref[...]
    owners = lax.shift_right_logical(table, 7).astype(F32).astype(BF)
    locals_ = (table & 127).astype(F32).astype(BF)
    here, there = iota((256, 256), 0), iota((256, 256), 1)
    gather = mask_bf((lax.shift_right_logical(here, 4) == lax.shift_right_logical(there, 4)) & ((here & 15) == 15))
    place = iota((256, 1), 0) & 15
    real = place < PER
    lane = iota((256, NT), 1)

    def columns(chunk, b):
        base = min((480 * b) // 128 * 128, BLK - WIDE)
        receiver = (lax.shift_right_logical(iota((256, 1), 0), 4) + 16 * b) * RPD + chunk * PER + place
        wanted = (iota((256, WIDE), 1) + base == receiver) & real
        slot = column(slot_ref, base, wanted).astype(I32)
        block = (slot >= BLK).astype(I32) + (slot >= 2 * BLK).astype(I32) + (slot >= 3 * BLK).astype(I32)
        slot = jnp.where(real, slot - BLK * block, -1)
        gain = column(gain_ref, base, wanted)
        mid = column(mid_ref, base, wanted).astype(I32)
        pick_row = mask_bf(iota((256, 64), 1) == lax.shift_right_logical(mid, 7))
        pick_lane = iota((256, 128), 1) == (mid & 127)
        owner = jnp.sum(jnp.where(pick_lane, mm(pick_row, owners), 0.0), axis=1, keepdims=True)
        local = jnp.sum(jnp.where(pick_lane, mm(pick_row, locals_), 0.0), axis=1, keepdims=True)
        spread = jnp.where(lane < NT // 2, owner, local)
        spread = jnp.where(((lane & 15) == place) & real, spread, 0.0).astype(BF)
        return slot, gain, spread

    for chunk in range(CHUNKS):
        for b in range(CROWS // 256):
            slot, gain, spread = columns(chunk, b)
            one_hot = mask_bf(iota((256, BLK), 1) == slot)
            if chunk == 0 and b == 0:
                copies[4].wait()
            out = mm(one_hot, x_ref[...]) * gain + mm(gather, spread)
            block_ref[chunk, b] = out.astype(BF)
        for dx in range(4):
            for dz in range(8):
                for dc in range(2):
                    row = (2 * ((z_pos + dz) & 7) + (core ^ dc)) * ROWS
                    row = pl.ds(pl.multiple_of(row, ROWS), ROWS)
                    piece = block_ref[chunk, (x_pos + dx) & 3, row, :]
                    if chunk == 0:
                        to = (dc * 4 + dx) * ROWS
                        outs[dz][to : to + ROWS, :] = piece
                    else:
                        to = (dc * 8 + dz) * ROWS
                        outs[8 + dx][to : to + ROWS, :] = piece


def pick(x, slot, gain, mid, table, at):
    hbm = pl.BlockSpec(memory_space=pltpu.HBM)
    return pl.pallas_call(
        pick_kernel,
        out_shape=[jax.ShapeDtypeStruct(shape, BF) for shape in [(128, NT)] * 8 + [(256, NT)] * 4],
        in_specs=[hbm] * 5 + [SMEM] * 3,
        out_specs=[VMEM] * 12,
        scratch_shapes=[
            pltpu.VMEM((BLK, NT), BF),
            pltpu.VMEM((1, BLK), I32),
            pltpu.VMEM((1, BLK), F32),
            pltpu.VMEM((1, BLK), I32),
            pltpu.VMEM((64, 128), I32),
            pltpu.VMEM((CHUNKS, 4, 256, NT), BF),
            pltpu.SemaphoreType.DMA((5,)),
        ],
        compiler_params=params(60),
        name="pick",
    )(x, slot, gain, mid, table, *at[:3])


def band_kernel(time_ref, shot_ref, time_out, shot_out):
    step, col = iota((256, 128), 0), iota((256, 128), 1)
    wrapped = (step < 128) == (col < 32)
    for k in range(3):
        base = jnp.broadcast_to(time_ref[k : k + 1, :], (128, 256))
        rolled = pltpu.roll(base, 0, 1, stride=1, stride_axis=0)
        band = rolled.T
        at = slice(128 * k, 128 * k + 128)
        time_out[0, :, at] = band.astype(BF)
        time_out[1, :, at] = jnp.where(wrapped, band, 0.0).astype(BF)
        base = jnp.broadcast_to(shot_ref[k : k + 1, :], (256, 640))
        rolled = pltpu.roll(base, 0, 1, stride=1, stride_axis=0)
        shot_out[0, :, 384 * k : 384 * k + 384] = rolled[:, 128:512].astype(BF)
        shot_out[1, :, 384 * k : 384 * k + 384] = rolled[:, :384].astype(BF)


def band_rows(taps_time, taps_shot):
    time_row = jnp.pad(taps_time.astype(BF).astype(F32), ((0, 0), (64, 128)))
    shot = taps_shot.astype(BF).astype(F32)
    shot_row = lax.pad(shot, jnp.float32(0), ((0, 0, 0), (8, 640 - 8 - 241, 7)))
    return time_row, shot_row


def filter_kernel(count, x_at, z_at, c_at, y_at, time_row, shot_row, *refs):
    parts, outs = refs[:count], refs[count : count + 4]
    time_ref, shot_ref, mid_ref, trace_ref, *rest = refs[count + 4 :]
    x_ref = rest[0]
    for dx in range(4):
        for z in range(8):
            for dc in range(2):
                if count == 1:
                    block = parts[0][z * 2 + dc, dx * ROWS : (dx + 1) * ROWS, :]
                    from_z, from_c = z, dc
                else:
                    ref, to = (parts[4], dx * 8 + z) if dc else (parts[dx], z)
                    block = ref[to * ROWS : (to + 1) * ROWS, :]
                    from_z, from_c = (z_at[0] - z) & 7, c_at[0] ^ dc
                shot = ((x_at[0] - dx) & 3) * 16 + from_z * 2 + from_c
                x_ref[pl.ds(pl.multiple_of(shot * ROWS, ROWS), ROWS), :] = block
    band_kernel(time_row, shot_row, time_ref, shot_ref)
    row = iota((256, NT), 0)
    lane = iota((256, NT), 1)
    keep = ((row & 15) == 15) & (lax.shift_right_logical(row, 4) == lax.shift_right_logical(lane & 255, 4))
    bad = (iota((1, 256), 1) & 15) == 15
    upper = mask_bf(iota((256, 256), 0) < iota((256, 256), 1))
    owner, local, marks, ranks = [], [], [], []
    before = jnp.zeros((128, 1), F32)
    for b in range(4):
        rows = slice(256 * b, 256 * b + 256)
        part = jnp.where(keep, x_ref[rows, :].astype(F32), 0.0)
        ids = jnp.sum(part, axis=0, keepdims=True)
        owner.append(jnp.where(bad, 127.0, ids[:, :256]))
        local.append(ids[:, 256:])
        for j in range(4):
            if j:
                lhs, band = x_ref[rows, 128 * j - 128 : 128 * j + 128], time_ref[0]
            else:
                lhs = jnp.concatenate([x_ref[rows, 384:], x_ref[rows, :128]], axis=1)
                band = time_ref[1]
            mids = mm(lhs, band).reshape(16, 2, 8, 384)
            for half in range(2):
                part = mids[:, half].reshape(128, 384).astype(BF)
                for k in range(3):
                    value = part[:, 128 * k : 128 * k + 128]
                    for w in range(2):
                        at = 128 * b - 128 * w
                        if 0 <= at < 384:
                            at += 384 * k
                            mid_ref[half, w, at : at + 128, 128 * j : 128 * j + 128] = value
            if j == 1:
                mark = jnp.where(iota((128, 256), 0).astype(F32) == owner[b], 1.0, 0.0)
                ranks.append(mm(mark.astype(BF), upper) + before)
                marks.append(mark)
                before = before + jnp.sum(mark, axis=1, keepdims=True)
    lower = mask_bf(iota((128, 128), 1) < iota((128, 128), 0))
    starts = mm(lower, jnp.broadcast_to(before, (128, 128)).astype(BF))[:, :1]
    y_pos = y_at[0]
    places = []
    for w in range(2):
        both = []
        for half in range(2):
            filt = mm(shot_ref[w], mid_ref[half, w])
            power = jnp.mean(filt * filt, axis=1, keepdims=True) + 1e-6
            done = pltpu.roll(filt * lax.rsqrt(power), NT - 32, 1)
            both.append(done.reshape(32, 1, 8, NT))
            b = 2 * w + half
            places.append(jnp.sum(marks[b] * (ranks[b] + starts), axis=0, keepdims=True))
        trace = jnp.concatenate(both, axis=1).reshape(512, NT).astype(BF)
        for y in range(4):
            trace_ref[(y - y_pos) & 3, 512 * w : 512 * w + 512, :] = trace[:, 128 * y : 128 * y + 128]
    place = jnp.concatenate(places, axis=1).astype(I32)
    owner = jnp.concatenate(owner, axis=1)
    local = jnp.concatenate(local, axis=1)
    place_lane = mask_bf(iota((128, CROWS), 0) == (place & 127))
    here = iota((8, CROWS), 0) == lax.shift_right_logical(place, 7)
    ids = jnp.concatenate([jnp.where(here, owner, 0.0), jnp.where(here, local, 0.0)], axis=0)
    ids = mm_nt(ids.astype(BF), place_lane)
    first = jnp.broadcast_to(starts, (128, 128)).T[:16]
    first = lax.shift_right_logical(first.astype(I32), 4)
    count = lax.shift_right_logical(pltpu.roll(first, 126, 1) - first + 4, 2)
    count = jnp.maximum(count, 1).astype(F32).astype(BF)
    first = jnp.minimum(first, QMAX).astype(F32).astype(BF)
    here, there = iota((128, 128), 0), iota((128, 128), 1)
    even = 2 * (there & 31)
    pick_first = mask_bf((here == even) & (there >= 64) & (there < 96))
    pick_count = mask_bf((here == even) & (there >= 96))
    first = mm(first, pick_first) + mm(count, pick_count)
    r, c = iota((16, 128), 0), iota((16, 128), 1)
    ids = jnp.where((r == 7) & (c >= 64), first, ids).astype(BF)
    traces = jnp.concatenate([trace_ref[d] for d in range(4)], axis=1)
    for b in range(2):
        size = min(512, VALID - 512 * b)
        order = mask_bf(iota((size, CROWS), 0) + 512 * b == place)
        rows = mm(order, traces).astype(BF)
        for d in range(4):
            outs[d][512 * b : 512 * b + size, :] = rows[:, 128 * d : 128 * d + 128]
    for d in range(4):
        outs[d][VALID:, :] = ids


def filtered(at, rows, parts):
    scratch = [
        pltpu.VMEM((2, 256, 384), BF),
        pltpu.VMEM((2, 256, 1152), BF),
        pltpu.VMEM((2, 2, 1152, NT), BF),
        pltpu.VMEM((4, CROWS, 128), BF),
    ]
    scratch.append(pltpu.VMEM((CROWS, NT), BF))
    return pl.pallas_call(
        lambda *refs: filter_kernel(len(parts), *refs),
        out_shape=[jax.ShapeDtypeStruct((YROWS, 128), BF)] * 4,
        in_specs=[SMEM] * 4 + [VMEM] * (2 + len(parts)),
        out_specs=[VMEM] * 4,
        scratch_shapes=scratch,
        compiler_params=params(),
    )(*at, *rows, *parts)


def regroup_kernel(z_at, c_at, *refs):
    for dz in range(8):
        for dx in range(4):
            for dc in range(2):
                source = (dc * 8 + dz) * ROWS
                to = ((z_at[0] + dz) & 7) * 2 + (c_at[0] ^ dc)
                refs[4][to, dx * ROWS : (dx + 1) * ROWS, :] = refs[dx][source : source + ROWS, :]


def turn_kernel(*refs):
    for dx in range(4):
        for dz in range(8):
            for dc in range(2):
                source = (dc * 4 + dx) * ROWS
                place = (dc * 8 + dz) * ROWS
                refs[8 + dx][place : place + ROWS, :] = refs[dz][source : source + ROWS, :]


def give_kernel(*refs):
    for dx in range(4):
        refs[4][128 * dx : 128 * dx + 128, :] = refs[dx][128:, :]


def shuffled(kernel, parts, shapes, scalars=()):
    return pl.pallas_call(
        kernel,
        out_shape=[jax.ShapeDtypeStruct(shape, BF) for shape in shapes],
        in_specs=[SMEM] * len(scalars) + [VMEM] * len(parts),
        out_specs=[VMEM] * len(shapes),
        compiler_params=params(8),
    )(*scalars, *parts)


def stack_kernel(last, core_ref, info_ref, l0, l1, l2, l3, *refs):
    lists = (l0, l1, l2, l3)
    table_ref, long_ref = refs[-2:]
    lane = iota((8, 128), 1)
    sub = iota((8, 128), 0)
    for n, ref in enumerate(lists):
        ids = ref[VALID:, :].astype(F32)
        code = jnp.where((sub == 7) & (lane >= 64), -1.0, ids[:8] * 128.0 + ids[8:])
        after = pltpu.roll(code, 7, 0)
        for e in range(8):
            shift = (64 * (n & 1) - 16 * e) % 128
            limit = 128 + 64 * (n & 1) - 16 * e
            a = pltpu.roll(code, shift, 1) if shift else code
            b = pltpu.roll(after, shift, 1) if shift else after
            rows = jnp.where(lane < limit, a, b)
            for r in range(8):
                table_ref[n, 8 * r + e] = jnp.broadcast_to(rows[r : r + 1, :], (8, 128))
    core = core_ref[0]
    bins = iota((256, 128), 0)
    bins = (bins & 127) + jnp.where(bins < 128, core, 1 - core) * 128
    bins = bins.astype(F32).astype(BF)
    low = lane < 64
    one, zero = jnp.ones((256, 128), BF), jnp.zeros((256, 128), BF)

    def hot(pair, first, second):
        code = jnp.where(low, first, second) - (pair * 256).astype(F32)
        code = jnp.where((code >= 0.0) & (code < 256.0), code, 300.0)
        code = jnp.concatenate([code, code], axis=0).astype(BF)
        code = jnp.broadcast_to(code[None], (16, 16, 128)).reshape(256, 128)
        return jnp.where(code == bins, one, zero)

    def window(pair, w):
        codes, rows = [], []
        for n in range(4):
            q = info_ref[n, pair]
            if w is None:
                code = table_ref[n, q]
            else:
                q0 = q + 4 * w
                q = jnp.minimum(q0, QMAX)
                code = jnp.where((lane & 63) >= (q0 - q) * 16, table_ref[n, q], -1.0)
            codes.append(code)
            rows.append(lists[n][pl.ds(pl.multiple_of(q * 16, 16), 64), :])
        left, right = hot(pair, *codes[:2]), hot(pair, *codes[2:])
        return mm(jnp.concatenate([left, right], axis=1), jnp.concatenate(rows, axis=0))

    def store(pair, total):
        if last:
            total = total + refs[0][pair]
            refs[1][pair] = total[:128].astype(BF)
            refs[2][pair] = total[128:].astype(BF)
        else:
            refs[0][pair] = total

    def windows(pair):
        counts = [info_ref[n, 32 + pair] for n in range(4)]
        return jnp.maximum(jnp.maximum(counts[0], counts[1]), jnp.maximum(counts[2], counts[3]))

    def body(pair, long):
        store(pair, window(pair, None))
        long_ref[long] = pair
        return long + jnp.where(windows(pair) > 1, 1, 0)

    long = lax.fori_loop(0, SHOTS // 2, body, jnp.int32(0), unroll=16)

    def rest(i, carry):
        pair = long_ref[i]
        total = lax.fori_loop(1, windows(pair), lambda w, t: t + window(pair, w), window(pair, None))
        store(pair, total)
        return carry

    lax.fori_loop(0, long, rest, 0)


def stacked(core, lists, sums=None):
    info = jnp.stack([v[VALID + 7, 64:] for v in lists]).astype(I32)
    if sums is None:
        out_shape, extra = jax.ShapeDtypeStruct((SHOTS // 2, 256, 128), F32), []
    else:
        out_shape, extra = (jax.ShapeDtypeStruct((SHOTS // 2, BIN, 128), BF),) * 2, [sums]
    return pl.pallas_call(
        lambda *refs: stack_kernel(sums is not None, *refs),
        out_shape=out_shape,
        in_specs=[SMEM, SMEM] + [VMEM] * (4 + len(extra)),
        out_specs=VMEM if sums is None else (VMEM, VMEM),
        scratch_shapes=[pltpu.VMEM((4, 64, 8, 128), F32), pltpu.SMEM((SHOTS // 2,), I32)],
        compiler_params=params(),
        name="stack0" if sums is None else "stack1",
    )(core, info, *lists, *extra)


def fold_kernel(x_ref, mine_ref, other_ref, *outs):
    for d in range(4):
        at = pl.ds(8 * ((x_ref[0] + d) & 3), 8)
        outs[d][...] = (mine_ref[at].astype(F32) + other_ref[at].astype(F32)).astype(BF)


def folded(x_pos, mine, other):
    return pl.pallas_call(
        fold_kernel,
        out_shape=[jax.ShapeDtypeStruct((8, BIN, 128), BF)] * 4,
        in_specs=[SMEM, VMEM, VMEM],
        out_specs=[VMEM] * 4,
        compiler_params=params(),
        name="fold",
    )(x_pos, mine, other)


def around(parts, axis):
    n = len(parts)
    out = [parts[0]]
    for d in range(1, n):
        out.append(lax.ppermute(parts[d], axis, [(i, (i + d) % n) for i in range(n)]))
    return out


def swapped(part):
    return lax.ppermute(part, "c", [(0, 1), (1, 0)])


def steps(gathers, trace_slot, gain, midbin, bin_row, taps_shot, taps_time):
    at = [lax.axis_index(a).reshape(1) for a in ("x", "z", "c", "y")]
    x_pos, z_pos, core = at[:3]
    x = gathers.reshape(BLK, NT)
    table = bin_row.reshape(64, 128)
    rows = band_rows(taps_time, taps_shot)
    sends = pick(x, trace_slot, gain, midbin, table, at)
    parts = around(sends[:8], "z")
    late = around(sends[8:], "x")
    (late,) = shuffled(regroup_kernel, late, [(16, 4 * ROWS, NT)], [z_pos, core])
    late = lax.all_to_all(late, ("z", "c"), split_axis=0, concat_axis=0, tiled=True)
    parts = around(shuffled(turn_kernel, parts, [(256, NT)] * 4), "x")
    (other,) = shuffled(give_kernel, parts, [(512, NT)])
    parts.append(swapped(other))
    lists = around(filtered(at, rows, parts), "y")
    later = around(filtered(at, rows, [late]), "y")
    mine, other = stacked(core, later, stacked(core, lists))
    other = swapped(other)
    parts = around(folded(x_pos, mine, other), "x")
    total = sum(p.astype(F32) for p in parts).astype(BF)
    parts = lax.all_to_all(total, "z", split_axis=0, concat_axis=0, tiled=True)
    scale = (8192 / 491520) ** 0.5
    return jnp.sum(parts.astype(F32), axis=0) * scale


def solution(mesh):
    finer = Mesh(mesh.devices.reshape(4, 8, 2, mesh.shape["cmp"]), ("x", "z", "c", "y"))
    shot = ("x", "z", "c")
    in_specs = (P(shot, "y", None), P(shot, "y"), P(shot, "y"), P(shot, "y"), P(), P(), P())
    return jax.shard_map(
        steps, mesh=finer, in_specs=in_specs, out_specs=P(shot, "y"), check_vma=False
    )
```

```python
import jax
import jax.numpy as jnp
from jax import lax
from jax.experimental import pallas as pl
from jax.experimental.pallas import tpu as pltpu
from jax.sharding import Mesh
from jax.sharding import PartitionSpec as P


BF = jnp.bfloat16
F32 = jnp.float32
I32 = jnp.int32
SHOTS, RPD, PER = 64, 30, 15
ROWS = 16
CROWS = SHOTS * ROWS
VALID = SHOTS * PER
NT, BLK, BIN = 512, 1920, 128
YROWS = VALID + 16
QMAX = (YROWS - 64) // 16
WIDE = 640
VMEM = pl.BlockSpec(memory_space=pltpu.VMEM)
SMEM = pl.BlockSpec(memory_space=pltpu.SMEM)


def params(mib=24):
    return pltpu.CompilerParams(vmem_limit_bytes=mib * 1024 * 1024)


def iota(shape, dim):
    return lax.broadcasted_iota(I32, shape, dim)


def mask_bf(mask):
    return jnp.where(mask, 1.0, 0.0).astype(BF)


def mm(a, b):
    return jnp.dot(a, b, preferred_element_type=F32)


def mm_nt(a, b):
    return lax.dot_general(a, b, (((1,), (1,)), ((), ())), preferred_element_type=F32)


def column(ref, base, wanted):
    row = ref[:, base : base + WIDE].astype(F32)
    return jnp.sum(jnp.where(wanted, row, 0.0), axis=1, keepdims=True)


def pick_kernel(chunk, x_hbm, slot_hbm, gain_hbm, mid_hbm, tab_hbm, x_at, z_at, c_at, *refs):
    outs, refs = refs[: 8 - 4 * chunk], refs[8 - 4 * chunk :]
    x_ref, slot_ref, gain_ref, mid_ref, tab_ref, block_ref, in_sems = refs
    sources = (slot_hbm, gain_hbm, mid_hbm, tab_hbm, x_hbm)
    targets = (slot_ref, gain_ref, mid_ref, tab_ref, x_ref)
    copies = [pltpu.make_async_copy(sources[i], targets[i], in_sems.at[i]) for i in range(5)]
    for copy in copies:
        copy.start()
    for copy in copies[:4]:
        copy.wait()
    x_pos, z_pos, core = x_at[0], z_at[0], c_at[0]
    table = tab_ref[...]
    owners = lax.shift_right_logical(table, 7).astype(F32).astype(BF)
    locals_ = (table & 127).astype(F32).astype(BF)
    here, there = iota((256, 256), 0), iota((256, 256), 1)
    gather = mask_bf((lax.shift_right_logical(here, 4) == lax.shift_right_logical(there, 4)) & ((here & 15) == 15))
    place = iota((256, 1), 0) & 15
    real = place < PER
    lane = iota((256, NT), 1)

    def columns(chunk, b):
        base = min((480 * b) // 128 * 128, BLK - WIDE)
        receiver = (lax.shift_right_logical(iota((256, 1), 0), 4) + 16 * b) * RPD + chunk * PER + place
        wanted = (iota((256, WIDE), 1) + base == receiver) & real
        slot = column(slot_ref, base, wanted).astype(I32)
        block = (slot >= BLK).astype(I32) + (slot >= 2 * BLK).astype(I32) + (slot >= 3 * BLK).astype(I32)
        slot = jnp.where(real, slot - BLK * block, -1)
        gain = column(gain_ref, base, wanted)
        mid = column(mid_ref, base, wanted).astype(I32)
        pick_row = mask_bf(iota((256, 64), 1) == lax.shift_right_logical(mid, 7))
        pick_lane = iota((256, 128), 1) == (mid & 127)
        owner = jnp.sum(jnp.where(pick_lane, mm(pick_row, owners), 0.0), axis=1, keepdims=True)
        local = jnp.sum(jnp.where(pick_lane, mm(pick_row, locals_), 0.0), axis=1, keepdims=True)
        spread = jnp.where(lane < NT // 2, owner, local)
        spread = jnp.where(((lane & 15) == place) & real, spread, 0.0).astype(BF)
        return slot, gain, spread

    for b in range(CROWS // 256):
        slot, gain, spread = columns(chunk, b)
        one_hot = mask_bf(iota((256, BLK), 1) == slot)
        if b == 0:
            copies[4].wait()
        out = mm(one_hot, x_ref[...]) * gain + mm(gather, spread)
        block_ref[b] = out.astype(BF)
    for dx in range(4):
        for dz in range(8):
            for dc in range(2):
                row = (2 * ((z_pos + dz) & 7) + (core ^ dc)) * ROWS
                piece = block_ref[(x_pos + dx) & 3, pl.ds(pl.multiple_of(row, ROWS), ROWS), :]
                ref, to = (outs[dx], dc * 8 + dz) if chunk else (outs[dz], dc * 4 + dx)
                ref[to * ROWS : (to + 1) * ROWS, :] = piece


def pick(chunk, x, slot, gain, mid, table, at):
    shape, count = ((256, NT), 4) if chunk else ((128, NT), 8)
    hbm = pl.BlockSpec(memory_space=pltpu.HBM)
    return pl.pallas_call(
        lambda *refs: pick_kernel(chunk, *refs),
        out_shape=[jax.ShapeDtypeStruct(shape, BF)] * count,
        in_specs=[hbm] * 5 + [SMEM] * 3,
        out_specs=[VMEM] * count,
        scratch_shapes=[
            pltpu.VMEM((BLK, NT), BF),
            pltpu.VMEM((1, BLK), I32),
            pltpu.VMEM((1, BLK), F32),
            pltpu.VMEM((1, BLK), I32),
            pltpu.VMEM((64, 128), I32),
            pltpu.VMEM((4, 256, NT), BF),
            pltpu.SemaphoreType.DMA((5,)),
        ],
        compiler_params=params(60),
    )(x, slot, gain, mid, table, *at[:3])


def band_kernel(time_ref, shot_ref, time_out, shot_out):
    step, col = iota((256, 128), 0), iota((256, 128), 1)
    wrapped = (step < 128) == (col < 32)
    for k in range(3):
        base = jnp.broadcast_to(time_ref[k : k + 1, :], (128, 256))
        rolled = pltpu.roll(base, 0, 1, stride=1, stride_axis=0)
        band = rolled.T
        at = slice(128 * k, 128 * k + 128)
        time_out[0, :, at] = band.astype(BF)
        time_out[1, :, at] = jnp.where(wrapped, band, 0.0).astype(BF)
        base = jnp.broadcast_to(shot_ref[k : k + 1, :], (256, 640))
        rolled = pltpu.roll(base, 0, 1, stride=1, stride_axis=0)
        shot_out[0, :, 384 * k : 384 * k + 384] = rolled[:, 128:512].astype(BF)
        shot_out[1, :, 384 * k : 384 * k + 384] = rolled[:, :384].astype(BF)


def band_rows(taps_time, taps_shot):
    time_row = jnp.pad(taps_time.astype(BF).astype(F32), ((0, 0), (64, 128)))
    shot = taps_shot.astype(BF).astype(F32)
    shot_row = lax.pad(shot, jnp.float32(0), ((0, 0, 0), (8, 640 - 8 - 241, 7)))
    return time_row, shot_row


def filter_kernel(count, x_at, z_at, c_at, y_at, time_row, shot_row, *refs):
    parts, outs = refs[:count], refs[count : count + 4]
    time_ref, shot_ref, mid_ref, trace_ref, *rest = refs[count + 4 :]
    x_ref = rest[0]
    for dx in range(4):
        for z in range(8):
            for dc in range(2):
                if count == 1:
                    block = parts[0][z * 2 + dc, dx * ROWS : (dx + 1) * ROWS, :]
                    from_z, from_c = z, dc
                else:
                    ref, to = (parts[4], dx * 8 + z) if dc else (parts[dx], z)
                    block = ref[to * ROWS : (to + 1) * ROWS, :]
                    from_z, from_c = (z_at[0] - z) & 7, c_at[0] ^ dc
                shot = ((x_at[0] - dx) & 3) * 16 + from_z * 2 + from_c
                x_ref[pl.ds(pl.multiple_of(shot * ROWS, ROWS), ROWS), :] = block
    band_kernel(time_row, shot_row, time_ref, shot_ref)
    row = iota((256, NT), 0)
    lane = iota((256, NT), 1)
    keep = ((row & 15) == 15) & (lax.shift_right_logical(row, 4) == lax.shift_right_logical(lane & 255, 4))
    bad = (iota((1, 256), 1) & 15) == 15
    upper = mask_bf(iota((256, 256), 0) < iota((256, 256), 1))
    owner, local, marks, ranks = [], [], [], []
    before = jnp.zeros((128, 1), F32)
    for b in range(4):
        rows = slice(256 * b, 256 * b + 256)
        part = jnp.where(keep, x_ref[rows, :].astype(F32), 0.0)
        ids = jnp.sum(part, axis=0, keepdims=True)
        owner.append(jnp.where(bad, 127.0, ids[:, :256]))
        local.append(ids[:, 256:])
        for j in range(4):
            if j:
                lhs, band = x_ref[rows, 128 * j - 128 : 128 * j + 128], time_ref[0]
            else:
                lhs = jnp.concatenate([x_ref[rows, 384:], x_ref[rows, :128]], axis=1)
                band = time_ref[1]
            mids = mm(lhs, band).reshape(16, 2, 8, 384)
            for half in range(2):
                part = mids[:, half].reshape(128, 384).astype(BF)
                for k in range(3):
                    value = part[:, 128 * k : 128 * k + 128]
                    for w in range(2):
                        at = 128 * b - 128 * w
                        if 0 <= at < 384:
                            at += 384 * k
                            mid_ref[half, w, at : at + 128, 128 * j : 128 * j + 128] = value
            if j == 1:
                mark = jnp.where(iota((128, 256), 0).astype(F32) == owner[b], 1.0, 0.0)
                ranks.append(mm(mark.astype(BF), upper) + before)
                marks.append(mark)
                before = before + jnp.sum(mark, axis=1, keepdims=True)
    lower = mask_bf(iota((128, 128), 1) < iota((128, 128), 0))
    starts = mm(lower, jnp.broadcast_to(before, (128, 128)).astype(BF))[:, :1]
    y_pos = y_at[0]
    places = []
    for w in range(2):
        both = []
        for half in range(2):
            filt = mm(shot_ref[w], mid_ref[half, w])
            power = jnp.mean(filt * filt, axis=1, keepdims=True) + 1e-6
            done = pltpu.roll(filt * lax.rsqrt(power), NT - 32, 1)
            both.append(done.reshape(32, 1, 8, NT))
            b = 2 * w + half
            places.append(jnp.sum(marks[b] * (ranks[b] + starts), axis=0, keepdims=True))
        trace = jnp.concatenate(both, axis=1).reshape(512, NT).astype(BF)
        for y in range(4):
            trace_ref[(y - y_pos) & 3, 512 * w : 512 * w + 512, :] = trace[:, 128 * y : 128 * y + 128]
    place = jnp.concatenate(places, axis=1).astype(I32)
    owner = jnp.concatenate(owner, axis=1)
    local = jnp.concatenate(local, axis=1)
    place_lane = mask_bf(iota((128, CROWS), 0) == (place & 127))
    here = iota((8, CROWS), 0) == lax.shift_right_logical(place, 7)
    ids = jnp.concatenate([jnp.where(here, owner, 0.0), jnp.where(here, local, 0.0)], axis=0)
    ids = mm_nt(ids.astype(BF), place_lane)
    first = jnp.broadcast_to(starts, (128, 128)).T[:16]
    first = lax.shift_right_logical(first.astype(I32), 4)
    count = lax.shift_right_logical(pltpu.roll(first, 126, 1) - first + 4, 2)
    count = jnp.maximum(count, 1).astype(F32).astype(BF)
    first = jnp.minimum(first, QMAX).astype(F32).astype(BF)
    here, there = iota((128, 128), 0), iota((128, 128), 1)
    even = 2 * (there & 31)
    pick_first = mask_bf((here == even) & (there >= 64) & (there < 96))
    pick_count = mask_bf((here == even) & (there >= 96))
    first = mm(first, pick_first) + mm(count, pick_count)
    r, c = iota((16, 128), 0), iota((16, 128), 1)
    ids = jnp.where((r == 7) & (c >= 64), first, ids).astype(BF)
    traces = jnp.concatenate([trace_ref[d] for d in range(4)], axis=1)
    for b in range(2):
        size = min(512, VALID - 512 * b)
        order = mask_bf(iota((size, CROWS), 0) + 512 * b == place)
        rows = mm(order, traces).astype(BF)
        for d in range(4):
            outs[d][512 * b : 512 * b + size, :] = rows[:, 128 * d : 128 * d + 128]
    for d in range(4):
        outs[d][VALID:, :] = ids


def filtered(at, rows, parts):
    scratch = [
        pltpu.VMEM((2, 256, 384), BF),
        pltpu.VMEM((2, 256, 1152), BF),
        pltpu.VMEM((2, 2, 1152, NT), BF),
        pltpu.VMEM((4, CROWS, 128), BF),
    ]
    scratch.append(pltpu.VMEM((CROWS, NT), BF))
    return pl.pallas_call(
        lambda *refs: filter_kernel(len(parts), *refs),
        out_shape=[jax.ShapeDtypeStruct((YROWS, 128), BF)] * 4,
        in_specs=[SMEM] * 4 + [VMEM] * (2 + len(parts)),
        out_specs=[VMEM] * 4,
        scratch_shapes=scratch,
        compiler_params=params(),
    )(*at, *rows, *parts)


def regroup_kernel(z_at, c_at, *refs):
    for dz in range(8):
        for dx in range(4):
            for dc in range(2):
                source = (dc * 8 + dz) * ROWS
                to = ((z_at[0] + dz) & 7) * 2 + (c_at[0] ^ dc)
                refs[4][to, dx * ROWS : (dx + 1) * ROWS, :] = refs[dx][source : source + ROWS, :]


def turn_kernel(*refs):
    for dx in range(4):
        for dz in range(8):
            for dc in range(2):
                source = (dc * 4 + dx) * ROWS
                place = (dc * 8 + dz) * ROWS
                refs[8 + dx][place : place + ROWS, :] = refs[dz][source : source + ROWS, :]


def give_kernel(*refs):
    for dx in range(4):
        refs[4][128 * dx : 128 * dx + 128, :] = refs[dx][128:, :]


def shuffled(kernel, parts, shapes, scalars=()):
    return pl.pallas_call(
        kernel,
        out_shape=[jax.ShapeDtypeStruct(shape, BF) for shape in shapes],
        in_specs=[SMEM] * len(scalars) + [VMEM] * len(parts),
        out_specs=[VMEM] * len(shapes),
        compiler_params=params(8),
    )(*scalars, *parts)


def stack_kernel(last, core_ref, info_ref, l0, l1, l2, l3, *refs):
    lists = (l0, l1, l2, l3)
    table_ref, long_ref = refs[-2:]
    lane = iota((8, 128), 1)
    sub = iota((8, 128), 0)
    for n, ref in enumerate(lists):
        ids = ref[VALID:, :].astype(F32)
        code = jnp.where((sub == 7) & (lane >= 64), -1.0, ids[:8] * 128.0 + ids[8:])
        after = pltpu.roll(code, 7, 0)
        for e in range(8):
            shift = (64 * (n & 1) - 16 * e) % 128
            limit = 128 + 64 * (n & 1) - 16 * e
            a = pltpu.roll(code, shift, 1) if shift else code
            b = pltpu.roll(after, shift, 1) if shift else after
            rows = jnp.where(lane < limit, a, b)
            for r in range(8):
                table_ref[n, 8 * r + e] = jnp.broadcast_to(rows[r : r + 1, :], (8, 128))
    core = core_ref[0]
    bins = iota((256, 128), 0)
    bins = (bins & 127) + jnp.where(bins < 128, core, 1 - core) * 128
    bins = bins.astype(F32).astype(BF)
    low = lane < 64
    one, zero = jnp.ones((256, 128), BF), jnp.zeros((256, 128), BF)

    def hot(pair, first, second):
        code = jnp.where(low, first, second) - (pair * 256).astype(F32)
        code = jnp.where((code >= 0.0) & (code < 256.0), code, 300.0)
        code = jnp.concatenate([code, code], axis=0).astype(BF)
        code = jnp.broadcast_to(code[None], (16, 16, 128)).reshape(256, 128)
        return jnp.where(code == bins, one, zero)

    def window(pair, w):
        codes, rows = [], []
        for n in range(4):
            q = info_ref[n, pair]
            if w is None:
                code = table_ref[n, q]
            else:
                q0 = q + 4 * w
                q = jnp.minimum(q0, QMAX)
                code = jnp.where((lane & 63) >= (q0 - q) * 16, table_ref[n, q], -1.0)
            codes.append(code)
            rows.append(lists[n][pl.ds(pl.multiple_of(q * 16, 16), 64), :])
        left, right = hot(pair, *codes[:2]), hot(pair, *codes[2:])
        return mm(jnp.concatenate([left, right], axis=1), jnp.concatenate(rows, axis=0))

    def store(pair, total):
        if last:
            total = total + refs[0][pair]
            refs[1][pair] = total[:128].astype(BF)
            refs[2][pair] = total[128:].astype(BF)
        else:
            refs[0][pair] = total

    def windows(pair):
        counts = [info_ref[n, 32 + pair] for n in range(4)]
        return jnp.maximum(jnp.maximum(counts[0], counts[1]), jnp.maximum(counts[2], counts[3]))

    def body(pair, long):
        store(pair, window(pair, None))
        long_ref[long] = pair
        return long + jnp.where(windows(pair) > 1, 1, 0)

    long = lax.fori_loop(0, SHOTS // 2, body, jnp.int32(0), unroll=16 if last else 8)

    def rest(i, carry):
        pair = long_ref[i]
        total = window(pair, None) + window(pair, 1)
        total = lax.fori_loop(2, windows(pair), lambda w, t: t + window(pair, w), total)
        store(pair, total)
        return carry

    lax.fori_loop(0, long, rest, 0)


def stacked(core, lists, sums=None):
    info = jnp.stack([v[VALID + 7, 64:] for v in lists]).astype(I32)
    if sums is None:
        out_shape, extra = jax.ShapeDtypeStruct((SHOTS // 2, 256, 128), F32), []
    else:
        out_shape, extra = (jax.ShapeDtypeStruct((SHOTS // 2, BIN, 128), BF),) * 2, [sums]
    return pl.pallas_call(
        lambda *refs: stack_kernel(sums is not None, *refs),
        out_shape=out_shape,
        in_specs=[SMEM, SMEM] + [VMEM] * (4 + len(extra)),
        out_specs=VMEM if sums is None else (VMEM, VMEM),
        scratch_shapes=[pltpu.VMEM((4, 64, 8, 128), F32), pltpu.SMEM((SHOTS // 2,), I32)],
        compiler_params=params(),
        name="stack0" if sums is None else "stack1",
    )(core, info, *lists, *extra)


def fold_kernel(x_ref, mine_ref, other_ref, *outs):
    for d in range(4):
        at = pl.ds(8 * ((x_ref[0] + d) & 3), 8)
        outs[d][...] = (mine_ref[at].astype(F32) + other_ref[at].astype(F32)).astype(BF)


def folded(x_pos, mine, other):
    return pl.pallas_call(
        fold_kernel,
        out_shape=[jax.ShapeDtypeStruct((8, BIN, 128), BF)] * 4,
        in_specs=[SMEM, VMEM, VMEM],
        out_specs=[VMEM] * 4,
        compiler_params=params(),
        name="fold",
    )(x_pos, mine, other)


def around(parts, axis):
    n = len(parts)
    out = [parts[0]]
    for d in range(1, n):
        out.append(lax.ppermute(parts[d], axis, [(i, (i + d) % n) for i in range(n)]))
    return out


def swapped(part):
    return lax.ppermute(part, "c", [(0, 1), (1, 0)])


def steps(gathers, trace_slot, gain, midbin, bin_row, taps_shot, taps_time):
    at = [lax.axis_index(a).reshape(1) for a in ("x", "z", "c", "y")]
    x_pos, z_pos, core = at[:3]
    x = gathers.reshape(BLK, NT)
    table = bin_row.reshape(64, 128)
    rows = band_rows(taps_time, taps_shot)
    parts = around(pick(0, x, trace_slot, gain, midbin, table, at), "z")
    late = around(pick(1, x, trace_slot, gain, midbin, table, at), "x")
    (late,) = shuffled(regroup_kernel, late, [(16, 4 * ROWS, NT)], [z_pos, core])
    late = lax.all_to_all(late, ("z", "c"), split_axis=0, concat_axis=0, tiled=True)
    parts = around(shuffled(turn_kernel, parts, [(256, NT)] * 4), "x")
    (other,) = shuffled(give_kernel, parts, [(512, NT)])
    parts.append(swapped(other))
    lists = around(filtered(at, rows, parts), "y")
    later = around(filtered(at, rows, [late]), "y")
    mine, other = stacked(core, later, stacked(core, lists))
    other = swapped(other)
    parts = around(folded(x_pos, mine, other), "x")
    total = sum(p.astype(F32) for p in parts).astype(BF)
    parts = lax.all_to_all(total, "z", split_axis=0, concat_axis=0, tiled=True)
    scale = (8192 / 491520) ** 0.5
    return jnp.sum(parts.astype(F32), axis=0) * scale


def solution(mesh):
    finer = Mesh(mesh.devices.reshape(4, 8, 2, mesh.shape["cmp"]), ("x", "z", "c", "y"))
    shot = ("x", "z", "c")
    in_specs = (P(shot, "y", None), P(shot, "y"), P(shot, "y"), P(shot, "y"), P(), P(), P())
    return jax.shard_map(
        steps, mesh=finer, in_specs=in_specs, out_specs=P(shot, "y"), check_vma=False
    )
```

```python
import jax
import jax.numpy as jnp
from jax import lax
from jax.experimental import pallas as pl
from jax.experimental.pallas import tpu as pltpu
from jax.sharding import Mesh
from jax.sharding import PartitionSpec as P


BF = jnp.bfloat16
F32 = jnp.float32
I32 = jnp.int32
SHOTS, RPD, PER = 64, 30, 15
ROWS = 16
CROWS = SHOTS * ROWS
VALID = SHOTS * PER
NT, BLK, BIN = 512, 1920, 128
YROWS = VALID + 16
QMAX = (YROWS - 64) // 16
WIDE = 640
VMEM = pl.BlockSpec(memory_space=pltpu.VMEM)
SMEM = pl.BlockSpec(memory_space=pltpu.SMEM)


def params(mib=24):
    return pltpu.CompilerParams(vmem_limit_bytes=mib * 1024 * 1024)


def iota(shape, dim):
    return lax.broadcasted_iota(I32, shape, dim)


def mask_bf(mask):
    return jnp.where(mask, 1.0, 0.0).astype(BF)


def mm(a, b):
    return jnp.dot(a, b, preferred_element_type=F32)


def mm_nt(a, b):
    return lax.dot_general(a, b, (((1,), (1,)), ((), ())), preferred_element_type=F32)


def column(ref, base, wanted):
    row = ref[:, base : base + WIDE].astype(F32)
    return jnp.sum(jnp.where(wanted, row, 0.0), axis=1, keepdims=True)


def pick_kernel(chunk, x_hbm, slot_hbm, gain_hbm, mid_hbm, tab_hbm, x_at, z_at, c_at, *refs):
    outs, refs = refs[: 1 + 3 * chunk], refs[1 + 3 * chunk :]
    x_ref, slot_ref, gain_ref, mid_ref, tab_ref, block_ref, in_sems = refs
    sources = (slot_hbm, gain_hbm, mid_hbm, tab_hbm, x_hbm)
    targets = (slot_ref, gain_ref, mid_ref, tab_ref, x_ref)
    copies = [pltpu.make_async_copy(sources[i], targets[i], in_sems.at[i]) for i in range(5)]
    for copy in copies:
        copy.start()
    for copy in copies[:4]:
        copy.wait()
    x_pos, z_pos, core = x_at[0], z_at[0], c_at[0]
    table = tab_ref[...]
    owners = lax.shift_right_logical(table, 7).astype(F32).astype(BF)
    locals_ = (table & 127).astype(F32).astype(BF)
    here, there = iota((256, 256), 0), iota((256, 256), 1)
    gather = mask_bf((lax.shift_right_logical(here, 4) == lax.shift_right_logical(there, 4)) & ((here & 15) == 15))
    place = iota((256, 1), 0) & 15
    real = place < PER
    lane = iota((256, NT), 1)

    def columns(chunk, b):
        base = min((480 * b) // 128 * 128, BLK - WIDE)
        receiver = (lax.shift_right_logical(iota((256, 1), 0), 4) + 16 * b) * RPD + chunk * PER + place
        wanted = (iota((256, WIDE), 1) + base == receiver) & real
        slot = column(slot_ref, base, wanted).astype(I32)
        block = (slot >= BLK).astype(I32) + (slot >= 2 * BLK).astype(I32) + (slot >= 3 * BLK).astype(I32)
        slot = jnp.where(real, slot - BLK * block, -1)
        gain = column(gain_ref, base, wanted)
        mid = column(mid_ref, base, wanted).astype(I32)
        pick_row = mask_bf(iota((256, 64), 1) == lax.shift_right_logical(mid, 7))
        pick_lane = iota((256, 128), 1) == (mid & 127)
        owner = jnp.sum(jnp.where(pick_lane, mm(pick_row, owners), 0.0), axis=1, keepdims=True)
        local = jnp.sum(jnp.where(pick_lane, mm(pick_row, locals_), 0.0), axis=1, keepdims=True)
        spread = jnp.where(lane < NT // 2, owner, local)
        spread = jnp.where(((lane & 15) == place) & real, spread, 0.0).astype(BF)
        return slot, gain, spread

    for b in range(CROWS // 256):
        slot, gain, spread = columns(chunk, b)
        one_hot = mask_bf(iota((256, BLK), 1) == slot)
        if b == 0:
            copies[4].wait()
        out = mm(one_hot, x_ref[...]) * gain + mm(gather, spread)
        block_ref[b] = out.astype(BF)
    for dx in range(4):
        for z in range(8):
            for c in range(2):
                x_to = (x_pos + dx) & 3
                if chunk:
                    row = (2 * ((z_pos + z) & 7) + (core ^ c)) * ROWS
                    row = pl.multiple_of(row, ROWS)
                    to = (c * 8 + z) * ROWS
                    outs[dx][to : to + ROWS, :] = block_ref[x_to, pl.ds(row, ROWS), :]
                else:
                    row = (2 * z + c) * ROWS
                    outs[0][2 * z + c, dx * ROWS : (dx + 1) * ROWS, :] = block_ref[x_to, row : row + ROWS, :]


def pick(chunk, x, slot, gain, mid, table, at):
    shape, count = ((256, NT), 4) if chunk else ((16, 4 * ROWS, NT), 1)
    hbm = pl.BlockSpec(memory_space=pltpu.HBM)
    return pl.pallas_call(
        lambda *refs: pick_kernel(chunk, *refs),
        out_shape=[jax.ShapeDtypeStruct(shape, BF)] * count,
        in_specs=[hbm] * 5 + [SMEM] * 3,
        out_specs=[VMEM] * count,
        scratch_shapes=[
            pltpu.VMEM((BLK, NT), BF),
            pltpu.VMEM((1, BLK), I32),
            pltpu.VMEM((1, BLK), F32),
            pltpu.VMEM((1, BLK), I32),
            pltpu.VMEM((64, 128), I32),
            pltpu.VMEM((4, 256, NT), BF),
            pltpu.SemaphoreType.DMA((5,)),
        ],
        compiler_params=params(60),
    )(x, slot, gain, mid, table, *at[:3])


def band_kernel(time_ref, shot_ref, time_out, shot_out):
    step, col = iota((256, 128), 0), iota((256, 128), 1)
    wrapped = (step < 128) == (col < 32)
    for k in range(3):
        base = jnp.broadcast_to(time_ref[k : k + 1, :], (128, 256))
        rolled = pltpu.roll(base, 0, 1, stride=1, stride_axis=0)
        band = rolled.T
        at = slice(128 * k, 128 * k + 128)
        time_out[0, :, at] = band.astype(BF)
        time_out[1, :, at] = jnp.where(wrapped, band, 0.0).astype(BF)
        base = jnp.broadcast_to(shot_ref[k : k + 1, :], (256, 640))
        rolled = pltpu.roll(base, 0, 1, stride=1, stride_axis=0)
        shot_out[0, :, 384 * k : 384 * k + 384] = rolled[:, 128:512].astype(BF)
        shot_out[1, :, 384 * k : 384 * k + 384] = rolled[:, :384].astype(BF)


def band_rows(taps_time, taps_shot):
    time_row = jnp.pad(taps_time.astype(BF).astype(F32), ((0, 0), (64, 128)))
    shot = taps_shot.astype(BF).astype(F32)
    shot_row = lax.pad(shot, jnp.float32(0), ((0, 0, 0), (8, 640 - 8 - 241, 7)))
    return time_row, shot_row


def filter_kernel(count, x_at, y_at, time_row, shot_row, *refs):
    parts, outs = refs[:count], refs[count : count + 4]
    time_ref, shot_ref, mid_ref, trace_ref, *rest = refs[count + 4 :]
    x_ref = rest[0]
    for dx in range(4):
        first = ((x_at[0] - dx) & 3) * 256
        if count > 1:
            x_ref[pl.ds(pl.multiple_of(first, 256), 256), :] = parts[dx][...]
        else:
            for k in range(16):
                to = pl.ds(pl.multiple_of(first + k * ROWS, ROWS), ROWS)
                x_ref[to, :] = parts[0][k, dx * ROWS : (dx + 1) * ROWS, :]
    band_kernel(time_row, shot_row, time_ref, shot_ref)
    row = iota((256, NT), 0)
    lane = iota((256, NT), 1)
    keep = ((row & 15) == 15) & (lax.shift_right_logical(row, 4) == lax.shift_right_logical(lane & 255, 4))
    bad = (iota((1, 256), 1) & 15) == 15
    upper = mask_bf(iota((256, 256), 0) < iota((256, 256), 1))
    owner, local, marks, ranks = [], [], [], []
    before = jnp.zeros((128, 1), F32)
    for b in range(4):
        rows = slice(256 * b, 256 * b + 256)
        part = jnp.where(keep, x_ref[rows, :].astype(F32), 0.0)
        ids = jnp.sum(part, axis=0, keepdims=True)
        owner.append(jnp.where(bad, 127.0, ids[:, :256]))
        local.append(ids[:, 256:])
        for j in range(4):
            if j:
                lhs, band = x_ref[rows, 128 * j - 128 : 128 * j + 128], time_ref[0]
            else:
                lhs = jnp.concatenate([x_ref[rows, 384:], x_ref[rows, :128]], axis=1)
                band = time_ref[1]
            mids = mm(lhs, band).reshape(16, 2, 8, 384)
            for half in range(2):
                part = mids[:, half].reshape(128, 384).astype(BF)
                for k in range(3):
                    value = part[:, 128 * k : 128 * k + 128]
                    for w in range(2):
                        at = 128 * b - 128 * w
                        if 0 <= at < 384:
                            at += 384 * k
                            mid_ref[half, w, at : at + 128, 128 * j : 128 * j + 128] = value
            if j == 1:
                mark = jnp.where(iota((128, 256), 0).astype(F32) == owner[b], 1.0, 0.0)
                ranks.append(mm(mark.astype(BF), upper) + before)
                marks.append(mark)
                before = before + jnp.sum(mark, axis=1, keepdims=True)
    lower = mask_bf(iota((128, 128), 1) < iota((128, 128), 0))
    starts = mm(lower, jnp.broadcast_to(before, (128, 128)).astype(BF))[:, :1]
    y_pos = y_at[0]
    places = []
    for w in range(2):
        both = []
        for half in range(2):
            filt = mm(shot_ref[w], mid_ref[half, w])
            power = jnp.mean(filt * filt, axis=1, keepdims=True) + 1e-6
            done = pltpu.roll(filt * lax.rsqrt(power), NT - 32, 1)
            both.append(done.reshape(32, 1, 8, NT))
            b = 2 * w + half
            places.append(jnp.sum(marks[b] * (ranks[b] + starts), axis=0, keepdims=True))
        trace = jnp.concatenate(both, axis=1).reshape(512, NT).astype(BF)
        for y in range(4):
            trace_ref[(y - y_pos) & 3, 512 * w : 512 * w + 512, :] = trace[:, 128 * y : 128 * y + 128]
    place = jnp.concatenate(places, axis=1).astype(I32)
    owner = jnp.concatenate(owner, axis=1)
    local = jnp.concatenate(local, axis=1)
    place_lane = mask_bf(iota((128, CROWS), 0) == (place & 127))
    here = iota((8, CROWS), 0) == lax.shift_right_logical(place, 7)
    ids = jnp.concatenate([jnp.where(here, owner, 0.0), jnp.where(here, local, 0.0)], axis=0)
    ids = mm_nt(ids.astype(BF), place_lane)
    first = jnp.broadcast_to(starts, (128, 128)).T[:16]
    first = lax.shift_right_logical(first.astype(I32), 4)
    count = lax.shift_right_logical(pltpu.roll(first, 126, 1) - first + 4, 2)
    count = jnp.maximum(count, 1).astype(F32).astype(BF)
    first = jnp.minimum(first, QMAX).astype(F32).astype(BF)
    here, there = iota((128, 128), 0), iota((128, 128), 1)
    even = 2 * (there & 31)
    pick_first = mask_bf((here == even) & (there >= 64) & (there < 96))
    pick_count = mask_bf((here == even) & (there >= 96))
    first = mm(first, pick_first) + mm(count, pick_count)
    r, c = iota((16, 128), 0), iota((16, 128), 1)
    ids = jnp.where((r == 7) & (c >= 64), first, ids).astype(BF)
    traces = jnp.concatenate([trace_ref[d] for d in range(4)], axis=1)
    for b in range(2):
        size = min(512, VALID - 512 * b)
        order = mask_bf(iota((size, CROWS), 0) + 512 * b == place)
        rows = mm(order, traces).astype(BF)
        for d in range(4):
            outs[d][512 * b : 512 * b + size, :] = rows[:, 128 * d : 128 * d + 128]
    for d in range(4):
        outs[d][VALID:, :] = ids


def filtered(at, rows, parts):
    scratch = [
        pltpu.VMEM((2, 256, 384), BF),
        pltpu.VMEM((2, 256, 1152), BF),
        pltpu.VMEM((2, 2, 1152, NT), BF),
        pltpu.VMEM((4, CROWS, 128), BF),
    ]
    scratch.append(pltpu.VMEM((CROWS, NT), BF))
    return pl.pallas_call(
        lambda *refs: filter_kernel(len(parts), *refs),
        out_shape=[jax.ShapeDtypeStruct((YROWS, 128), BF)] * 4,
        in_specs=[SMEM] * 2 + [VMEM] * (2 + len(parts)),
        out_specs=[VMEM] * 4,
        scratch_shapes=scratch,
        compiler_params=params(),
    )(at[0], at[3], *rows, *parts)


def regroup_kernel(z_at, c_at, *refs):
    for dz in range(8):
        for dx in range(4):
            for dc in range(2):
                source = (dc * 8 + dz) * ROWS
                to = ((z_at[0] + dz) & 7) * 2 + (c_at[0] ^ dc)
                refs[4][to, dx * ROWS : (dx + 1) * ROWS, :] = refs[dx][source : source + ROWS, :]


def turn_kernel(ref, *outs):
    for dx in range(4):
        for k in range(16):
            outs[dx][k * ROWS : (k + 1) * ROWS, :] = ref[k, dx * ROWS : (dx + 1) * ROWS, :]


def shuffled(kernel, parts, shapes, scalars=()):
    return pl.pallas_call(
        kernel,
        out_shape=[jax.ShapeDtypeStruct(shape, BF) for shape in shapes],
        in_specs=[SMEM] * len(scalars) + [VMEM] * len(parts),
        out_specs=[VMEM] * len(shapes),
        compiler_params=params(8),
    )(*scalars, *parts)


def stack_kernel(last, core_ref, info_ref, l0, l1, l2, l3, *refs):
    lists = (l0, l1, l2, l3)
    table_ref, long_ref = refs[-2:]
    lane = iota((8, 128), 1)
    sub = iota((8, 128), 0)
    for n, ref in enumerate(lists):
        ids = ref[VALID:, :].astype(F32)
        code = jnp.where((sub == 7) & (lane >= 64), -1.0, ids[:8] * 128.0 + ids[8:])
        after = pltpu.roll(code, 7, 0)
        for e in range(8):
            shift = (64 * (n & 1) - 16 * e) % 128
            limit = 128 + 64 * (n & 1) - 16 * e
            a = pltpu.roll(code, shift, 1) if shift else code
            b = pltpu.roll(after, shift, 1) if shift else after
            rows = jnp.where(lane < limit, a, b)
            for r in range(8):
                table_ref[n, 8 * r + e] = jnp.broadcast_to(rows[r : r + 1, :], (8, 128))
    core = core_ref[0]
    bins = iota((256, 128), 0)
    bins = (bins & 127) + jnp.where(bins < 128, core, 1 - core) * 128
    bins = bins.astype(F32).astype(BF)
    low = lane < 64
    one, zero = jnp.ones((256, 128), BF), jnp.zeros((256, 128), BF)

    def hot(pair, first, second):
        code = jnp.where(low, first, second) - (pair * 256).astype(F32)
        code = jnp.where((code >= 0.0) & (code < 256.0), code, 300.0)
        code = jnp.concatenate([code, code], axis=0).astype(BF)
        code = jnp.broadcast_to(code[None], (16, 16, 128)).reshape(256, 128)
        return jnp.where(code == bins, one, zero)

    def window(pair, w):
        codes, rows = [], []
        for n in range(4):
            q = info_ref[n, pair]
            if w is None:
                code = table_ref[n, q]
            else:
                q0 = q + 4 * w
                q = jnp.minimum(q0, QMAX)
                code = jnp.where((lane & 63) >= (q0 - q) * 16, table_ref[n, q], -1.0)
            codes.append(code)
            rows.append(lists[n][pl.ds(pl.multiple_of(q * 16, 16), 64), :])
        left, right = hot(pair, *codes[:2]), hot(pair, *codes[2:])
        return mm(jnp.concatenate([left, right], axis=1), jnp.concatenate(rows, axis=0))

    def store(pair, total):
        if last:
            total = total + refs[0][pair]
            refs[1][pair] = total[:128].astype(BF)
            refs[2][pair] = total[128:].astype(BF)
        else:
            refs[0][pair] = total

    def windows(pair):
        counts = [info_ref[n, 32 + pair] for n in range(4)]
        return jnp.maximum(jnp.maximum(counts[0], counts[1]), jnp.maximum(counts[2], counts[3]))

    def body(pair, long):
        store(pair, window(pair, None))
        long_ref[long] = pair
        return long + jnp.where(windows(pair) > 1, 1, 0)

    long = lax.fori_loop(0, SHOTS // 2, body, jnp.int32(0), unroll=16 if last else 8)

    def rest(i, carry):
        pair = long_ref[i]
        total = window(pair, None) + window(pair, 1)
        total = lax.fori_loop(2, windows(pair), lambda w, t: t + window(pair, w), total)
        store(pair, total)
        return carry

    lax.fori_loop(0, long, rest, 0)


def stacked(core, lists, sums=None):
    info = jnp.stack([v[VALID + 7, 64:] for v in lists]).astype(I32)
    if sums is None:
        out_shape, extra = jax.ShapeDtypeStruct((SHOTS // 2, 256, 128), F32), []
    else:
        out_shape, extra = (jax.ShapeDtypeStruct((SHOTS // 2, BIN, 128), BF),) * 2, [sums]
    return pl.pallas_call(
        lambda *refs: stack_kernel(sums is not None, *refs),
        out_shape=out_shape,
        in_specs=[SMEM, SMEM] + [VMEM] * (4 + len(extra)),
        out_specs=VMEM if sums is None else (VMEM, VMEM),
        scratch_shapes=[pltpu.VMEM((4, 64, 8, 128), F32), pltpu.SMEM((SHOTS // 2,), I32)],
        compiler_params=params(),
        name="stack0" if sums is None else "stack1",
    )(core, info, *lists, *extra)


def fold_kernel(x_ref, mine_ref, other_ref, *outs):
    for d in range(4):
        at = pl.ds(8 * ((x_ref[0] + d) & 3), 8)
        outs[d][...] = (mine_ref[at].astype(F32) + other_ref[at].astype(F32)).astype(BF)


def folded(x_pos, mine, other):
    return pl.pallas_call(
        fold_kernel,
        out_shape=[jax.ShapeDtypeStruct((8, BIN, 128), BF)] * 4,
        in_specs=[SMEM, VMEM, VMEM],
        out_specs=[VMEM] * 4,
        compiler_params=params(),
        name="fold",
    )(x_pos, mine, other)


def around(parts, axis):
    n = len(parts)
    out = [parts[0]]
    for d in range(1, n):
        out.append(lax.ppermute(parts[d], axis, [(i, (i + d) % n) for i in range(n)]))
    return out


def swapped(part):
    return lax.ppermute(part, "c", [(0, 1), (1, 0)])


def steps(gathers, trace_slot, gain, midbin, bin_row, taps_shot, taps_time):
    at = [lax.axis_index(a).reshape(1) for a in ("x", "z", "c", "y")]
    x_pos, z_pos, core = at[:3]
    x = gathers.reshape(BLK, NT)
    table = bin_row.reshape(64, 128)
    rows = band_rows(taps_time, taps_shot)
    (early,) = pick(0, x, trace_slot, gain, midbin, table, at)
    early = lax.all_to_all(early, ("z", "c"), split_axis=0, concat_axis=0, tiled=True)
    late = around(pick(1, x, trace_slot, gain, midbin, table, at), "x")
    (late,) = shuffled(regroup_kernel, late, [(16, 4 * ROWS, NT)], [z_pos, core])
    late = lax.all_to_all(late, ("z", "c"), split_axis=0, concat_axis=0, tiled=True)
    parts = around(shuffled(turn_kernel, [early], [(256, NT)] * 4), "x")
    lists = around(filtered(at, rows, parts), "y")
    later = around(filtered(at, rows, [late]), "y")
    mine, other = stacked(core, later, stacked(core, lists))
    other = swapped(other)
    parts = around(folded(x_pos, mine, other), "x")
    total = sum(p.astype(F32) for p in parts).astype(BF)
    parts = lax.all_to_all(total, "z", split_axis=0, concat_axis=0, tiled=True)
    scale = (8192 / 491520) ** 0.5
    return jnp.sum(parts.astype(F32) * scale, axis=0)


def solution(mesh):
    finer = Mesh(mesh.devices.reshape(4, 8, 2, mesh.shape["cmp"]), ("x", "z", "c", "y"))
    shot = ("x", "z", "c")
    in_specs = (P(shot, "y", None), P(shot, "y"), P(shot, "y"), P(shot, "y"), P(), P(), P())
    return jax.shard_map(
        steps, mesh=finer, in_specs=in_specs, out_specs=P(shot, "y"), check_vma=False
    )
```

```python
import jax
import jax.numpy as jnp
from jax import lax
from jax.experimental import pallas as pl
from jax.experimental.pallas import tpu as pltpu
from jax.sharding import Mesh
from jax.sharding import PartitionSpec as P


BF = jnp.bfloat16
F32 = jnp.float32
I32 = jnp.int32
SHOTS, RPD, PER = 64, 30, 15
ROWS = 16
CROWS = SHOTS * ROWS
VALID = SHOTS * PER
NT, BLK, BIN = 512, 1920, 128
YROWS = VALID + 16
QMAX = (YROWS - 64) // 16
WIDE = 640
VMEM = pl.BlockSpec(memory_space=pltpu.VMEM)
SMEM = pl.BlockSpec(memory_space=pltpu.SMEM)


def params(mib=24):
    return pltpu.CompilerParams(vmem_limit_bytes=mib * 1024 * 1024)


def iota(shape, dim):
    return lax.broadcasted_iota(I32, shape, dim)


def mask_bf(mask):
    return jnp.where(mask, 1.0, 0.0).astype(BF)


def mm(a, b):
    return jnp.dot(a, b, preferred_element_type=F32)


def mm_nt(a, b):
    return lax.dot_general(a, b, (((1,), (1,)), ((), ())), preferred_element_type=F32)


def column(ref, base, wanted):
    row = ref[:, base : base + WIDE].astype(F32)
    return jnp.sum(jnp.where(wanted, row, 0.0), axis=1, keepdims=True)


def pick_kernel(chunk, x_hbm, slot_hbm, gain_hbm, mid_hbm, tab_hbm, x_at, z_at, c_at, *refs):
    outs, refs = refs[: 1 + 3 * chunk], refs[1 + 3 * chunk :]
    x_ref, slot_ref, gain_ref, mid_ref, tab_ref, block_ref, in_sems = refs
    sources = (slot_hbm, gain_hbm, mid_hbm, tab_hbm, x_hbm)
    targets = (slot_ref, gain_ref, mid_ref, tab_ref, x_ref)
    copies = [pltpu.make_async_copy(sources[i], targets[i], in_sems.at[i]) for i in range(5)]
    for copy in copies:
        copy.start()
    for copy in copies[:4]:
        copy.wait()
    x_pos, z_pos, core = x_at[0], z_at[0], c_at[0]
    table = tab_ref[...]
    owners = lax.shift_right_logical(table, 7).astype(F32).astype(BF)
    locals_ = (table & 127).astype(F32).astype(BF)
    here, there = iota((256, 256), 0), iota((256, 256), 1)
    gather = mask_bf((lax.shift_right_logical(here, 4) == lax.shift_right_logical(there, 4)) & ((here & 15) == 15))
    place = iota((256, 1), 0) & 15
    real = place < PER
    lane = iota((256, NT), 1)

    def columns(chunk, b):
        base = min((480 * b) // 128 * 128, BLK - WIDE)
        receiver = (lax.shift_right_logical(iota((256, 1), 0), 4) + 16 * b) * RPD + chunk * PER + place
        wanted = (iota((256, WIDE), 1) + base == receiver) & real
        slot = column(slot_ref, base, wanted).astype(I32)
        block = (slot >= BLK).astype(I32) + (slot >= 2 * BLK).astype(I32) + (slot >= 3 * BLK).astype(I32)
        slot = jnp.where(real, slot - BLK * block, -1)
        gain = column(gain_ref, base, wanted)
        mid = column(mid_ref, base, wanted).astype(I32)
        pick_row = mask_bf(iota((256, 64), 1) == lax.shift_right_logical(mid, 7))
        pick_lane = iota((256, 128), 1) == (mid & 127)
        owner = jnp.sum(jnp.where(pick_lane, mm(pick_row, owners), 0.0), axis=1, keepdims=True)
        local = jnp.sum(jnp.where(pick_lane, mm(pick_row, locals_), 0.0), axis=1, keepdims=True)
        spread = jnp.where(lane < NT // 2, owner, local)
        spread = jnp.where(((lane & 15) == place) & real, spread, 0.0).astype(BF)
        return slot, gain, spread

    for b in range(CROWS // 256):
        slot, gain, spread = columns(chunk, b)
        one_hot = mask_bf(iota((256, BLK), 1) == slot)
        if b == 0:
            copies[4].wait()
        out = mm(one_hot, x_ref[...]) * gain + mm(gather, spread)
        block_ref[b] = out.astype(BF)
    for dx in range(4):
        for z in range(8):
            for c in range(2):
                x_to = (x_pos + dx) & 3
                if chunk:
                    row = (2 * ((z_pos + z) & 7) + (core ^ c)) * ROWS
                    row = pl.multiple_of(row, ROWS)
                    to = (c * 8 + z) * ROWS
                    outs[dx][to : to + ROWS, :] = block_ref[x_to, pl.ds(row, ROWS), :]
                else:
                    row = (2 * z + c) * ROWS
                    outs[0][2 * z + c, dx * ROWS : (dx + 1) * ROWS, :] = block_ref[x_to, row : row + ROWS, :]


def pick(chunk, x, slot, gain, mid, table, at):
    shape, count = ((256, NT), 4) if chunk else ((16, 4 * ROWS, NT), 1)
    hbm = pl.BlockSpec(memory_space=pltpu.HBM)
    return pl.pallas_call(
        lambda *refs: pick_kernel(chunk, *refs),
        out_shape=[jax.ShapeDtypeStruct(shape, BF)] * count,
        in_specs=[hbm] * 5 + [SMEM] * 3,
        out_specs=[VMEM] * count,
        scratch_shapes=[
            pltpu.VMEM((BLK, NT), BF),
            pltpu.VMEM((1, BLK), I32),
            pltpu.VMEM((1, BLK), F32),
            pltpu.VMEM((1, BLK), I32),
            pltpu.VMEM((64, 128), I32),
            pltpu.VMEM((4, 256, NT), BF),
            pltpu.SemaphoreType.DMA((5,)),
        ],
        compiler_params=params(60),
    )(x, slot, gain, mid, table, *at[:3])


def band_kernel(time_ref, shot_ref, time_out, shot_out):
    step, col = iota((256, 128), 0), iota((256, 128), 1)
    wrapped = (step < 128) == (col < 32)
    for k in range(3):
        base = jnp.broadcast_to(time_ref[k : k + 1, :], (128, 256))
        rolled = pltpu.roll(base, 0, 1, stride=1, stride_axis=0)
        band = rolled.T
        at = slice(128 * k, 128 * k + 128)
        time_out[0, :, at] = band.astype(BF)
        time_out[1, :, at] = jnp.where(wrapped, band, 0.0).astype(BF)
        base = jnp.broadcast_to(shot_ref[k : k + 1, :], (256, 640))
        rolled = pltpu.roll(base, 0, 1, stride=1, stride_axis=0)
        shot_out[0, :, 384 * k : 384 * k + 384] = rolled[:, 128:512].astype(BF)
        shot_out[1, :, 384 * k : 384 * k + 384] = rolled[:, :384].astype(BF)


def band_rows(taps_time, taps_shot):
    time_row = jnp.pad(taps_time.astype(BF).astype(F32), ((0, 0), (64, 128)))
    shot = taps_shot.astype(BF).astype(F32)
    shot_row = lax.pad(shot, jnp.float32(0), ((0, 0, 0), (8, 640 - 8 - 241, 7)))
    return time_row, shot_row


def filter_kernel(count, x_at, y_at, time_row, shot_row, *refs):
    parts, outs = refs[:count], refs[count : count + 4]
    time_ref, shot_ref, mid_ref, trace_ref, *rest = refs[count + 4 :]
    x_ref = rest[0]
    for dx in range(4):
        first = ((x_at[0] - dx) & 3) * 256
        if count > 1:
            x_ref[pl.ds(pl.multiple_of(first, 256), 256), :] = parts[dx][...]
        else:
            for k in range(16):
                to = pl.ds(pl.multiple_of(first + k * ROWS, ROWS), ROWS)
                x_ref[to, :] = parts[0][k, dx * ROWS : (dx + 1) * ROWS, :]
    band_kernel(time_row, shot_row, time_ref, shot_ref)
    row = iota((256, NT), 0)
    lane = iota((256, NT), 1)
    keep = ((row & 15) == 15) & (lax.shift_right_logical(row, 4) == lax.shift_right_logical(lane & 255, 4))
    bad = (iota((1, 256), 1) & 15) == 15
    upper = mask_bf(iota((256, 256), 0) < iota((256, 256), 1))
    owner, local, marks, ranks = [], [], [], []
    before = jnp.zeros((128, 1), F32)
    for b in range(4):
        rows = slice(256 * b, 256 * b + 256)
        part = jnp.where(keep, x_ref[rows, :].astype(F32), 0.0)
        ids = jnp.sum(part, axis=0, keepdims=True)
        owner.append(jnp.where(bad, 127.0, ids[:, :256]))
        local.append(ids[:, 256:])
        for j in range(4):
            if j:
                lhs, band = x_ref[rows, 128 * j - 128 : 128 * j + 128], time_ref[0]
            else:
                lhs = jnp.concatenate([x_ref[rows, 384:], x_ref[rows, :128]], axis=1)
                band = time_ref[1]
            mids = mm(lhs, band).reshape(16, 2, 8, 384)
            for half in range(2):
                part = mids[:, half].reshape(128, 384).astype(BF)
                for k in range(3):
                    value = part[:, 128 * k : 128 * k + 128]
                    for w in range(2):
                        at = 128 * b - 128 * w
                        if 0 <= at < 384:
                            at += 384 * k
                            mid_ref[half, w, at : at + 128, 128 * j : 128 * j + 128] = value
            if j == 1:
                mark = jnp.where(iota((128, 256), 0).astype(F32) == owner[b], 1.0, 0.0)
                ranks.append(mm(mark.astype(BF), upper) + before)
                marks.append(mark)
                before = before + jnp.sum(mark, axis=1, keepdims=True)
    lower = mask_bf(iota((128, 128), 1) < iota((128, 128), 0))
    starts = mm(lower, jnp.broadcast_to(before, (128, 128)).astype(BF))[:, :1]
    y_pos = y_at[0]
    places = []
    for w in range(2):
        both = []
        for half in range(2):
            filt = mm(shot_ref[w], mid_ref[half, w])
            power = jnp.mean(filt * filt, axis=1, keepdims=True) + 1e-6
            done = pltpu.roll(filt * lax.rsqrt(power), NT - 32, 1)
            both.append(done.reshape(32, 1, 8, NT))
            b = 2 * w + half
            places.append(jnp.sum(marks[b] * (ranks[b] + starts), axis=0, keepdims=True))
        trace = jnp.concatenate(both, axis=1).reshape(512, NT).astype(BF)
        for y in range(4):
            trace_ref[(y - y_pos) & 3, 512 * w : 512 * w + 512, :] = trace[:, 128 * y : 128 * y + 128]
    place = jnp.concatenate(places, axis=1).astype(I32)
    owner = jnp.concatenate(owner, axis=1)
    local = jnp.concatenate(local, axis=1)
    place_lane = mask_bf(iota((128, CROWS), 0) == (place & 127))
    here = iota((8, CROWS), 0) == lax.shift_right_logical(place, 7)
    ids = jnp.concatenate([jnp.where(here, owner, 0.0), jnp.where(here, local, 0.0)], axis=0)
    ids = mm_nt(ids.astype(BF), place_lane)
    first = jnp.broadcast_to(starts, (128, 128)).T[:16]
    first = lax.shift_right_logical(first.astype(I32), 4)
    count = lax.shift_right_logical(pltpu.roll(first, 126, 1) - first + 4, 2)
    count = jnp.maximum(count, 1).astype(F32).astype(BF)
    first = jnp.minimum(first, QMAX).astype(F32).astype(BF)
    here, there = iota((128, 128), 0), iota((128, 128), 1)
    even = 2 * (there & 31)
    pick_first = mask_bf((here == even) & (there >= 64) & (there < 96))
    pick_count = mask_bf((here == even) & (there >= 96))
    first = mm(first, pick_first) + mm(count, pick_count)
    r, c = iota((16, 128), 0), iota((16, 128), 1)
    ids = jnp.where((r == 7) & (c >= 64), first, ids).astype(BF)
    traces = jnp.concatenate([trace_ref[d] for d in range(4)], axis=1)
    for b in range(2):
        size = min(512, VALID - 512 * b)
        order = mask_bf(iota((size, CROWS), 0) + 512 * b == place)
        rows = mm(order, traces).astype(BF)
        for d in range(4):
            outs[d][512 * b : 512 * b + size, :] = rows[:, 128 * d : 128 * d + 128]
    for d in range(4):
        outs[d][VALID:, :] = ids


def filtered(at, rows, parts):
    scratch = [
        pltpu.VMEM((2, 256, 384), BF),
        pltpu.VMEM((2, 256, 1152), BF),
        pltpu.VMEM((2, 2, 1152, NT), BF),
        pltpu.VMEM((4, CROWS, 128), BF),
    ]
    scratch.append(pltpu.VMEM((CROWS, NT), BF))
    return pl.pallas_call(
        lambda *refs: filter_kernel(len(parts), *refs),
        out_shape=[jax.ShapeDtypeStruct((YROWS, 128), BF)] * 4,
        in_specs=[SMEM] * 2 + [VMEM] * (2 + len(parts)),
        out_specs=[VMEM] * 4,
        scratch_shapes=scratch,
        compiler_params=params(),
    )(at[0], at[3], *rows, *parts)


def regroup_kernel(z_at, c_at, *refs):
    for dz in range(8):
        for dx in range(4):
            for dc in range(2):
                source = (dc * 8 + dz) * ROWS
                to = ((z_at[0] + dz) & 7) * 2 + (c_at[0] ^ dc)
                refs[4][to, dx * ROWS : (dx + 1) * ROWS, :] = refs[dx][source : source + ROWS, :]


def turn_kernel(ref, *outs):
    for dx in range(4):
        for k in range(16):
            outs[dx][k * ROWS : (k + 1) * ROWS, :] = ref[k, dx * ROWS : (dx + 1) * ROWS, :]


def shuffled(kernel, parts, shapes, scalars=()):
    return pl.pallas_call(
        kernel,
        out_shape=[jax.ShapeDtypeStruct(shape, BF) for shape in shapes],
        in_specs=[SMEM] * len(scalars) + [VMEM] * len(parts),
        out_specs=[VMEM] * len(shapes),
        compiler_params=params(8),
    )(*scalars, *parts)


def stack_kernel(last, core_ref, x_at, info_ref, l0, l1, l2, l3, *refs):
    lists = (l0, l1, l2, l3)
    table_ref, long_ref = refs[-2:]
    lane = iota((8, 128), 1)
    sub = iota((8, 128), 0)
    for n, ref in enumerate(lists):
        ids = ref[VALID:, :].astype(F32)
        code = jnp.where((sub == 7) & (lane >= 64), -1.0, ids[:8] * 128.0 + ids[8:])
        after = pltpu.roll(code, 7, 0)
        for e in range(8):
            shift = (64 * (n & 1) - 16 * e) % 128
            limit = 128 + 64 * (n & 1) - 16 * e
            a = pltpu.roll(code, shift, 1) if shift else code
            b = pltpu.roll(after, shift, 1) if shift else after
            rows = jnp.where(lane < limit, a, b)
            for r in range(8):
                table_ref[n, 8 * r + e] = jnp.broadcast_to(rows[r : r + 1, :], (8, 128))
    core = core_ref[0]
    bins = iota((256, 128), 0)
    bins = (bins & 127) + jnp.where(bins < 128, core, 1 - core) * 128
    bins = bins.astype(F32).astype(BF)
    low = lane < 64
    one, zero = jnp.ones((256, 128), BF), jnp.zeros((256, 128), BF)

    def hot(pair, first, second):
        code = jnp.where(low, first, second) - (pair * 256).astype(F32)
        code = jnp.where((code >= 0.0) & (code < 256.0), code, 300.0)
        code = jnp.concatenate([code, code], axis=0).astype(BF)
        code = jnp.broadcast_to(code[None], (16, 16, 128)).reshape(256, 128)
        return jnp.where(code == bins, one, zero)

    def window(pair, w):
        codes, rows = [], []
        for n in range(4):
            q = info_ref[n, pair]
            if w is None:
                code = table_ref[n, q]
            else:
                q0 = q + 4 * w
                q = jnp.minimum(q0, QMAX)
                code = jnp.where((lane & 63) >= (q0 - q) * 16, table_ref[n, q], -1.0)
            codes.append(code)
            rows.append(lists[n][pl.ds(pl.multiple_of(q * 16, 16), 64), :])
        left, right = hot(pair, *codes[:2]), hot(pair, *codes[2:])
        return mm(jnp.concatenate([left, right], axis=1), jnp.concatenate(rows, axis=0))

    count = SHOTS // 2
    if last is not None:
        count //= 2

    def pair_of(i):
        if last is None:
            return i
        dx = jnp.where(i < 8, last[0], last[1])
        return ((x_at[0] + dx) & 3) * 8 + (i & 7)

    def store(i, pair, total):
        if last is None:
            refs[0][i] = total
        else:
            total = total + refs[0][pair]
            refs[1][i] = total[:128].astype(BF)
            refs[2][i] = total[128:].astype(BF)

    def windows(pair):
        counts = [info_ref[n, 32 + pair] for n in range(4)]
        return jnp.maximum(jnp.maximum(counts[0], counts[1]), jnp.maximum(counts[2], counts[3]))

    def body(i, long):
        pair = pair_of(i)
        store(i, pair, window(pair, None))
        long_ref[long] = i
        return long + jnp.where(windows(pair) > 1, 1, 0)

    long = lax.fori_loop(0, count, body, jnp.int32(0), unroll=8 if last is None else 16)

    def rest(k, carry):
        i = long_ref[k]
        pair = pair_of(i)
        total = window(pair, None) + window(pair, 1)
        total = lax.fori_loop(2, windows(pair), lambda w, t: t + window(pair, w), total)
        store(i, pair, total)
        return carry

    lax.fori_loop(0, long, rest, 0)


def info_of(lists):
    return jnp.stack([v[VALID + 7, 64:] for v in lists]).astype(I32)


def stacked(core, x_pos, info, lists, last=None, sums=None):
    if last is None:
        out_shape, extra = jax.ShapeDtypeStruct((SHOTS // 2, 256, 128), F32), []
    else:
        out_shape, extra = (jax.ShapeDtypeStruct((SHOTS // 4, BIN, 128), BF),) * 2, [sums]
    return pl.pallas_call(
        lambda *refs: stack_kernel(last, *refs),
        out_shape=out_shape,
        in_specs=[SMEM, SMEM, SMEM] + [VMEM] * (4 + len(extra)),
        out_specs=VMEM if last is None else (VMEM, VMEM),
        scratch_shapes=[pltpu.VMEM((4, 64, 8, 128), F32), pltpu.SMEM((SHOTS // 2,), I32)],
        compiler_params=params(),
    )(core, x_pos, info, *lists, *extra)


def fold_kernel(mine_ref, other_ref, *outs):
    for k in range(2):
        at = slice(8 * k, 8 * k + 8)
        outs[k][...] = (mine_ref[at].astype(F32) + other_ref[at].astype(F32)).astype(BF)


def folded(mine, other):
    return pl.pallas_call(
        fold_kernel,
        out_shape=[jax.ShapeDtypeStruct((8, BIN, 128), BF)] * 2,
        in_specs=[VMEM, VMEM],
        out_specs=[VMEM] * 2,
        compiler_params=params(16),
        name="fold",
    )(mine, other)


def around(parts, axis):
    n = len(parts)
    out = [parts[0]]
    for d in range(1, n):
        out.append(lax.ppermute(parts[d], axis, [(i, (i + d) % n) for i in range(n)]))
    return out


def swapped(part):
    return lax.ppermute(part, "c", [(0, 1), (1, 0)])


def steps(gathers, trace_slot, gain, midbin, bin_row, taps_shot, taps_time):
    at = [lax.axis_index(a).reshape(1) for a in ("x", "z", "c", "y")]
    x_pos, z_pos, core = at[:3]
    x = gathers.reshape(BLK, NT)
    table = bin_row.reshape(64, 128)
    rows = band_rows(taps_time, taps_shot)
    (early,) = pick(0, x, trace_slot, gain, midbin, table, at)
    early = lax.all_to_all(early, ("z", "c"), split_axis=0, concat_axis=0, tiled=True)
    late = around(pick(1, x, trace_slot, gain, midbin, table, at), "x")
    (late,) = shuffled(regroup_kernel, late, [(16, 4 * ROWS, NT)], [z_pos, core])
    late = lax.all_to_all(late, ("z", "c"), split_axis=0, concat_axis=0, tiled=True)
    parts = around(shuffled(turn_kernel, [early], [(256, NT)] * 4), "x")
    lists = around(filtered(at, rows, parts), "y")
    later = around(filtered(at, rows, [late]), "y")
    sums = stacked(core, x_pos, info_of(lists), lists)
    info = info_of(later)
    parts = [None] * 4
    for last in ((1, 3), (2, 0)):
        mine, other = stacked(core, x_pos, info, later, last, sums)
        near, far = folded(mine, swapped(other))
        parts[last[0]], parts[last[1]] = near, far
    parts = around(parts, "x")
    total = sum(p.astype(F32) for p in parts).astype(BF)
    parts = lax.all_to_all(total, "z", split_axis=0, concat_axis=0, tiled=True)
    scale = (8192 / 491520) ** 0.5
    return jnp.sum(parts.astype(F32) * scale, axis=0)


def solution(mesh):
    finer = Mesh(mesh.devices.reshape(4, 8, 2, mesh.shape["cmp"]), ("x", "z", "c", "y"))
    shot = ("x", "z", "c")
    in_specs = (P(shot, "y", None), P(shot, "y"), P(shot, "y"), P(shot, "y"), P(), P(), P())
    return jax.shard_map(
        steps, mesh=finer, in_specs=in_specs, out_specs=P(shot, "y"), check_vma=False
    )
```

```python
import jax
import jax.numpy as jnp
from jax import lax
from jax.experimental import pallas as pl
from jax.experimental.pallas import tpu as pltpu
from jax.sharding import Mesh
from jax.sharding import PartitionSpec as P


BF = jnp.bfloat16
F32 = jnp.float32
I32 = jnp.int32
SHOTS, RPD, PER = 64, 30, 15
ROWS = 16
CROWS = SHOTS * ROWS
VALID = SHOTS * PER
NT, BLK, BIN = 512, 1920, 128
YROWS = VALID + 16
QMAX = (YROWS - 64) // 16
WIDE = 640
VMEM = pl.BlockSpec(memory_space=pltpu.VMEM)
SMEM = pl.BlockSpec(memory_space=pltpu.SMEM)


def params(mib=24):
    return pltpu.CompilerParams(vmem_limit_bytes=mib * 1024 * 1024)


def iota(shape, dim):
    return lax.broadcasted_iota(I32, shape, dim)


def mask_bf(mask):
    return jnp.where(mask, 1.0, 0.0).astype(BF)


def mm(a, b):
    return jnp.dot(a, b, preferred_element_type=F32)


def mm_nt(a, b):
    return lax.dot_general(a, b, (((1,), (1,)), ((), ())), preferred_element_type=F32)


def column(ref, base, wanted):
    row = ref[:, base : base + WIDE].astype(F32)
    return jnp.sum(jnp.where(wanted, row, 0.0), axis=1, keepdims=True)


def pick_kernel(chunk, x_hbm, slot_hbm, gain_hbm, mid_hbm, tab_hbm, x_at, z_at, c_at, *refs):
    outs, refs = refs[: 1 + 3 * chunk], refs[1 + 3 * chunk :]
    x_ref, slot_ref, gain_ref, mid_ref, tab_ref, block_ref, in_sems = refs
    sources = (slot_hbm, gain_hbm, mid_hbm, tab_hbm, x_hbm)
    targets = (slot_ref, gain_ref, mid_ref, tab_ref, x_ref)
    copies = [pltpu.make_async_copy(sources[i], targets[i], in_sems.at[i]) for i in range(5)]
    for copy in copies:
        copy.start()
    for copy in copies[:4]:
        copy.wait()
    x_pos, z_pos, core = x_at[0], z_at[0], c_at[0]
    table = tab_ref[...]
    owners = lax.shift_right_logical(table, 7).astype(F32).astype(BF)
    locals_ = (table & 127).astype(F32).astype(BF)
    here, there = iota((256, 256), 0), iota((256, 256), 1)
    gather = mask_bf((lax.shift_right_logical(here, 4) == lax.shift_right_logical(there, 4)) & ((here & 15) == 15))
    place = iota((256, 1), 0) & 15
    real = place < PER
    lane = iota((256, NT), 1)

    def columns(chunk, b):
        base = min((480 * b) // 128 * 128, BLK - WIDE)
        receiver = (lax.shift_right_logical(iota((256, 1), 0), 4) + 16 * b) * RPD + chunk * PER + place
        wanted = (iota((256, WIDE), 1) + base == receiver) & real
        slot = column(slot_ref, base, wanted).astype(I32)
        block = (slot >= BLK).astype(I32) + (slot >= 2 * BLK).astype(I32) + (slot >= 3 * BLK).astype(I32)
        slot = jnp.where(real, slot - BLK * block, -1)
        gain = column(gain_ref, base, wanted)
        mid = column(mid_ref, base, wanted).astype(I32)
        pick_row = mask_bf(iota((256, 64), 1) == lax.shift_right_logical(mid, 7))
        pick_lane = iota((256, 128), 1) == (mid & 127)
        owner = jnp.sum(jnp.where(pick_lane, mm(pick_row, owners), 0.0), axis=1, keepdims=True)
        local = jnp.sum(jnp.where(pick_lane, mm(pick_row, locals_), 0.0), axis=1, keepdims=True)
        spread = jnp.where(lane < NT // 2, owner, local)
        spread = jnp.where(((lane & 15) == place) & real, spread, 0.0).astype(BF)
        return slot, gain, spread

    for b in range(CROWS // 256):
        slot, gain, spread = columns(chunk, b)
        one_hot = mask_bf(iota((256, BLK), 1) == slot)
        if b == 0:
            copies[4].wait()
        out = mm(one_hot, x_ref[...]) * gain + mm(gather, spread)
        block_ref[b] = out.astype(BF)
    for dx in range(4):
        for z in range(8):
            for c in range(2):
                x_to = (x_pos + dx) & 3
                if chunk:
                    row = (2 * ((z_pos + z) & 7) + (core ^ c)) * ROWS
                    row = pl.multiple_of(row, ROWS)
                    to = (c * 8 + z) * ROWS
                    outs[dx][to : to + ROWS, :] = block_ref[x_to, pl.ds(row, ROWS), :]
                else:
                    row = (2 * z + c) * ROWS
                    outs[0][2 * z + c, dx * ROWS : (dx + 1) * ROWS, :] = block_ref[x_to, row : row + ROWS, :]


def pick(chunk, x, slot, gain, mid, table, at):
    shape, count = ((256, NT), 4) if chunk else ((16, 4 * ROWS, NT), 1)
    hbm = pl.BlockSpec(memory_space=pltpu.HBM)
    return pl.pallas_call(
        lambda *refs: pick_kernel(chunk, *refs),
        out_shape=[jax.ShapeDtypeStruct(shape, BF)] * count,
        in_specs=[hbm] * 5 + [SMEM] * 3,
        out_specs=[VMEM] * count,
        scratch_shapes=[
            pltpu.VMEM((BLK, NT), BF),
            pltpu.VMEM((1, BLK), I32),
            pltpu.VMEM((1, BLK), F32),
            pltpu.VMEM((1, BLK), I32),
            pltpu.VMEM((64, 128), I32),
            pltpu.VMEM((4, 256, NT), BF),
            pltpu.SemaphoreType.DMA((5,)),
        ],
        compiler_params=params(60),
    )(x, slot, gain, mid, table, *at[:3])


def band_kernel(time_ref, shot_ref, time_out, shot_out):
    step, col = iota((256, 128), 0), iota((256, 128), 1)
    wrapped = (step < 128) == (col < 32)
    for k in range(3):
        base = jnp.broadcast_to(time_ref[k : k + 1, :], (128, 256))
        rolled = pltpu.roll(base, 0, 1, stride=1, stride_axis=0)
        band = rolled.T
        at = slice(128 * k, 128 * k + 128)
        time_out[0, :, at] = band.astype(BF)
        time_out[1, :, at] = jnp.where(wrapped, band, 0.0).astype(BF)
        base = jnp.broadcast_to(shot_ref[k : k + 1, :], (256, 640))
        rolled = pltpu.roll(base, 0, 1, stride=1, stride_axis=0)
        shot_out[0, :, 384 * k : 384 * k + 384] = rolled[:, 128:512].astype(BF)
        shot_out[1, :, 384 * k : 384 * k + 384] = rolled[:, :384].astype(BF)


def band_rows(taps_time, taps_shot):
    time_row = jnp.pad(taps_time.astype(BF).astype(F32), ((0, 0), (64, 128)))
    shot = taps_shot.astype(BF).astype(F32)
    shot_row = lax.pad(shot, jnp.float32(0), ((0, 0, 0), (8, 640 - 8 - 241, 7)))
    return time_row, shot_row


def filter_kernel(count, x_at, y_at, time_row, shot_row, *refs):
    parts, outs = refs[:count], refs[count : count + 4]
    time_ref, shot_ref, mid_ref, trace_ref, *rest = refs[count + 4 :]
    x_ref = rest[0]
    for dx in range(4):
        first = ((x_at[0] - dx) & 3) * 256
        if count > 1:
            x_ref[pl.ds(pl.multiple_of(first, 256), 256), :] = parts[dx][...]
        else:
            for k in range(16):
                to = pl.ds(pl.multiple_of(first + k * ROWS, ROWS), ROWS)
                x_ref[to, :] = parts[0][k, dx * ROWS : (dx + 1) * ROWS, :]
    band_kernel(time_row, shot_row, time_ref, shot_ref)
    row = iota((256, NT), 0)
    lane = iota((256, NT), 1)
    keep = ((row & 15) == 15) & (lax.shift_right_logical(row, 4) == lax.shift_right_logical(lane & 255, 4))
    bad = (iota((1, 256), 1) & 15) == 15
    upper = mask_bf(iota((256, 256), 0) < iota((256, 256), 1))
    owner, local, marks, ranks = [], [], [], []
    before = jnp.zeros((128, 1), F32)
    for b in range(4):
        rows = slice(256 * b, 256 * b + 256)
        part = jnp.where(keep, x_ref[rows, :].astype(F32), 0.0)
        ids = jnp.sum(part, axis=0, keepdims=True)
        owner.append(jnp.where(bad, 127.0, ids[:, :256]))
        local.append(ids[:, 256:])
        for j in range(4):
            if j:
                lhs, band = x_ref[rows, 128 * j - 128 : 128 * j + 128], time_ref[0]
            else:
                lhs = jnp.concatenate([x_ref[rows, 384:], x_ref[rows, :128]], axis=1)
                band = time_ref[1]
            mids = mm(lhs, band).reshape(16, 2, 8, 384)
            for half in range(2):
                part = mids[:, half].reshape(128, 384).astype(BF)
                for k in range(3):
                    value = part[:, 128 * k : 128 * k + 128]
                    for w in range(2):
                        at = 128 * b - 128 * w
                        if 0 <= at < 384:
                            at += 384 * k
                            mid_ref[half, w, at : at + 128, 128 * j : 128 * j + 128] = value
            if j == 1:
                mark = jnp.where(iota((128, 256), 0).astype(F32) == owner[b], 1.0, 0.0)
                ranks.append(mm(mark.astype(BF), upper) + before)
                marks.append(mark)
                before = before + jnp.sum(mark, axis=1, keepdims=True)
    lower = mask_bf(iota((128, 128), 1) < iota((128, 128), 0))
    starts = mm(lower, jnp.broadcast_to(before, (128, 128)).astype(BF))[:, :1]
    y_pos = y_at[0]
    places = []
    for w in range(2):
        both = []
        for half in range(2):
            filt = mm(shot_ref[w], mid_ref[half, w])
            power = jnp.mean(filt * filt, axis=1, keepdims=True) + 1e-6
            done = pltpu.roll(filt * lax.rsqrt(power), NT - 32, 1)
            both.append(done.reshape(32, 1, 8, NT))
            b = 2 * w + half
            places.append(jnp.sum(marks[b] * (ranks[b] + starts), axis=0, keepdims=True))
        trace = jnp.concatenate(both, axis=1).reshape(512, NT).astype(BF)
        for y in range(4):
            trace_ref[(y - y_pos) & 3, 512 * w : 512 * w + 512, :] = trace[:, 128 * y : 128 * y + 128]
    place = jnp.concatenate(places, axis=1).astype(I32)
    owner = jnp.concatenate(owner, axis=1)
    local = jnp.concatenate(local, axis=1)
    place_lane = mask_bf(iota((128, CROWS), 0) == (place & 127))
    here = iota((8, CROWS), 0) == lax.shift_right_logical(place, 7)
    ids = jnp.concatenate([jnp.where(here, owner, 0.0), jnp.where(here, local, 0.0)], axis=0)
    ids = mm_nt(ids.astype(BF), place_lane)
    first = jnp.broadcast_to(starts, (128, 128)).T[:16]
    first = lax.shift_right_logical(first.astype(I32), 4)
    count = lax.shift_right_logical(pltpu.roll(first, 126, 1) - first + 4, 2)
    count = jnp.maximum(count, 1).astype(F32).astype(BF)
    first = jnp.minimum(first, QMAX).astype(F32).astype(BF)
    here, there = iota((128, 128), 0), iota((128, 128), 1)
    even = 2 * (there & 31)
    pick_first = mask_bf((here == even) & (there >= 64) & (there < 96))
    pick_count = mask_bf((here == even) & (there >= 96))
    first = mm(first, pick_first) + mm(count, pick_count)
    r, c = iota((16, 128), 0), iota((16, 128), 1)
    ids = jnp.where((r == 7) & (c >= 64), first, ids).astype(BF)
    traces = jnp.concatenate([trace_ref[d] for d in range(4)], axis=1)
    for b in range(2):
        size = min(512, VALID - 512 * b)
        order = mask_bf(iota((size, CROWS), 0) + 512 * b == place)
        rows = mm(order, traces).astype(BF)
        for d in range(4):
            outs[d][512 * b : 512 * b + size, :] = rows[:, 128 * d : 128 * d + 128]
    for d in range(4):
        outs[d][VALID:, :] = ids


def filtered(at, rows, parts):
    scratch = [
        pltpu.VMEM((2, 256, 384), BF),
        pltpu.VMEM((2, 256, 1152), BF),
        pltpu.VMEM((2, 2, 1152, NT), BF),
        pltpu.VMEM((4, CROWS, 128), BF),
    ]
    scratch.append(pltpu.VMEM((CROWS, NT), BF))
    return pl.pallas_call(
        lambda *refs: filter_kernel(len(parts), *refs),
        out_shape=[jax.ShapeDtypeStruct((YROWS, 128), BF)] * 4,
        in_specs=[SMEM] * 2 + [VMEM] * (2 + len(parts)),
        out_specs=[VMEM] * 4,
        scratch_shapes=scratch,
        compiler_params=params(),
    )(at[0], at[3], *rows, *parts)


def regroup_kernel(z_at, c_at, *refs):
    for dz in range(8):
        for dx in range(4):
            for dc in range(2):
                source = (dc * 8 + dz) * ROWS
                to = ((z_at[0] + dz) & 7) * 2 + (c_at[0] ^ dc)
                refs[4][to, dx * ROWS : (dx + 1) * ROWS, :] = refs[dx][source : source + ROWS, :]


def turn_kernel(ref, *outs):
    for dx in range(4):
        for k in range(16):
            outs[dx][k * ROWS : (k + 1) * ROWS, :] = ref[k, dx * ROWS : (dx + 1) * ROWS, :]


def shuffled(kernel, parts, shapes, scalars=()):
    return pl.pallas_call(
        kernel,
        out_shape=[jax.ShapeDtypeStruct(shape, BF) for shape in shapes],
        in_specs=[SMEM] * len(scalars) + [VMEM] * len(parts),
        out_specs=[VMEM] * len(shapes),
        compiler_params=params(8),
    )(*scalars, *parts)


def stack_kernel(last, core_ref, x_at, info_ref, l0, l1, l2, l3, *refs):
    lists = (l0, l1, l2, l3)
    table_ref, long_ref = refs[-2:]
    lane = iota((8, 128), 1)
    sub = iota((8, 128), 0)
    for n, ref in enumerate(lists):
        ids = ref[VALID:, :].astype(F32)
        code = jnp.where((sub == 7) & (lane >= 64), -1.0, ids[:8] * 128.0 + ids[8:])
        after = pltpu.roll(code, 7, 0)
        for e in range(8):
            shift = (64 * (n & 1) - 16 * e) % 128
            limit = 128 + 64 * (n & 1) - 16 * e
            a = pltpu.roll(code, shift, 1) if shift else code
            b = pltpu.roll(after, shift, 1) if shift else after
            rows = jnp.where(lane < limit, a, b)
            for r in range(8):
                table_ref[n, 8 * r + e] = jnp.broadcast_to(rows[r : r + 1, :], (8, 128))
    core = core_ref[0]
    bins = iota((256, 128), 0)
    bins = (bins & 127) + jnp.where(bins < 128, core, 1 - core) * 128
    bins = bins.astype(F32).astype(BF)
    low = lane < 64
    one, zero = jnp.ones((256, 128), BF), jnp.zeros((256, 128), BF)

    def hot(pair, first, second):
        code = jnp.where(low, first, second) - (pair * 256).astype(F32)
        code = jnp.where((code >= 0.0) & (code < 256.0), code, 300.0)
        code = jnp.concatenate([code, code], axis=0).astype(BF)
        code = jnp.broadcast_to(code[None], (16, 16, 128)).reshape(256, 128)
        return jnp.where(code == bins, one, zero)

    def window(pair, w):
        codes, rows = [], []
        for n in range(4):
            q = info_ref[n, pair]
            if w is None:
                code = table_ref[n, q]
            else:
                q0 = q + 4 * w
                q = jnp.minimum(q0, QMAX)
                code = jnp.where((lane & 63) >= (q0 - q) * 16, table_ref[n, q], -1.0)
            codes.append(code)
            rows.append(lists[n][pl.ds(pl.multiple_of(q * 16, 16), 64), :])
        left, right = hot(pair, *codes[:2]), hot(pair, *codes[2:])
        return mm(jnp.concatenate([left, right], axis=1), jnp.concatenate(rows, axis=0))

    count = SHOTS // 2
    if last is not None:
        count = 8 * len(last)

    def pair_of(i):
        if last is None:
            return i
        dx = jnp.where(i < 8, last[0], last[-1])
        return ((x_at[0] + dx) & 3) * 8 + (i & 7)

    def store(i, pair, total):
        if last is None:
            refs[0][i] = total
        else:
            total = total + refs[0][pair]
            refs[1][i] = total[:128].astype(BF)
            refs[2][i] = total[128:].astype(BF)

    def windows(pair):
        counts = [info_ref[n, 32 + pair] for n in range(4)]
        return jnp.maximum(jnp.maximum(counts[0], counts[1]), jnp.maximum(counts[2], counts[3]))

    def body(i, long):
        pair = pair_of(i)
        store(i, pair, window(pair, None))
        long_ref[long] = i
        return long + jnp.where(windows(pair) > 1, 1, 0)

    long = lax.fori_loop(0, count, body, jnp.int32(0), unroll=min(count, 8 if last is None else 16))

    def rest(k, carry):
        i = long_ref[k]
        pair = pair_of(i)
        total = window(pair, None) + window(pair, 1)
        total = lax.fori_loop(2, windows(pair), lambda w, t: t + window(pair, w), total)
        store(i, pair, total)
        return carry

    lax.fori_loop(0, long, rest, 0)


def info_of(lists):
    return jnp.stack([v[VALID + 7, 64:] for v in lists]).astype(I32)


def stacked(core, x_pos, info, lists, last=None, sums=None):
    if last is None:
        out_shape, extra = jax.ShapeDtypeStruct((SHOTS // 2, 256, 128), F32), []
    else:
        out_shape, extra = (jax.ShapeDtypeStruct((8 * len(last), BIN, 128), BF),) * 2, [sums]
    return pl.pallas_call(
        lambda *refs: stack_kernel(last, *refs),
        out_shape=out_shape,
        in_specs=[SMEM, SMEM, SMEM] + [VMEM] * (4 + len(extra)),
        out_specs=VMEM if last is None else (VMEM, VMEM),
        scratch_shapes=[pltpu.VMEM((4, 64, 8, 128), F32), pltpu.SMEM((SHOTS // 2,), I32)],
        compiler_params=params(),
    )(core, x_pos, info, *lists, *extra)


def fold_kernel(mine_ref, other_ref, *outs):
    for k in range(len(outs)):
        at = slice(8 * k, 8 * k + 8)
        outs[k][...] = (mine_ref[at].astype(F32) + other_ref[at].astype(F32)).astype(BF)


def folded(mine, other):
    parts = mine.shape[0] // 8
    return pl.pallas_call(
        fold_kernel,
        out_shape=[jax.ShapeDtypeStruct((8, BIN, 128), BF)] * parts,
        in_specs=[VMEM, VMEM],
        out_specs=[VMEM] * parts,
        compiler_params=params(16),
        name="fold",
    )(mine, other)


def around(parts, axis):
    n = len(parts)
    out = [parts[0]]
    for d in range(1, n):
        out.append(lax.ppermute(parts[d], axis, [(i, (i + d) % n) for i in range(n)]))
    return out


def swapped(part):
    return lax.ppermute(part, "c", [(0, 1), (1, 0)])


def steps(gathers, trace_slot, gain, midbin, bin_row, taps_shot, taps_time):
    at = [lax.axis_index(a).reshape(1) for a in ("x", "z", "c", "y")]
    x_pos, z_pos, core = at[:3]
    x = gathers.reshape(BLK, NT)
    table = bin_row.reshape(64, 128)
    rows = band_rows(taps_time, taps_shot)
    (early,) = pick(0, x, trace_slot, gain, midbin, table, at)
    early = lax.all_to_all(early, ("z", "c"), split_axis=0, concat_axis=0, tiled=True)
    late = around(pick(1, x, trace_slot, gain, midbin, table, at), "x")
    (late,) = shuffled(regroup_kernel, late, [(16, 4 * ROWS, NT)], [z_pos, core])
    late = lax.all_to_all(late, ("z", "c"), split_axis=0, concat_axis=0, tiled=True)
    parts = around(shuffled(turn_kernel, [early], [(256, NT)] * 4), "x")
    lists = around(filtered(at, rows, parts), "y")
    later = around(filtered(at, rows, [late]), "y")
    sums = stacked(core, x_pos, info_of(lists), lists)
    info = info_of(later)
    parts = [None] * 4
    for last in ((2,), (1, 3), (0,)):
        mine, other = stacked(core, x_pos, info, later, last, sums)
        done = folded(mine, swapped(other))
        for k, dx in enumerate(last):
            parts[dx] = done[k]
    parts = around(parts, "x")
    total = sum(p.astype(F32) for p in parts).astype(BF)
    parts = lax.all_to_all(total, "z", split_axis=0, concat_axis=0, tiled=True)
    scale = (8192 / 491520) ** 0.5
    return jnp.sum(parts.astype(F32) * scale, axis=0)


def solution(mesh):
    finer = Mesh(mesh.devices.reshape(4, 8, 2, mesh.shape["cmp"]), ("x", "z", "c", "y"))
    shot = ("x", "z", "c")
    in_specs = (P(shot, "y", None), P(shot, "y"), P(shot, "y"), P(shot, "y"), P(), P(), P())
    return jax.shard_map(
        steps, mesh=finer, in_specs=in_specs, out_specs=P(shot, "y"), check_vma=False
    )
```
